128 devices in a mesh: seq: 32 (over z, x, core), head: 4 (over y).
Axes of the slice: x: 4, y: 4, z: 4, core: 2. Of those that a mesh axis runs over, the one named last changes fastest.
Arguments:
- token_ids: int32 [32768], P('seq'), may hold values from 0 to 255
- embedding: bfloat16 [256, 1024], replicated, may hold values from -6 to 6
- fine_norm: float32 [1024], replicated, may hold values from 0.1 to 1.9
- fine_query: bfloat16 [1024, 1024], P(None, 'head'), may hold values from -2 to 2
- fine_key: bfloat16 [1024, 1024], P(None, 'head'), may hold values from -2 to 2
- fine_value: bfloat16 [1024, 1024], P(None, 'head'), may hold values from -0.1875 to 0.1875
- fine_output: bfloat16 [1024, 1024], P('head'), may hold values from -0.1875 to 0.1875
- shorten_weight: bfloat16 [4, 1024, 1024], P(None, 'head'), may hold values from -0.09375 to 0.09375
- coarse_norm: float32 [1024], replicated, may hold values from 0.1 to 1.9
- coarse_query: bfloat16 [1024, 1024], P(None, 'head'), may hold values from -2 to 2
- coarse_key: bfloat16 [1024, 1024], P(None, 'head'), may hold values from -2 to 2
- coarse_value: bfloat16 [1024, 1024], P(None, 'head'), may hold values from -0.1875 to 0.1875
- coarse_output: bfloat16 [1024, 1024], P('head'), may hold values from -0.1875 to 0.1875
- ffn_norm: float32 [1024], replicated, may hold values from 0.1 to 1.9
- ffn_up: bfloat16 [1024, 4096], P(None, 'head'), may hold values from -0.1875 to 0.1875
- ffn_down: bfloat16 [4096, 1024], P('head'), may hold values from -0.09375 to 0.09375
- upsample_weight: bfloat16 [1024, 4, 1024], P(None, None, 'head'), may hold values from -0.1875 to 0.1875
Outputs:
- block_output: bfloat16 [32768, 1024], P('seq', 'head')
The draws below stay inside these ranges and needn't reach their ends.
All inputs are finite; a program needn't handle non-finite values.
Results may differ from the reference program's by a relative error of at most 0.0102.
Values may be sent and summed in bfloat16 or wider, within the bound.
No kernel may reach another device: no remote copies, remote signals or barrier semaphores. Data moves between devices by JAX's collectives and lax.ppermute only.
A program may use at most 128 MiB of HBM per device.

```python
import math
import jax
import jax.numpy as jnp
from jax import lax

D = 1024
HEADS = 16
HEAD_DIM = 64
FF = 4096
VOCAB = 256
SHORTEN = 4
WINDOW = 1024
TOKENS = 32768
COARSE = 8192


def draw_token_ids(key, part):
    region = 512
    region_count = TOKENS // region
    subkeys = jax.random.split(key, 5)
    centers = jax.random.randint(subkeys[0], (region_count,), 0, 256)
    spreads = jax.random.randint(subkeys[1], (region_count,), 2, 48)
    raw_noise = jax.random.randint(subkeys[2], (TOKENS,), 0, 65536)
    center_rows = jnp.repeat(centers, region)
    spread_rows = jnp.repeat(spreads, region)
    levels = jnp.clip(center_rows + raw_noise % (2 * spread_rows + 1) - spread_rows, 0, 255)
    lowest = jax.random.randint(subkeys[3], (), 0, TOKENS)
    stride = jax.random.randint(subkeys[4], (), 1, TOKENS)
    highest = (lowest + stride) % TOKENS
    levels = levels.at[lowest].set(0).at[highest].set(255)
    return levels.astype(jnp.int32)


def drawn_pair(key, which):
    base_key = jax.random.fold_in(key, which)
    first_key, second_key = jax.random.split(base_key, 2)
    columns = HEADS * HEAD_DIM
    querying = jax.random.normal(first_key, (D, columns), jnp.float32) * D ** (-0.5)
    keying = jax.random.normal(second_key, (D, columns), jnp.float32) * D ** (-0.5)
    return (jnp.clip(querying, -2.0, 2.0), jnp.clip(keying, -2.0, 2.0))


def draw_fine_query(key, part):
    return drawn_pair(key, 11)[0].astype(jnp.bfloat16)


def draw_fine_key(key, part):
    return drawn_pair(key, 11)[1].astype(jnp.bfloat16)


def draw_coarse_query(key, part):
    return drawn_pair(key, 23)[0].astype(jnp.bfloat16)


def draw_coarse_key(key, part):
    return drawn_pair(key, 23)[1].astype(jnp.bfloat16)


def shard_levels(own_key, shape, cuts, smallest, largest):
    def one(axis_at, parts):
        draws = jax.random.uniform(jax.random.fold_in(jax.random.fold_in(own_key, 6), axis_at), (parts,), jnp.float32, smallest / len(cuts), largest / len(cuts))
        return jnp.repeat(jnp.exp(draws), shape[axis_at] // parts).reshape((-1,) + (1,) * (len(shape) - axis_at - 1))

    level = one(*cuts[0])
    for cut in cuts[1:]:
        level = level * one(*cut)
    return level


def gaussian(key, extent, scale, bound, pieces=(), kind=jnp.bfloat16):
    values = scale * jax.random.normal(key, extent, jnp.float32)
    if pieces:
        values = values * shard_levels(key, extent, pieces, -0.22, 0.18)
    return jnp.clip(values, -bound, bound).astype(kind)


def setup_inputs(seed: int = 0) -> dict:
    seeds = jax.random.split(jax.random.key(seed), 18)
    return {
        "token_ids": draw_token_ids(jax.random.fold_in(seeds[17], 71), 0),
        "embedding": gaussian(seeds[1], (VOCAB, D), 1.0, 6.0),
        "fine_norm": jnp.clip(1.0 + 0.18 * jax.random.normal(seeds[2], (D,), jnp.float32), 0.1, 1.9),
        "fine_query": draw_fine_query(jax.random.fold_in(seeds[17], 71), 0),
        "fine_key": draw_fine_key(jax.random.fold_in(seeds[17], 71), 0),
        "fine_value": gaussian(seeds[5], (D, HEADS * HEAD_DIM), D ** -0.5, 0.1875, ((1, 4),)),
        "fine_output": gaussian(seeds[6], (HEADS * HEAD_DIM, D), (HEADS * HEAD_DIM) ** -0.5, 0.1875, ((0, 4),)),
        "shorten_weight": gaussian(seeds[7], (SHORTEN, D, D), (SHORTEN * D) ** -0.5, 0.09375, ((1, 4),)),
        "coarse_norm": jnp.clip(1.0 + 0.18 * jax.random.normal(seeds[8], (D,), jnp.float32), 0.1, 1.9),
        "coarse_query": draw_coarse_query(jax.random.fold_in(seeds[17], 71), 0),
        "coarse_key": draw_coarse_key(jax.random.fold_in(seeds[17], 71), 0),
        "coarse_value": gaussian(seeds[11], (D, HEADS * HEAD_DIM), D ** -0.5, 0.1875, ((1, 4),)),
        "coarse_output": gaussian(seeds[12], (HEADS * HEAD_DIM, D), (HEADS * HEAD_DIM) ** -0.5, 0.1875, ((0, 4),)),
        "ffn_norm": jnp.clip(1.0 + 0.18 * jax.random.normal(seeds[13], (D,), jnp.float32), 0.1, 1.9),
        "ffn_up": gaussian(seeds[14], (D, FF), D ** -0.5, 0.1875, ((1, 4),)),
        "ffn_down": gaussian(seeds[15], (FF, D), FF ** -0.5, 0.09375, ((0, 4),)),
        "upsample_weight": gaussian(seeds[16], (D, SHORTEN, D), D ** -0.5, 0.1875, ((2, 4),)),
    }


epsilon = 1e-06
masked_low = -1e+30

def rms_scale(values, gain):
    data = values.astype(jnp.float32)
    power = lax.optimization_barrier(jnp.mean(data * data, axis=-1, keepdims=True))
    return (data * lax.rsqrt(power + epsilon) * gain).astype(jnp.bfloat16)

def project(left, right):
    return jnp.dot(left, right, preferred_element_type=jnp.float32)

def rotate(values, positions):
    rows = values.shape[0]
    halfway = HEAD_DIM // 2
    pairs = values.reshape(rows, -1, 2, halfway)
    column_index = jnp.arange(halfway, dtype=jnp.int32)
    periods = 2 ** (4 + column_index * 14 // halfway)
    cycle = (positions[:, None] % periods[None, :]).astype(jnp.float32)
    angle = cycle * (2.0 * math.pi / periods.astype(jnp.float32))[None, :]
    cosine = jnp.cos(angle)[:, None, :]
    sine_part = jnp.sin(angle)[:, None, :]
    lower = pairs[:, :, 0]
    upper = pairs[:, :, 1]
    turned = jnp.stack([lower * cosine - upper * sine_part, upper * cosine + lower * sine_part], axis=2)
    return turned.reshape(rows, -1)

def weighted(scores, allowed, values):
    highest = lax.optimization_barrier(jnp.max(jnp.where(allowed, scores, masked_low), axis=-1, keepdims=True))
    weights = jnp.where(allowed, jnp.exp(scores - highest), 0.0)
    totals = lax.optimization_barrier(jnp.sum(weights, axis=-1))
    rounded = lax.optimization_barrier(weights.astype(jnp.bfloat16))
    mixed = jnp.einsum('hqk,khd->qhd', rounded.astype(jnp.float32), values.astype(jnp.float32))
    return mixed / jnp.transpose(totals)[:, :, None]

def fine_attention(query, keys, values):
    length = query.shape[0]
    block = min(512, length)
    padding = jnp.zeros((WINDOW,) + keys.shape[1:], keys.dtype)
    keys_long = jnp.concatenate([padding, keys])
    values_long = jnp.concatenate([padding, values])
    offsets = jnp.arange(block, dtype=jnp.int32)
    reaches = jnp.arange(block + WINDOW, dtype=jnp.int32)
    scale = HEAD_DIM ** (-0.5)

    def one_block(index):
        begin = index * block
        query_rows = lax.dynamic_slice_in_dim(query, begin, block, 0)
        key_rows = lax.dynamic_slice_in_dim(keys_long, begin, block + WINDOW, 0)
        value_rows = lax.dynamic_slice_in_dim(values_long, begin, block + WINDOW, 0)
        scores = jnp.einsum('qhd,khd->hqk', query_rows.astype(jnp.float32), key_rows.astype(jnp.float32)) * scale
        allowed = (reaches[None, :] > offsets[:, None]) & (reaches[None, :] <= offsets[:, None] + WINDOW) & (begin + reaches[None, :] >= WINDOW)
        return weighted(scores, allowed[None], value_rows)
    mixed = lax.map(one_block, jnp.arange(length // block, dtype=jnp.int32))
    return mixed.reshape(length, -1).astype(jnp.bfloat16)

def coarse_attention(query, keys, values):
    length = query.shape[0]
    block = min(512, length)
    positions = jnp.arange(length, dtype=jnp.int32)
    offsets = jnp.arange(block, dtype=jnp.int32)
    scale = HEAD_DIM ** (-0.5)

    def one_block(index):
        begin = index * block
        query_rows = lax.dynamic_slice_in_dim(query, begin, block, 0)
        scores = jnp.einsum('qhd,khd->hqk', query_rows.astype(jnp.float32), keys.astype(jnp.float32)) * scale
        allowed = positions[None, :] <= begin + offsets[:, None]
        return weighted(scores, allowed[None], values)
    mixed = lax.map(one_block, jnp.arange(length // block, dtype=jnp.int32))
    return mixed.reshape(length, -1).astype(jnp.bfloat16)

def split_heads(values):
    return values.reshape(values.shape[0], HEADS, HEAD_DIM)

def reference(token_ids, embedding, fine_norm, fine_query, fine_key, fine_value, fine_output, shorten_weight, coarse_norm, coarse_query, coarse_key, coarse_value, coarse_output, ffn_norm, ffn_up, ffn_down, upsample_weight):
    fine_pos = jnp.arange(TOKENS, dtype=jnp.int32)
    coarse_pos = jnp.arange(COARSE, dtype=jnp.int32)
    start = embedding[token_ids]
    fine_in = rms_scale(start, fine_norm)
    fine_q = split_heads(rotate(project(fine_in, fine_query), fine_pos).astype(jnp.bfloat16))
    fine_k = split_heads(rotate(project(fine_in, fine_key), fine_pos).astype(jnp.bfloat16))
    fine_v = split_heads(project(fine_in, fine_value).astype(jnp.bfloat16))
    fine_mixed = fine_attention(fine_q, fine_k, fine_v)
    fine = (start.astype(jnp.float32) + project(fine_mixed, fine_output)).astype(jnp.bfloat16)
    padded = jnp.concatenate([jnp.zeros((SHORTEN - 1, D), jnp.bfloat16), fine])
    grouped = jnp.concatenate([padded[offset:offset + TOKENS:SHORTEN] for offset in range(SHORTEN)], axis=1)
    short = project(grouped, shorten_weight.reshape(SHORTEN * D, D)).astype(jnp.bfloat16)
    coarse_in = rms_scale(short, coarse_norm)
    coarse_q = split_heads(rotate(project(coarse_in, coarse_query), coarse_pos).astype(jnp.bfloat16))
    coarse_k = split_heads(rotate(project(coarse_in, coarse_key), coarse_pos).astype(jnp.bfloat16))
    coarse_v = split_heads(project(coarse_in, coarse_value).astype(jnp.bfloat16))
    coarse_mixed = coarse_attention(coarse_q, coarse_k, coarse_v)
    first = short.astype(jnp.float32) + project(coarse_mixed, coarse_output)
    inner = jax.nn.gelu(project(rms_scale(first, ffn_norm), ffn_up)).astype(jnp.bfloat16)
    second = (first + project(inner, ffn_down)).astype(jnp.bfloat16)
    lifted = project(second, upsample_weight.reshape(D, SHORTEN * D)).reshape(TOKENS, D)
    return (fine.astype(jnp.float32) + lifted).astype(jnp.bfloat16)
```

```python
import functools
import math

import jax
import jax.numpy as jnp
import numpy as np
from jax import lax
from jax.experimental import pallas as pl
from jax.experimental.pallas import tpu as pltpu
from jax.sharding import Mesh
from jax.sharding import PartitionSpec as P

D = 1024
HEAD_DIM = 64
SHORTEN = 4
WINDOW = 1024
BLOCK = 256
HALO = 16
ROWS = 1024
PAST = WINDOW + BLOCK
KEYS = PAST + ROWS
SHARE = 256
COARSE_ROWS = 256
SEQ = ("z", "x", "core")

epsilon = 1e-06
masked_low = -1e30
q_scale = HEAD_DIM ** (-0.5) * math.log2(math.e)
bf16 = jnp.bfloat16
f32 = jnp.float32


def angle_tables():
    lane = np.arange(128) % 32
    period = 2.0 ** (4 + lane * 14 // 32)
    coarse = (256.0 * np.arange(32)[:, None]) % period[None]
    near = np.arange(256)[:, None] % period[None]
    a = coarse * (2.0 * np.pi / period)[None]
    b = near * (2.0 * np.pi / period)[None]
    return [t.astype(np.float32) for t in (np.cos(a), np.sin(a), np.cos(b), np.sin(b))]


def shift(value, axis, steps, count):
    return lax.ppermute(value, axis, [(i, (i + steps) % count) for i in range(count)])


def later(value, axis, steps, count):
    return lax.ppermute(value, axis, [(i, i + steps) for i in range(count - steps)])


def exchange(block_for, axis, count):
    me = lax.axis_index(axis)
    got = [block_for(me)]
    for s in range(1, count):
        got.append(shift(block_for((me + s) % count), axis, s, count))
    return got


def dot(left, right):
    return jnp.dot(left, right, preferred_element_type=f32)


def dot_t(left, right):
    return lax.dot_general(left, right, (((1,), (1,)), ((), ())), preferred_element_type=f32)


def norm_rows(data, gain):
    power = jnp.mean(data * data, axis=-1, keepdims=True)
    return (data * lax.rsqrt(power + epsilon) * gain).astype(bf16)


def partner(values):
    width = values.shape[1]
    lane = lax.broadcasted_iota(jnp.int32, values.shape, 1)
    ahead = pltpu.roll(values, width - 32, 1)
    behind = pltpu.roll(values, 32, 1)
    return jnp.where(lane % 64 < 32, -ahead, behind)


def halves(table):
    high = table.astype(bf16)
    low = (table - high.astype(f32)).astype(bf16)
    return high, low


def fine_kernel(
    place_ref, ids_ref, emb_ref, gain_ref, wq_ref, wk_ref, wv_ref,
    ca_ref, sa_ref, cb_ref, sb_ref,
    out_ref, q_ref, k_ref, v_ref, tab_ref,
):
    step = pl.program_id(0)
    lowest = jnp.maximum(PAST - place_ref[0] * ROWS, 0)
    head_lane = lax.broadcasted_iota(jnp.int32, (1, SHARE), 1) // HEAD_DIM

    @pl.when(step == 0)
    def _():
        fine_in = norm_rows(emb_ref[...].astype(f32), gain_ref[...])
        tq = dot(fine_in, wq_ref[...]) * q_scale
        tk = dot(fine_in, wk_ref[...])
        for n, table in enumerate((tq, partner(tq), tk, partner(tk))):
            high, low = halves(table)
            tab_ref[2 * n] = high
            tab_ref[2 * n + 1] = low
        tab_ref[8] = dot(fine_in, wv_ref[...]).astype(bf16)
        cb = cb_ref[...]
        sb = sb_ref[...]

        def build(block, _):
            begin = pl.multiple_of(block * BLOCK, BLOCK)
            ids = ids_ref[pl.ds(begin, BLOCK), :]
            levels = lax.broadcasted_iota(jnp.int32, (BLOCK, 256), 1)
            hot = (ids == levels).astype(f32).astype(bf16)
            ca = ca_ref[pl.ds(block, 1), :]
            sa = sa_ref[pl.ds(block, 1), :]
            cosine = ca * cb - sa * sb
            sine = sa * cb + ca * sb
            cosine = jnp.concatenate([cosine, cosine], axis=1)
            sine = jnp.concatenate([sine, sine], axis=1)

            def turned(n):
                plain = dot(hot, tab_ref[n]) + dot(hot, tab_ref[n + 1])
                other = dot(hot, tab_ref[n + 2]) + dot(hot, tab_ref[n + 3])
                return (plain * cosine + other * sine).astype(bf16)

            k_ref[pl.ds(begin, BLOCK), :] = turned(4)
            v_ref[pl.ds(begin, BLOCK), :] = dot(hot, tab_ref[8]).astype(bf16)

            @pl.when(block >= PAST // BLOCK - 1)
            def _():
                at = pl.multiple_of(begin - (PAST - BLOCK), BLOCK)
                q_ref[pl.ds(at, BLOCK), :] = turned(0)

            return 0

        lax.fori_loop(0, KEYS // BLOCK, build, 0)

        halo_q = q_ref[BLOCK - HALO : BLOCK, :]
        stacked = jnp.concatenate(
            [jnp.where(head_lane == h, halo_q, jnp.zeros_like(halo_q)) for h in range(4)], axis=0
        )
        scores = dot_t(stacked, k_ref[0:PAST, :])
        row = lax.broadcasted_iota(jnp.int32, scores.shape, 0) % HALO + (PAST - HALO)
        col = lax.broadcasted_iota(jnp.int32, scores.shape, 1)
        allowed = (col <= row) & (col > row - WINDOW) & (col >= lowest)
        scores = jnp.where(allowed, scores, masked_low)
        top = jnp.max(scores, axis=1, keepdims=True)
        weights = jnp.exp2(scores - top)
        total = jnp.sum(weights, axis=1, keepdims=True)
        mixed = dot(weights.astype(bf16), v_ref[0:PAST, :]) / total
        result = jnp.zeros((HALO, SHARE), f32)
        for h in range(4):
            result = jnp.where(head_lane == h, mixed[h * HALO : (h + 1) * HALO], result)
        out_ref[0:HALO, :] = result.astype(bf16)

    begin = pl.multiple_of((step + 1) * BLOCK, BLOCK)
    keys = k_ref[pl.ds(begin, PAST), :]
    values = v_ref[pl.ds(begin, PAST), :]
    query = q_ref[pl.ds(begin, BLOCK), :]
    row = lax.broadcasted_iota(jnp.int32, (BLOCK, BLOCK), 0)
    col = lax.broadcasted_iota(jnp.int32, (BLOCK, BLOCK), 1)
    biases = [
        jnp.where(begin + t * BLOCK >= lowest, 0.0, masked_low).astype(f32) for t in range(4)
    ]
    first_bias = jnp.where(col > row, 0.0, masked_low) + biases[0]
    last_bias = jnp.where(col <= row, 0.0, masked_low)
    result = jnp.zeros((BLOCK, SHARE), f32)
    for h in range(4):
        scores = dot_t(jnp.where(head_lane == h, query, jnp.zeros_like(query)), keys)
        tiles = [scores[:, t * BLOCK : (t + 1) * BLOCK] for t in range(5)]
        tiles = (
            [tiles[0] + first_bias]
            + [tiles[t] + biases[t] for t in range(1, 4)]
            + [tiles[4] + last_bias]
        )
        peak = tiles[0]
        for t in range(1, 5):
            peak = jnp.maximum(peak, tiles[t])
        top = jnp.max(peak, axis=1, keepdims=True)
        weights = [jnp.exp2(tile - top) for tile in tiles]
        summed = weights[0]
        for t in range(1, 5):
            summed = summed + weights[t]
        total = jnp.sum(summed, axis=1, keepdims=True)
        mixed = dot(jnp.concatenate([w.astype(bf16) for w in weights], axis=1), values)
        result = jnp.where(head_lane == h, mixed / total, result)
    at = pl.multiple_of(HALO + step * BLOCK, HALO)
    out_ref[pl.ds(at, BLOCK), :] = result.astype(bf16)


def vmem():
    return pl.BlockSpec(memory_space=pltpu.VMEM)


def smem():
    return pl.BlockSpec(memory_space=pltpu.SMEM)


def fine_attention(place, ids, embedding, gain, wq, wk, wv, tables):
    return pl.pallas_call(
        fine_kernel,
        grid=(4,),
        out_shape=jax.ShapeDtypeStruct((HALO + ROWS, SHARE), bf16),
        in_specs=[smem()] + [vmem()] * 10,
        out_specs=vmem(),
        scratch_shapes=[
            pltpu.VMEM((BLOCK + ROWS, SHARE), bf16),
            pltpu.VMEM((KEYS, SHARE), bf16),
            pltpu.VMEM((KEYS, SHARE), bf16),
            pltpu.VMEM((9, 256, SHARE), bf16),
        ],
        compiler_params=pltpu.CompilerParams(vmem_limit_bytes=48 << 20),
        name="fine_attention",
    )(place, ids, embedding, gain, wq, wk, wv, *tables)


def coarse_pack_kernel(place_ref, x_ref, wq_ref, wk_ref, wv_ref, ca_ref, sa_ref, cb_ref, sb_ref, out_ref):
    x = x_ref[...]
    place = place_ref[0]
    ca = ca_ref[pl.ds(place, 1), :]
    sa = sa_ref[pl.ds(place, 1), :]
    cb = cb_ref[...]
    sb = sb_ref[...]
    cosine = ca * cb - sa * sb
    sine = sa * cb + ca * sb
    cosine = jnp.concatenate([cosine, cosine], axis=1)
    sine = jnp.concatenate([sine, sine], axis=1)

    def turned(values):
        return values * cosine + partner(values) * sine

    q = turned(dot(x, wq_ref[...])) * q_scale
    k = turned(dot(x, wk_ref[...]))
    v = dot(x, wv_ref[...])
    low_lanes = lax.broadcasted_iota(jnp.int32, (1, 128), 1) < 64
    half = COARSE_ROWS // 2
    for h in range(4):
        pair = (h // 2) * 128
        kp = k[:, pair : pair + 128]
        vp = v[:, pair : pair + 128]
        qp = q[:, pair : pair + 128]
        if h % 2 == 0:
            kv = jnp.where(low_lanes, kp, pltpu.roll(vp, 64, 1))
            qq = jnp.where(low_lanes, qp[:half], pltpu.roll(qp[half:], 64, 1))
        else:
            kv = jnp.where(low_lanes, pltpu.roll(kp, 64, 1), vp)
            qq = jnp.where(low_lanes, pltpu.roll(qp[:half], 64, 1), qp[half:])
        out_ref[h, 0:COARSE_ROWS, :] = kv.astype(bf16)
        out_ref[h, COARSE_ROWS : COARSE_ROWS + half, :] = qq.astype(bf16)


def coarse_pack(place, x, wq, wk, wv, tables):
    return pl.pallas_call(
        coarse_pack_kernel,
        out_shape=jax.ShapeDtypeStruct((4, COARSE_ROWS * 3 // 2, 128), bf16),
        in_specs=[smem()] + [vmem()] * 8,
        out_specs=vmem(),
        compiler_params=pltpu.CompilerParams(vmem_limit_bytes=32 << 20),
        name="coarse_pack",
    )(place, x, wq, wk, wv, *tables)


def coarse_kernel(chunk_ref, q_ref, near_ref, far_ref, out_ref, q_all, top_ref, total_ref, acc_ref):
    half = COARSE_ROWS // 2
    low_lanes = lax.broadcasted_iota(jnp.int32, (1, 128), 1) < 64
    for z in range(4):
        packed = q_ref[z].astype(f32)
        zero = jnp.zeros_like(packed)
        q_all[z * 256 : z * 256 + half, :] = jnp.where(low_lanes, packed, zero).astype(bf16)
        q_all[z * 256 + half : (z + 1) * 256, :] = jnp.where(
            low_lanes, pltpu.roll(packed, 64, 1), zero
        ).astype(bf16)
    row = lax.broadcasted_iota(jnp.int32, (256, 256), 0)
    col = lax.broadcasted_iota(jnp.int32, (256, 256), 1)
    for z in range(4):
        kv = near_ref[0, z]
        at = pl.ds(z * 256, 256)
        scores = jnp.where(col <= row, dot_t(q_all[at, :], kv), masked_low)
        top = jnp.max(scores, axis=1, keepdims=True)
        weights = jnp.exp2(scores - top)
        top_ref[at, :] = jnp.broadcast_to(top, (256, 128))
        total_ref[at, :] = jnp.broadcast_to(jnp.sum(weights, axis=1, keepdims=True), (256, 128))
        acc_ref[at, :] = dot(weights.astype(bf16), kv)

    def absorb(begin, rows, parts):
        at = pl.ds(begin, rows)
        query = q_all[at, :]
        scores = [dot_t(query, kv) for kv in parts]
        peak = scores[0]
        for s in scores[1:]:
            peak = jnp.maximum(peak, s)
        old = top_ref[at, :]
        top = jnp.maximum(old, jnp.max(peak, axis=1, keepdims=True))
        factor = jnp.exp2(old - top)
        both = jnp.concatenate([top, top], axis=1)
        weights = [jnp.exp2(s - both) for s in scores]
        summed = weights[0]
        for w in weights[1:]:
            summed = summed + w
        contrib = dot(weights[0].astype(bf16), parts[0])
        for w, kv in zip(weights[1:], parts[1:]):
            contrib = contrib + dot(w.astype(bf16), kv)
        top_ref[at, :] = top
        total_ref[at, :] = total_ref[at, :] * factor + jnp.sum(summed, axis=1, keepdims=True)
        acc_ref[at, :] = acc_ref[at, :] * factor + contrib

    for s in range(4):
        for z in range(3):
            absorb((z + 1) * 256, (3 - z) * 256, [near_ref[s, z], far_ref[s, z]])

    for s in range(4):
        for n, ref in enumerate((near_ref, far_ref)):
            if s == 0 and n == 0:
                continue

            @pl.when(chunk_ref[2 * s + n] < chunk_ref[0])
            def _(ref=ref, s=s):
                for z in range(4):
                    absorb(z * 256, 256, [ref[s, z]])

    mixed = acc_ref[...] / total_ref[...]
    out_ref[...] = pltpu.roll(mixed, 64, 1)[:, :64].astype(bf16)


def coarse_attention(chunks, q, near, far):
    return pl.pallas_call(
        coarse_kernel,
        out_shape=jax.ShapeDtypeStruct((1024, 64), bf16),
        in_specs=[smem()] + [vmem()] * 3,
        out_specs=vmem(),
        scratch_shapes=[
            pltpu.VMEM((1024, 128), bf16),
            pltpu.VMEM((1024, 128), f32),
            pltpu.VMEM((1024, 128), f32),
            pltpu.VMEM((1024, 128), f32),
        ],
        compiler_params=pltpu.CompilerParams(vmem_limit_bytes=48 << 20),
        name="coarse_attention",
    )(chunks, q, near, far)


def to_shares(values):
    rows = values.shape[0] // 4
    return lax.all_to_all(values.reshape(4, rows, -1), "head", 0, 0)


def everyone(values):
    wide = jnp.broadcast_to(values[None], (4, *values.shape))
    return lax.all_to_all(wide, "head", 0, 0).reshape(-1, values.shape[-1])


def local(
    token_ids, embedding, fine_norm, fine_query, fine_key, fine_value, fine_output,
    shorten_weight, coarse_norm, coarse_query, coarse_key, coarse_value, coarse_output,
    ffn_norm, ffn_up, ffn_down, upsample_weight,
):
    place = lax.axis_index(SEQ).astype(jnp.int32)
    head_place = lax.axis_index("head")
    x_place = lax.axis_index("x").astype(jnp.int32)
    core_place = lax.axis_index("core").astype(jnp.int32)
    tables = [jnp.asarray(t) for t in angle_tables()]
    place_1 = place[None]

    prior = later(token_ids, SEQ, 1, 32)
    before = later(token_ids[ROWS - BLOCK :], SEQ, 2, 32)
    all_ids = jnp.concatenate([before, prior, token_ids])
    outputs = [fine_output] + [shift(fine_output, "head", s, 4) for s in range(1, 4)]

    mixed = fine_attention(
        place_1, all_ids[:, None], embedding, fine_norm[None], fine_query, fine_key, fine_value, tables
    )

    got = exchange(
        lambda d: lax.dynamic_slice_in_dim(mixed, d * 256, 256 + HALO, 0), "head", 4
    )
    own_ids = lax.dynamic_slice_in_dim(
        all_ids, PAST - HALO + head_place * 256, 256 + HALO, 0
    )
    hot = (own_ids[:, None] == jnp.arange(256, dtype=jnp.int32)[None]).astype(bf16)
    start = dot(hot, embedding)
    merged = start
    for part, weight in zip(got, outputs):
        merged = merged + dot(part, weight)
    token = place * ROWS + head_place * 256 - HALO + jnp.arange(256 + HALO, dtype=jnp.int32)
    fine_rows = jnp.where(token[:, None] >= 0, merged, 0.0).astype(bf16)

    by_feature = lax.all_to_all(
        fine_rows.reshape(256 + HALO, 4, SHARE), "head", 1, 0, tiled=False
    )
    flat = by_feature.reshape(4 * (256 + HALO), SHARE)
    m_index = jnp.arange(COARSE_ROWS, dtype=jnp.int32)
    column = jnp.arange(4 * (256 + HALO), dtype=jnp.int32)
    pieces = []
    for r in range(SHORTEN):
        t = 4 * m_index + r - 3
        quarter = jnp.maximum(t, 0) // 256
        source = quarter * (256 + HALO) + HALO + (t - quarter * 256)
        choose = (source[:, None] == column[None]).astype(bf16)
        pieces.append(dot(choose, flat).astype(bf16))
    grouped = jnp.concatenate(pieces, axis=1)
    short_terms = dot(grouped, shorten_weight.reshape(SHORTEN * SHARE, D)).astype(bf16)
    short = jnp.sum(to_shares(short_terms).astype(f32), axis=0).astype(bf16)
    short_f = short.astype(f32)

    coarse_in = everyone(norm_rows(short_f, coarse_norm))
    packed = coarse_pack(place_1, coarse_in, coarse_query, coarse_key, coarse_value, tables)
    turned = lax.all_to_all(packed, "z", 0, 0)
    q = turned[:, COARSE_ROWS:]
    kv = turned[:, :COARSE_ROWS]
    near = jnp.stack([kv] + [shift(kv, "x", s, 4) for s in range(1, 4)])
    far = shift(near, "core", 1, 2)
    steps = jnp.arange(4, dtype=jnp.int32)
    columns_x = (x_place - steps + 4) % 4
    chunks = jnp.stack([2 * columns_x + core_place, 2 * columns_x + 1 - core_place], axis=1).reshape(8)
    attended = coarse_attention(chunks, q, near, far)

    heads_in = lax.all_to_all(attended.reshape(16, 64, 64), ("z", "head"), 0, 0)
    coarse_mixed = (
        heads_in.reshape(4, 4, 64, 64).transpose(2, 1, 0, 3).reshape(64, D)
    )
    coarse_full = lax.all_gather(coarse_output, "head", axis=0, tiled=True)
    first = short_f + dot(coarse_mixed, coarse_full)
    ffn_in = everyone(norm_rows(first, ffn_norm))
    inner = jax.nn.gelu(dot(ffn_in, ffn_up)).astype(bf16)
    partial = dot(inner, ffn_down).astype(bf16)
    second = (first + jnp.sum(to_shares(partial).astype(f32), axis=0)).astype(bf16)
    second_all = everyone(second)
    lifted = dot(second_all, upsample_weight.reshape(D, SHORTEN * SHARE)).reshape(ROWS, SHARE)
    fine = by_feature[:, HALO:].reshape(ROWS, SHARE)
    return (fine.astype(f32) + lifted).astype(bf16)


def solution(mesh):
    split = Mesh(mesh.devices.reshape(4, 4, 2, 4), ("z", "x", "core", "head"))
    return jax.shard_map(
        local,
        mesh=split,
        in_specs=(
            P(SEQ), P(), P(), P(None, "head"), P(None, "head"), P(None, "head"), P("head", None),
            P(None, "head", None), P(), P(None, "head"), P(None, "head"), P(None, "head"),
            P("head", None), P(), P(None, "head"), P("head", None), P(None, None, "head"),
        ),
        out_specs=P(SEQ, "head"),
        check_vma=False,
    )
```

```python
import functools
import math

import jax
import jax.numpy as jnp
import numpy as np
from jax import lax
from jax.experimental import pallas as pl
from jax.experimental.pallas import tpu as pltpu
from jax.sharding import Mesh
from jax.sharding import PartitionSpec as P

D = 1024
HEAD_DIM = 64
SHORTEN = 4
WINDOW = 1024
BLOCK = 256
HALO = 16
ROWS = 1024
PAST = WINDOW + BLOCK
KEYS = PAST + ROWS
SHARE = 256
COARSE_ROWS = 256
SEQ = ("z", "x", "core")

epsilon = 1e-06
masked_low = -1e30
q_scale = HEAD_DIM ** (-0.5) * math.log2(math.e)
bf16 = jnp.bfloat16
f32 = jnp.float32


def angle_tables():
    lane = np.arange(128) % 32
    period = 2.0 ** (4 + lane * 14 // 32)
    coarse = (256.0 * np.arange(32)[:, None]) % period[None]
    near = np.arange(256)[:, None] % period[None]
    a = coarse * (2.0 * np.pi / period)[None]
    b = near * (2.0 * np.pi / period)[None]
    return [t.astype(np.float32) for t in (np.cos(a), np.sin(a), np.cos(b), np.sin(b))]


def shift(value, axis, steps, count):
    return lax.ppermute(value, axis, [(i, (i + steps) % count) for i in range(count)])


def later(value, axis, steps, count):
    return lax.ppermute(value, axis, [(i, i + steps) for i in range(count - steps)])


def exchange(block_for, axis, count):
    me = lax.axis_index(axis)
    got = [block_for(me)]
    for s in range(1, count):
        got.append(shift(block_for((me + s) % count), axis, s, count))
    return got


def dot(left, right):
    return jnp.dot(left, right, preferred_element_type=f32)


def dot_t(left, right):
    return lax.dot_general(left, right, (((1,), (1,)), ((), ())), preferred_element_type=f32)


def norm_rows(data, gain):
    power = jnp.mean(data * data, axis=-1, keepdims=True)
    return (data * lax.rsqrt(power + epsilon) * gain).astype(bf16)


def partner(values):
    width = values.shape[1]
    lane = lax.broadcasted_iota(jnp.int32, values.shape, 1)
    ahead = pltpu.roll(values, width - 32, 1)
    behind = pltpu.roll(values, 32, 1)
    return jnp.where(lane % 64 < 32, -ahead, behind)


def halves(table):
    high = table.astype(bf16)
    low = (table - high.astype(f32)).astype(bf16)
    return high, low


def turn_tables(ca, sa, cb, sb):
    cosine = ca * cb - sa * sb
    sine = sa * cb + ca * sb
    return jnp.concatenate([cosine, cosine], axis=1), jnp.concatenate([sine, sine], axis=1)


def pick(ids, levels=256):
    columns = lax.broadcasted_iota(jnp.int32, (ids.shape[0], levels), 1)
    return (ids == columns).astype(f32).astype(bf16)


def turned_rows(hot, tab_ref, n, cosine, sine):
    plain = dot(hot, tab_ref[n]) + dot(hot, tab_ref[n + 1])
    other = dot(hot, tab_ref[n + 2]) + dot(hot, tab_ref[n + 3])
    return (plain * cosine + other * sine).astype(bf16)


def fine_own_kernel(
    ids_ref, emb_ref, gain_ref, wq_ref, wk_ref, wv_ref, ca_ref, sa_ref, cb_ref, sb_ref,
    tab_ref, q_ref, k_ref, v_ref,
):
    fine_in = norm_rows(emb_ref[...].astype(f32), gain_ref[...])
    tq = dot(fine_in, wq_ref[...]) * q_scale
    tk = dot(fine_in, wk_ref[...])
    for n, table in enumerate((tq, partner(tq), tk, partner(tk))):
        high, low = halves(table)
        tab_ref[2 * n] = high
        tab_ref[2 * n + 1] = low
    tab_ref[8] = dot(fine_in, wv_ref[...]).astype(bf16)
    cb = cb_ref[...]
    sb = sb_ref[...]
    for block in range(ROWS // BLOCK):
        at = slice(block * BLOCK, (block + 1) * BLOCK)
        hot = pick(ids_ref[at, :])
        far = PAST // BLOCK + block
        cosine, sine = turn_tables(ca_ref[far : far + 1, :], sa_ref[far : far + 1, :], cb, sb)
        q_ref[at, :] = turned_rows(hot, tab_ref, 0, cosine, sine)
        k_ref[at, :] = turned_rows(hot, tab_ref, 4, cosine, sine)
        v_ref[at, :] = dot(hot, tab_ref[8]).astype(bf16)


def fine_kernel(
    place_ref, ids_ref, tab_ref, q_ref, k_own_ref, v_own_ref, ca_ref, sa_ref, cb_ref, sb_ref,
    out_ref, k_ref, v_ref,
):
    step = pl.program_id(0)
    lowest = jnp.maximum(PAST - place_ref[0] * ROWS, 0)
    head_lane = lax.broadcasted_iota(jnp.int32, (1, SHARE), 1) // HEAD_DIM

    @pl.when(step == 0)
    def _():
        cb = cb_ref[...]
        sb = sb_ref[...]
        k_ref[PAST:, :] = k_own_ref[...]
        v_ref[PAST:, :] = v_own_ref[...]
        for block in range(PAST // BLOCK):
            at = slice(block * BLOCK, (block + 1) * BLOCK)
            hot = pick(ids_ref[at, :])
            cosine, sine = turn_tables(
                ca_ref[block : block + 1, :], sa_ref[block : block + 1, :], cb, sb
            )
            k_ref[at, :] = turned_rows(hot, tab_ref, 4, cosine, sine)
            v_ref[at, :] = dot(hot, tab_ref[8]).astype(bf16)

        halo_q = turned_rows(
            pick(ids_ref[PAST - HALO : PAST, :]), tab_ref, 0, cosine[-HALO:], sine[-HALO:]
        )
        stacked = jnp.concatenate(
            [jnp.where(head_lane == h, halo_q, jnp.zeros_like(halo_q)) for h in range(4)], axis=0
        )
        scores = dot_t(stacked, k_ref[0:PAST, :])
        row = lax.broadcasted_iota(jnp.int32, scores.shape, 0) % HALO + (PAST - HALO)
        col = lax.broadcasted_iota(jnp.int32, scores.shape, 1)
        allowed = (col <= row) & (col > row - WINDOW) & (col >= lowest)
        scores = jnp.where(allowed, scores, masked_low)
        top = jnp.max(scores, axis=1, keepdims=True)
        weights = jnp.exp2(scores - top)
        total = jnp.sum(weights, axis=1, keepdims=True)
        mixed = dot(weights.astype(bf16), v_ref[0:PAST, :]) / total
        result = jnp.zeros((HALO, SHARE), f32)
        for h in range(4):
            result = jnp.where(head_lane == h, mixed[h * HALO : (h + 1) * HALO], result)
        out_ref[0:HALO, :] = result.astype(bf16)

    begin = pl.multiple_of((step + 1) * BLOCK, BLOCK)
    keys = k_ref[pl.ds(begin, PAST), :]
    values = v_ref[pl.ds(begin, PAST), :]
    query = q_ref[pl.ds(pl.multiple_of(step * BLOCK, BLOCK), BLOCK), :]
    row = lax.broadcasted_iota(jnp.int32, (BLOCK, BLOCK), 0)
    col = lax.broadcasted_iota(jnp.int32, (BLOCK, BLOCK), 1)
    biases = [
        jnp.where(begin + t * BLOCK >= lowest, 0.0, masked_low).astype(f32) for t in range(4)
    ]
    first_bias = jnp.where(col > row, 0.0, masked_low) + biases[0]
    last_bias = jnp.where(col <= row, 0.0, masked_low)
    result = jnp.zeros((BLOCK, SHARE), f32)
    for h in range(4):
        scores = dot_t(jnp.where(head_lane == h, query, jnp.zeros_like(query)), keys)
        tiles = [scores[:, t * BLOCK : (t + 1) * BLOCK] for t in range(5)]
        tiles = (
            [tiles[0] + first_bias]
            + [tiles[t] + biases[t] for t in range(1, 4)]
            + [tiles[4] + last_bias]
        )
        peak = tiles[0]
        for t in range(1, 5):
            peak = jnp.maximum(peak, tiles[t])
        top = jnp.max(peak, axis=1, keepdims=True)
        weights = [jnp.exp2(tile - top) for tile in tiles]
        summed = weights[0]
        for t in range(1, 5):
            summed = summed + weights[t]
        total = jnp.sum(summed, axis=1, keepdims=True)
        mixed = dot(jnp.concatenate([w.astype(bf16) for w in weights], axis=1), values)
        result = jnp.where(head_lane == h, mixed / total, result)
    at = pl.multiple_of(HALO + step * BLOCK, HALO)
    out_ref[pl.ds(at, BLOCK), :] = result.astype(bf16)


def vmem():
    return pl.BlockSpec(memory_space=pltpu.VMEM)


def smem():
    return pl.BlockSpec(memory_space=pltpu.SMEM)


def call(kernel, name, shapes, scalars, arrays, scratch=(), grid=None, limit=48):
    one = not isinstance(shapes, (list, tuple))
    extra = {} if grid is None else {"grid": grid}
    return pl.pallas_call(
        kernel,
        out_shape=shapes,
        in_specs=[smem()] * len(scalars) + [vmem()] * len(arrays),
        out_specs=vmem() if one else [vmem()] * len(shapes),
        scratch_shapes=list(scratch),
        compiler_params=pltpu.CompilerParams(vmem_limit_bytes=limit << 20),
        name=name,
        **extra,
    )(*scalars, *arrays)


def half_lanes(ref, quarter, half):
    begin = pl.multiple_of(quarter * 256 + half * 128, 128)
    return ref[:, pl.ds(begin, 128)]


def fine_rows_kernel(
    where_ref, ids_ref, emb_ref, g0, g1, g2, g3, own_ref, mine_ref, other_ref, out_ref
):
    place, head, core = where_ref[0], where_ref[1], where_ref[2]
    merged = dot(pick(ids_ref[...]), emb_ref[...]) + dot(g0[...], own_ref[...])
    for s, got in ((1, g1), (2, g2), (3, g3)):
        merged += dot(half_lanes(got, 0, core), mine_ref[s - 1])
        merged += dot(half_lanes(got, 0, 1 - core), other_ref[s - 1])
    rows = 256 + HALO
    token = (
        place * ROWS + head * 256 - HALO + lax.broadcasted_iota(jnp.int32, (rows, D), 0)
    )
    fine = jnp.where(token >= 0, merged, 0.0).astype(bf16)
    index = lax.broadcasted_iota(jnp.int32, (256, rows), 0)
    column = lax.broadcasted_iota(jnp.int32, (256, rows), 1)
    source = 4 * (index % 64) + index // 64 + (HALO - 3)
    choose = (source == column).astype(f32).astype(bf16)
    grouped = dot(choose, fine).astype(bf16)
    for d in range(4):
        out_ref[d, 0:256, :] = grouped[:, d * SHARE : (d + 1) * SHARE]
        out_ref[d, 256:rows, :] = fine[256:rows, d * SHARE : (d + 1) * SHARE]


def short_part_kernel(group_ref, w_ref, out_ref):
    total = dot(group_ref[0:64, :], w_ref[0])
    for r in range(1, SHORTEN):
        total += dot(group_ref[r * 64 : (r + 1) * 64, :], w_ref[r])
    out_ref[...] = total.astype(bf16)


def coarse_pack_kernel(
    where_ref, s0, s1, s2, s3, gain_ref, wq_ref, wk_ref, wv_ref, ca_ref, sa_ref, cb_ref, sb_ref,
    out_ref, short_ref,
):
    place, head = where_ref[0], where_ref[1]
    for s, ref in enumerate((s0, s1, s2, s3)):
        begin = pl.multiple_of(lax.rem(head - s + 4, 4) * 64, 64)
        short_ref[pl.ds(begin, 64), :] = ref[...]
    x = norm_rows(short_ref[...].astype(f32), gain_ref[...])
    cosine, sine = turn_tables(
        ca_ref[pl.ds(place, 1), :], sa_ref[pl.ds(place, 1), :], cb_ref[...], sb_ref[...]
    )

    def turned(values):
        return values * cosine + partner(values) * sine

    q = turned(dot(x, wq_ref[...])) * q_scale
    k = turned(dot(x, wk_ref[...]))
    v = dot(x, wv_ref[...])
    low_lanes = lax.broadcasted_iota(jnp.int32, (1, 128), 1) < 64
    half = COARSE_ROWS // 2
    for h in range(4):
        pair = (h // 2) * 128
        kp = k[:, pair : pair + 128]
        vp = v[:, pair : pair + 128]
        qp = q[:, pair : pair + 128]
        if h % 2 == 0:
            kv = jnp.where(low_lanes, kp, pltpu.roll(vp, 64, 1))
            qq = jnp.where(low_lanes, qp[:half], pltpu.roll(qp[half:], 64, 1))
        else:
            kv = jnp.where(low_lanes, pltpu.roll(kp, 64, 1), vp)
            qq = jnp.where(low_lanes, pltpu.roll(qp[:half], 64, 1), qp[half:])
        out_ref[h, 0:COARSE_ROWS, :] = kv.astype(bf16)
        out_ref[h, COARSE_ROWS : COARSE_ROWS + half, :] = qq.astype(bf16)


def absorb(q_ref, top_ref, total_ref, acc_ref, begin, rows, parts):
    at = pl.ds(begin, rows)
    query = q_ref[at, :]
    scores = [dot_t(query, kv) for kv in parts]
    peak = scores[0]
    for s in scores[1:]:
        peak = jnp.maximum(peak, s)
    old = top_ref[at, :]
    top = jnp.maximum(old, jnp.max(peak, axis=1, keepdims=True))
    factor = jnp.exp2(old - top)
    both = jnp.concatenate([top, top], axis=1)
    weights = [jnp.exp2(s - both) for s in scores]
    summed = weights[0]
    for w in weights[1:]:
        summed = summed + w
    contrib = dot(weights[0].astype(bf16), parts[0])
    for w, kv in zip(weights[1:], parts[1:]):
        contrib = contrib + dot(w.astype(bf16), kv)
    top_ref[at, :] = top
    total_ref[at, :] = total_ref[at, :] * factor + jnp.sum(summed, axis=1, keepdims=True)
    acc_ref[at, :] = acc_ref[at, :] * factor + contrib


def coarse_first_kernel(turned_ref, q_ref, top_ref, total_ref, acc_ref):
    half = COARSE_ROWS // 2
    low_lanes = lax.broadcasted_iota(jnp.int32, (1, 128), 1) < 64
    row = lax.broadcasted_iota(jnp.int32, (256, 256), 0)
    col = lax.broadcasted_iota(jnp.int32, (256, 256), 1)
    for z in range(4):
        packed = turned_ref[z, COARSE_ROWS:, :].astype(f32)
        zero = jnp.zeros_like(packed)
        q_ref[z * 256 : z * 256 + half, :] = jnp.where(low_lanes, packed, zero).astype(bf16)
        q_ref[z * 256 + half : (z + 1) * 256, :] = jnp.where(
            low_lanes, pltpu.roll(packed, 64, 1), zero
        ).astype(bf16)
        kv = turned_ref[z, :COARSE_ROWS, :]
        at = pl.ds(z * 256, 256)
        scores = jnp.where(col <= row, dot_t(q_ref[at, :], kv), masked_low)
        top = jnp.max(scores, axis=1, keepdims=True)
        weights = jnp.exp2(scores - top)
        top_ref[at, :] = jnp.broadcast_to(top, (256, 128))
        total_ref[at, :] = jnp.broadcast_to(jnp.sum(weights, axis=1, keepdims=True), (256, 128))
        acc_ref[at, :] = dot(weights.astype(bf16), kv)
    for z in range(3):
        absorb(
            q_ref, top_ref, total_ref, acc_ref, (z + 1) * 256, (3 - z) * 256,
            [turned_ref[z, :COARSE_ROWS, :]],
        )


def absorb_chunks(chunk_ref, first_chunk, refs, state):
    for a in range(0, len(refs), 2):
        for z in range(3):
            absorb(*state, (z + 1) * 256, (3 - z) * 256, [r[z] for r in refs[a : a + 2]])
    for n, ref in enumerate(refs):

        @pl.when(chunk_ref[first_chunk + n] < chunk_ref[0])
        def _(ref=ref):
            for z in range(4):
                absorb(*state, z * 256, 256, [ref[z]])


def coarse_near_kernel(
    chunk_ref, n1, n2, n3, q_ref, top_in, total_in, acc_in, top_ref, total_ref, acc_ref
):
    top_ref[...] = top_in[...]
    total_ref[...] = total_in[...]
    acc_ref[...] = acc_in[...]
    absorb_chunks(chunk_ref, 1, [n1, n2, n3], (q_ref, top_ref, total_ref, acc_ref))


def coarse_far_kernel(
    chunk_ref, far_ref, q_ref, top_in, total_in, acc_in, out_ref, top_ref, total_ref, acc_ref
):
    top_ref[...] = top_in[...]
    total_ref[...] = total_in[...]
    acc_ref[...] = acc_in[...]
    refs = [far_ref.at[s] for s in range(4)]
    absorb_chunks(chunk_ref, 4, refs, (q_ref, top_ref, total_ref, acc_ref))
    mixed = acc_ref[...] / total_ref[...]
    low_lanes = lax.broadcasted_iota(jnp.int32, (1, 128), 1) < 64
    for z in range(4):
        upper = pltpu.roll(mixed[z * 256 : z * 256 + 128], 64, 1)
        lower = mixed[z * 256 + 128 : (z + 1) * 256]
        out_ref[z] = jnp.where(low_lanes, upper, lower).astype(bf16)


def feed_kernel(
    where_ref, heads_ref, own_ref, mine_ref, other_ref, short_ref, gain_ref, up_ref, down_ref,
    part_ref, first_ref, mixed_ref, all_ref,
):
    head, core = where_ref[1], where_ref[2]
    low_lanes = lax.broadcasted_iota(jnp.int32, (1, 128), 1) < 64
    for y in range(4):
        for pair in range(2):
            even = heads_ref[2 * pair * 4 + y].astype(f32)
            odd = heads_ref[(2 * pair + 1) * 4 + y].astype(f32)
            at = slice(y * 256 + pair * 128, y * 256 + (pair + 1) * 128)
            mixed_ref[0:128, at] = jnp.where(low_lanes, even, pltpu.roll(odd, 64, 1)).astype(bf16)
            mixed_ref[128:256, at] = jnp.where(low_lanes, pltpu.roll(even, 64, 1), odd).astype(bf16)
    first = short_ref[...].astype(f32)
    for half in range(2):
        first += dot(half_lanes(mixed_ref, head, half), own_ref[half * 128 : (half + 1) * 128, :])
    for s in range(1, 4):
        source = lax.rem(head - s + 4, 4)
        first += dot(half_lanes(mixed_ref, source, core), mine_ref[s - 1])
        first += dot(half_lanes(mixed_ref, source, 1 - core), other_ref[s - 1])
    all_ref[...] = first
    first_ref[...] = all_ref[pl.ds(pl.multiple_of(head * 64, 64), 64), :]
    feed = norm_rows(first, gain_ref[...])
    inner = jax.nn.gelu(dot(feed, up_ref[...])).astype(bf16)
    part_ref[...] = dot(inner, down_ref[...]).astype(bf16).reshape(4, 64, D)


def final_kernel(where_ref, s0, s1, s2, s3, b0, b1, b2, b3, up_ref, out_ref):
    head = where_ref[1]
    rows = 256 + HALO
    second = jnp.concatenate([ref[...] for ref in (s0, s1, s2, s3)], axis=0)
    lifted = dot(second, up_ref[...])
    index = lax.broadcasted_iota(jnp.int32, (256, rows), 0)
    column = lax.broadcasted_iota(jnp.int32, (256, rows), 1)
    r, m = index // 64, index % 64
    source = jnp.where(r == 0, 192 + m, jnp.where(m == 63, 268 + r, (r - 1) * 64 + m + 1))
    choose = (source == column).astype(f32).astype(bf16)
    index = lax.broadcasted_iota(jnp.int32, (256, 256), 0)
    column = lax.broadcasted_iota(jnp.int32, (256, 256), 1)
    weave = ((index % 4) * 64 + index // 4 == column).astype(f32).astype(bf16)
    for s, block in enumerate((b0, b1, b2, b3)):
        mine = lifted[s * 64 : (s + 1) * 64]
        raised = jnp.concatenate([mine[:, q * SHARE : (q + 1) * SHARE] for q in range(4)], axis=0)
        value = (dot(choose, block[...]) + raised).astype(bf16)
        begin = pl.multiple_of(lax.rem(head - s + 4, 4) * 256, 256)
        out_ref[pl.ds(begin, 256), :] = dot(weave, value).astype(bf16)


def gather_rest(weight, core):
    half = lax.dynamic_slice_in_dim(weight, core * 128, 128, 0)
    mine = jnp.stack([shift(half, "head", s, 4) for s in range(1, 4)])
    return mine, shift(mine, "core", 1, 2)


def local(
    token_ids, embedding, fine_norm, fine_query, fine_key, fine_value, fine_output,
    shorten_weight, coarse_norm, coarse_query, coarse_key, coarse_value, coarse_output,
    ffn_norm, ffn_up, ffn_down, upsample_weight,
):
    place = lax.axis_index(SEQ).astype(jnp.int32)
    head = lax.axis_index("head").astype(jnp.int32)
    x_place = lax.axis_index("x").astype(jnp.int32)
    core = lax.axis_index("core").astype(jnp.int32)
    tables = [jnp.asarray(t) for t in angle_tables()]
    where = jnp.stack([place, head, core])

    prior = later(token_ids, SEQ, 1, 32)
    before = later(token_ids[ROWS - BLOCK :], SEQ, 2, 32)
    share = jax.ShapeDtypeStruct((ROWS, SHARE), bf16)
    tab, q, k_own, v_own = call(
        fine_own_kernel, "fine_own",
        [jax.ShapeDtypeStruct((9, 256, SHARE), bf16), share, share, share], [],
        [token_ids[:, None], embedding, fine_norm[None], fine_query, fine_key, fine_value, *tables],
    )
    past_ids = jnp.concatenate([before, prior])
    past_ids, fine_output_held = lax.optimization_barrier((past_ids, fine_output))
    out_mine, out_other = gather_rest(fine_output_held, core)

    mixed = call(
        fine_kernel, "fine_attention", jax.ShapeDtypeStruct((HALO + ROWS, SHARE), bf16),
        [where], [past_ids[:, None], tab, q, k_own, v_own, *tables],
        [pltpu.VMEM((KEYS, SHARE), bf16), pltpu.VMEM((KEYS, SHARE), bf16)], grid=(4,),
    )

    rows = 256 + HALO
    got = exchange(lambda d: lax.dynamic_slice_in_dim(mixed, d * 256, rows, 0), "head", 4)
    own_ids = lax.dynamic_slice_in_dim(
        jnp.concatenate([past_ids[PAST - HALO :], token_ids]), head * 256, rows, 0
    )
    sends = call(
        fine_rows_kernel, "fine_rows", jax.ShapeDtypeStruct((4, rows, SHARE), bf16),
        [where], [own_ids[:, None], embedding, *got, fine_output, out_mine, out_other],
    )
    blocks = exchange(lambda d: lax.dynamic_index_in_dim(sends, d, 0, keepdims=False), "head", 4)

    terms = []
    for s, block in enumerate(blocks):
        part = call(
            short_part_kernel, "short_part", jax.ShapeDtypeStruct((64, D), bf16), [],
            [block, shorten_weight],
        )
        terms.append(part if s == 0 else shift(part, "head", 4 - s, 4))
    short_own = sum(t.astype(f32) for t in terms).astype(bf16)
    shorts = [short_own] + [shift(short_own, "head", s, 4) for s in range(1, 4)]
    packed, short = call(
        coarse_pack_kernel, "coarse_pack",
        [
            jax.ShapeDtypeStruct((4, COARSE_ROWS * 3 // 2, 128), bf16),
            jax.ShapeDtypeStruct((COARSE_ROWS, D), bf16),
        ],
        [where],
        [*shorts, coarse_norm[None], coarse_query, coarse_key, coarse_value, *tables],
    )

    turned = lax.all_to_all(packed, "z", 0, 0)
    turned, coarse_output_held = lax.optimization_barrier((turned, coarse_output))
    kv = turned[:, :COARSE_ROWS]
    near = [shift(kv, "x", s, 4) for s in range(1, 4)]
    far = shift(jnp.stack([kv, *near]), "core", 1, 2)
    co_mine, co_other = gather_rest(coarse_output_held, core)
    steps = jnp.arange(4, dtype=jnp.int32)
    columns_x = (x_place - steps + 4) % 4
    chunks = jnp.concatenate([2 * columns_x + core, 2 * columns_x + 1 - core])
    wide = jax.ShapeDtypeStruct((1024, 128), f32)
    state = call(
        coarse_first_kernel, "coarse_first",
        [jax.ShapeDtypeStruct((1024, 128), bf16), wide, wide, wide], [], [turned],
    )
    q_all, sums = state[0], state[1:]
    sums = call(coarse_near_kernel, "coarse_near", [wide] * 3, [chunks], [*near, q_all, *sums])
    attended = call(
        coarse_far_kernel, "coarse_far", jax.ShapeDtypeStruct((4, 128, 128), bf16),
        [chunks], [far, q_all, *sums], [pltpu.VMEM((1024, 128), f32)] * 3,
    )

    wide_sends = jnp.broadcast_to(attended[:, None], (4, 4, 128, 128)).reshape(16, 128, 128)
    heads_in = lax.all_to_all(wide_sends, ("z", "head"), 0, 0)
    parts, first_own = call(
        feed_kernel, "feed",
        [jax.ShapeDtypeStruct((4, 64, D), bf16), jax.ShapeDtypeStruct((64, D), f32)],
        [where],
        [heads_in, coarse_output, co_mine, co_other, short, ffn_norm[None], ffn_up, ffn_down],
        [pltpu.VMEM((COARSE_ROWS, D), bf16), pltpu.VMEM((COARSE_ROWS, D), f32)],
    )
    sums = exchange(lambda d: lax.dynamic_index_in_dim(parts, d, 0, keepdims=False), "head", 4)
    second_own = (first_own + sum(t.astype(f32) for t in sums)).astype(bf16)
    seconds = [second_own] + [shift(second_own, "head", s, 4) for s in range(1, 4)]
    return call(
        final_kernel, "final", jax.ShapeDtypeStruct((ROWS, SHARE), bf16),
        [where], [*seconds, *blocks, upsample_weight.reshape(D, SHORTEN * SHARE)],
    )


def solution(mesh):
    split = Mesh(mesh.devices.reshape(4, 4, 2, 4), ("z", "x", "core", "head"))
    return jax.shard_map(
        local,
        mesh=split,
        in_specs=(
            P(SEQ), P(), P(), P(None, "head"), P(None, "head"), P(None, "head"), P("head", None),
            P(None, "head", None), P(), P(None, "head"), P(None, "head"), P(None, "head"),
            P("head", None), P(), P(None, "head"), P("head", None), P(None, None, "head"),
        ),
        out_specs=P(SEQ, "head"),
        check_vma=False,
    )
```

```python
import functools
import math

import jax
import jax.numpy as jnp
import numpy as np
from jax import lax
from jax.experimental import pallas as pl
from jax.experimental.pallas import tpu as pltpu
from jax.sharding import Mesh
from jax.sharding import PartitionSpec as P

D = 1024
HEAD_DIM = 64
SHORTEN = 4
WINDOW = 1024
BLOCK = 256
HALO = 16
ROWS = 1024
PAST = WINDOW + BLOCK
KEYS = PAST + ROWS
SHARE = 256
COARSE_ROWS = 256
SEQ = ("z", "x", "core")

epsilon = 1e-06
masked_low = -1e30
q_scale = HEAD_DIM ** (-0.5) * math.log2(math.e)
bf16 = jnp.bfloat16
f32 = jnp.float32


def angle_tables():
    lane = np.arange(128) % 32
    period = 2.0 ** (4 + lane * 14 // 32)
    coarse = (256.0 * np.arange(32)[:, None]) % period[None]
    near = np.arange(256)[:, None] % period[None]
    a = coarse * (2.0 * np.pi / period)[None]
    b = near * (2.0 * np.pi / period)[None]
    return [t.astype(np.float32) for t in (np.cos(a), np.sin(a), np.cos(b), np.sin(b))]


def shift(value, axis, steps, count):
    return lax.ppermute(value, axis, [(i, (i + steps) % count) for i in range(count)])


def later(value, axis, steps, count):
    return lax.ppermute(value, axis, [(i, i + steps) for i in range(count - steps)])


def exchange(block_for, axis, count):
    me = lax.axis_index(axis)
    got = [block_for(me)]
    for s in range(1, count):
        got.append(shift(block_for((me + s) % count), axis, s, count))
    return got


def dot(left, right):
    return jnp.dot(left, right, preferred_element_type=f32)


def dot_t(left, right):
    return lax.dot_general(left, right, (((1,), (1,)), ((), ())), preferred_element_type=f32)


def norm_rows(data, gain):
    power = jnp.mean(data * data, axis=-1, keepdims=True)
    return (data * lax.rsqrt(power + epsilon) * gain).astype(bf16)


def partner(values):
    width = values.shape[1]
    lane = lax.broadcasted_iota(jnp.int32, values.shape, 1)
    ahead = pltpu.roll(values, width - 32, 1)
    behind = pltpu.roll(values, 32, 1)
    return jnp.where(lane % 64 < 32, -ahead, behind)


def halves(table):
    high = table.astype(bf16)
    low = (table - high.astype(f32)).astype(bf16)
    return high, low


def turn_tables(ca, sa, cb, sb):
    cosine = ca * cb - sa * sb
    sine = sa * cb + ca * sb
    return jnp.concatenate([cosine, cosine], axis=1), jnp.concatenate([sine, sine], axis=1)


def pick(ids, levels=256):
    columns = lax.broadcasted_iota(jnp.int32, (ids.shape[0], levels), 1)
    return (ids == columns).astype(f32).astype(bf16)


def turned_rows(hot, tab_ref, n, cosine, sine):
    plain = dot(hot, tab_ref[n]) + dot(hot, tab_ref[n + 1])
    other = dot(hot, tab_ref[n + 2]) + dot(hot, tab_ref[n + 3])
    return (plain * cosine + other * sine).astype(bf16)


def fine_own_kernel(
    ids_ref, emb_ref, gain_ref, ca_ref, sa_ref, cb_ref, sb_ref, wq_hbm, wk_hbm, wv_hbm,
    tab_ref, q_ref, k_ref, v_ref, w_ref, sems,
):
    copies = begin_copies(
        [(w, w_ref.at[n]) for n, w in enumerate((wq_hbm, wk_hbm, wv_hbm))], sems
    )
    wq_ref, wk_ref, wv_ref = (w_ref.at[n] for n in range(3))
    fine_in = norm_rows(emb_ref[...].astype(f32), gain_ref[...])
    finish_copies(copies)
    tq = dot(fine_in, wq_ref[...]) * q_scale
    tk = dot(fine_in, wk_ref[...])
    for n, table in enumerate((tq, partner(tq), tk, partner(tk))):
        high, low = halves(table)
        tab_ref[2 * n] = high
        tab_ref[2 * n + 1] = low
    tab_ref[8] = dot(fine_in, wv_ref[...]).astype(bf16)
    cb = cb_ref[...]
    sb = sb_ref[...]
    for block in range(ROWS // BLOCK):
        at = slice(block * BLOCK, (block + 1) * BLOCK)
        hot = pick(ids_ref[at, :])
        far = PAST // BLOCK + block
        cosine, sine = turn_tables(ca_ref[far : far + 1, :], sa_ref[far : far + 1, :], cb, sb)
        q_ref[at, :] = turned_rows(hot, tab_ref, 0, cosine, sine)
        k_ref[at, :] = turned_rows(hot, tab_ref, 4, cosine, sine)
        v_ref[at, :] = dot(hot, tab_ref[8]).astype(bf16)


def fine_kernel(
    place_ref, ids_ref, tab_ref, q_ref, k_own_ref, v_own_ref, ca_ref, sa_ref, cb_ref, sb_ref,
    out_ref, k_ref, v_ref,
):
    step = pl.program_id(0)
    lowest = jnp.maximum(PAST - place_ref[0] * ROWS, 0)
    head_lane = lax.broadcasted_iota(jnp.int32, (1, SHARE), 1) // HEAD_DIM

    @pl.when(step == 0)
    def _():
        cb = cb_ref[...]
        sb = sb_ref[...]
        k_ref[PAST:, :] = k_own_ref[...]
        v_ref[PAST:, :] = v_own_ref[...]
        for block in range(PAST // BLOCK):
            at = slice(block * BLOCK, (block + 1) * BLOCK)
            hot = pick(ids_ref[at, :])
            cosine, sine = turn_tables(
                ca_ref[block : block + 1, :], sa_ref[block : block + 1, :], cb, sb
            )
            k_ref[at, :] = turned_rows(hot, tab_ref, 4, cosine, sine)
            v_ref[at, :] = dot(hot, tab_ref[8]).astype(bf16)

        halo_q = turned_rows(
            pick(ids_ref[PAST - HALO : PAST, :]), tab_ref, 0, cosine[-HALO:], sine[-HALO:]
        )
        stacked = jnp.concatenate(
            [jnp.where(head_lane == h, halo_q, jnp.zeros_like(halo_q)) for h in range(4)], axis=0
        )
        scores = dot_t(stacked, k_ref[0:PAST, :])
        row = lax.broadcasted_iota(jnp.int32, scores.shape, 0) % HALO + (PAST - HALO)
        col = lax.broadcasted_iota(jnp.int32, scores.shape, 1)
        allowed = (col <= row) & (col > row - WINDOW) & (col >= lowest)
        scores = jnp.where(allowed, scores, masked_low)
        top = jnp.max(scores, axis=1, keepdims=True)
        weights = jnp.exp2(scores - top)
        total = jnp.sum(weights, axis=1, keepdims=True)
        mixed = dot(weights.astype(bf16), v_ref[0:PAST, :]) / total
        result = jnp.zeros((HALO, SHARE), f32)
        for h in range(4):
            result = jnp.where(head_lane == h, mixed[h * HALO : (h + 1) * HALO], result)
        out_ref[0:HALO, :] = result.astype(bf16)

    begin = pl.multiple_of((step + 1) * BLOCK, BLOCK)
    keys = k_ref[pl.ds(begin, PAST), :]
    values = v_ref[pl.ds(begin, PAST), :]
    query = q_ref[pl.ds(pl.multiple_of(step * BLOCK, BLOCK), BLOCK), :]
    row = lax.broadcasted_iota(jnp.int32, (BLOCK, BLOCK), 0)
    col = lax.broadcasted_iota(jnp.int32, (BLOCK, BLOCK), 1)
    biases = [
        jnp.where(begin + t * BLOCK >= lowest, 0.0, masked_low).astype(f32) for t in range(4)
    ]
    first_bias = jnp.where(col > row, 0.0, masked_low) + biases[0]
    last_bias = jnp.where(col <= row, 0.0, masked_low)
    ones = jnp.ones((PAST, 128), bf16)
    low_lanes = lax.broadcasted_iota(jnp.int32, (1, 128), 1) < 64
    results = []
    for h in range(4):
        scores = dot_t(jnp.where(head_lane == h, query, jnp.zeros_like(query)), keys)
        tiles = [scores[:, t * BLOCK : (t + 1) * BLOCK] for t in range(5)]
        tiles = (
            [tiles[0] + first_bias]
            + [tiles[t] + biases[t] for t in range(1, 4)]
            + [tiles[4] + last_bias]
        )
        peak = tiles[0]
        for t in range(1, 5):
            peak = jnp.maximum(peak, tiles[t])
        top = jnp.max(peak, axis=1, keepdims=True)
        weights = [jnp.exp2(tile - top).astype(bf16) for tile in tiles]
        pair = (h // 2) * 128
        wide = jnp.concatenate([values[:, pair : pair + 128], ones], axis=1)
        mixed = dot(jnp.concatenate(weights, axis=1), wide)
        results.append(mixed[:, :128] / mixed[:, 128:])
    result = jnp.concatenate(
        [jnp.where(low_lanes, results[2 * n], results[2 * n + 1]) for n in range(2)], axis=1
    )
    at = pl.multiple_of(HALO + step * BLOCK, HALO)
    out_ref[pl.ds(at, BLOCK), :] = result.astype(bf16)


def vmem():
    return pl.BlockSpec(memory_space=pltpu.VMEM)


def smem():
    return pl.BlockSpec(memory_space=pltpu.SMEM)


def call(kernel, name, shapes, scalars, arrays, scratch=(), grid=None, limit=48, us=2, hbm=()):
    one = not isinstance(shapes, (list, tuple))
    extra = {} if grid is None else {"grid": grid}
    return pl.pallas_call(
        kernel,
        out_shape=shapes,
        in_specs=[smem()] * len(scalars)
        + [vmem()] * len(arrays)
        + [pl.BlockSpec(memory_space=pl.ANY)] * len(hbm),
        out_specs=vmem() if one else [vmem()] * len(shapes),
        scratch_shapes=list(scratch),
        compiler_params=pltpu.CompilerParams(vmem_limit_bytes=limit << 20),
        cost_estimate=pl.CostEstimate(
            flops=us * 10**9, transcendentals=0, bytes_accessed=us * 2 * 10**6
        ),
        name=name,
        **extra,
    )(*scalars, *arrays, *hbm)


def begin_copies(pairs, sems):
    copies = [pltpu.make_async_copy(a, b, sems.at[n]) for n, (a, b) in enumerate(pairs)]
    for copy in copies:
        copy.start()
    return copies


def finish_copies(copies):
    for copy in copies:
        copy.wait()


def fine_rows_kernel(
    where_ref, ids_ref, emb_ref, g0, g1, g2, g3, own_hbm, mine_hbm, other_hbm, out_ref, w_ref, sems
):
    place, head, core = where_ref[0], where_ref[1], where_ref[2]
    copies = begin_copies(
        [(own_hbm, w_ref.at[0:256])]
        + [(mine_hbm.at[s - 1], w_ref.at[pl.ds(s * 256 + core * 128, 128)]) for s in range(1, 4)]
        + [
            (other_hbm.at[s - 1], w_ref.at[pl.ds(s * 256 + 128 - core * 128, 128)])
            for s in range(1, 4)
        ],
        sems,
    )
    merged = dot(pick(ids_ref[...]), emb_ref[...])
    finish_copies(copies)
    merged += dot(jnp.concatenate([g0[...], g1[...], g2[...], g3[...]], axis=1), w_ref[...])
    rows = 256 + HALO
    token = (
        place * ROWS + head * 256 - HALO + lax.broadcasted_iota(jnp.int32, (rows, D), 0)
    )
    fine = jnp.where(token >= 0, merged, 0.0).astype(bf16)
    index = lax.broadcasted_iota(jnp.int32, (256, rows), 0)
    column = lax.broadcasted_iota(jnp.int32, (256, rows), 1)
    source = 4 * (index % 64) + index // 64 + (HALO - 3)
    choose = (source == column).astype(f32).astype(bf16)
    grouped = dot(choose, fine).astype(bf16)
    for d in range(4):
        out_ref[d, 0:256, :] = grouped[:, d * SHARE : (d + 1) * SHARE]
        out_ref[d, 256:rows, :] = fine[256:rows, d * SHARE : (d + 1) * SHARE]


def short_part_kernel(group_ref, w_ref, out_ref):
    total = dot(group_ref[0:64, :], w_ref[0])
    for r in range(1, SHORTEN):
        total += dot(group_ref[r * 64 : (r + 1) * 64, :], w_ref[r])
    out_ref[...] = total.astype(bf16)


def coarse_pack_kernel(
    where_ref, s0, s1, s2, s3, gain_ref, wq_ref, wk_ref, wv_ref, ca_ref, sa_ref, cb_ref, sb_ref,
    out_ref, short_ref,
):
    place, head = where_ref[0], where_ref[1]
    for s, ref in enumerate((s0, s1, s2, s3)):
        begin = pl.multiple_of(lax.rem(head - s + 4, 4) * 64, 64)
        short_ref[pl.ds(begin, 64), :] = ref[...]
    x = norm_rows(short_ref[...].astype(f32), gain_ref[...])
    cosine, sine = turn_tables(
        ca_ref[pl.ds(place, 1), :], sa_ref[pl.ds(place, 1), :], cb_ref[...], sb_ref[...]
    )

    def turned(values):
        return values * cosine + partner(values) * sine

    q = turned(dot(x, wq_ref[...])) * q_scale
    k = turned(dot(x, wk_ref[...]))
    v = dot(x, wv_ref[...])
    low_lanes = lax.broadcasted_iota(jnp.int32, (1, 128), 1) < 64
    half = COARSE_ROWS // 2
    for h in range(4):
        pair = (h // 2) * 128
        kp = k[:, pair : pair + 128]
        vp = v[:, pair : pair + 128]
        qp = q[:, pair : pair + 128]
        if h % 2 == 0:
            kv = jnp.where(low_lanes, kp, pltpu.roll(vp, 64, 1))
            qq = jnp.where(low_lanes, qp[:half], pltpu.roll(qp[half:], 64, 1))
        else:
            kv = jnp.where(low_lanes, pltpu.roll(kp, 64, 1), vp)
            qq = jnp.where(low_lanes, pltpu.roll(qp[:half], 64, 1), qp[half:])
        out_ref[h, 0:COARSE_ROWS, :] = kv.astype(bf16)
        out_ref[h, COARSE_ROWS : COARSE_ROWS + half, :] = qq.astype(bf16)


def with_ones(kv):
    return jnp.concatenate([kv, jnp.ones((kv.shape[0], 128), bf16)], axis=1)


def absorb(q_ref, top_ref, total_ref, acc_ref, begin, rows, parts):
    at = pl.ds(begin, rows)
    query = q_ref[at, :]
    scores = [dot_t(query, kv) for kv in parts]
    peak = scores[0]
    for s in scores[1:]:
        peak = jnp.maximum(peak, s)
    old = top_ref[at, :]
    top = jnp.maximum(old, jnp.max(peak, axis=1, keepdims=True))
    factor = jnp.exp2(old - top)
    both = jnp.concatenate([top, top], axis=1)
    contrib = dot(jnp.exp2(scores[0] - both).astype(bf16), with_ones(parts[0]))
    for s, kv in zip(scores[1:], parts[1:]):
        contrib = contrib + dot(jnp.exp2(s - both).astype(bf16), with_ones(kv))
    top_ref[at, :] = top
    total_ref[at, :] = total_ref[at, :] * factor + contrib[:, 128:]
    acc_ref[at, :] = acc_ref[at, :] * factor + contrib[:, :128]


def coarse_first_kernel(flag_ref, turned_ref, far_ref, q_ref, top_ref, total_ref, acc_ref):
    half = COARSE_ROWS // 2
    low_lanes = lax.broadcasted_iota(jnp.int32, (1, 128), 1) < 64
    row = lax.broadcasted_iota(jnp.int32, (256, 256), 0)
    col = lax.broadcasted_iota(jnp.int32, (256, 256), 1)
    for z in range(4):
        packed = turned_ref[z, COARSE_ROWS:, :].astype(f32)
        zero = jnp.zeros_like(packed)
        q_ref[z * 256 : z * 256 + half, :] = jnp.where(low_lanes, packed, zero).astype(bf16)
        q_ref[z * 256 + half : (z + 1) * 256, :] = jnp.where(
            low_lanes, pltpu.roll(packed, 64, 1), zero
        ).astype(bf16)
        kv = turned_ref[z, :COARSE_ROWS, :]
        at = pl.ds(z * 256, 256)
        scores = jnp.where(col <= row, dot_t(q_ref[at, :], kv), masked_low)
        top = jnp.max(scores, axis=1, keepdims=True)
        contrib = dot(jnp.exp2(scores - top).astype(bf16), with_ones(kv))
        top_ref[at, :] = jnp.broadcast_to(top, (256, 128))
        total_ref[at, :] = contrib[:, 128:]
        acc_ref[at, :] = contrib[:, :128]
    state = (q_ref, top_ref, total_ref, acc_ref)
    for z in range(3):
        absorb(
            *state, (z + 1) * 256, (3 - z) * 256, [turned_ref[z, :COARSE_ROWS, :], far_ref[z]]
        )

    @pl.when(flag_ref[0] > 0)
    def _():
        for z in range(4):
            absorb(*state, z * 256, 256, [far_ref[z]])


def coarse_more_kernel(which, last, flag_ref, *refs):
    count = 2 * len(which)
    chunks = refs[:count]
    q_ref, top_in, total_in, acc_in = refs[count : count + 4]
    out_ref = refs[count + 4] if last else None
    top_ref, total_ref, acc_ref = refs[-3:]
    top_ref[...] = top_in[...]
    total_ref[...] = total_in[...]
    acc_ref[...] = acc_in[...]
    state = (q_ref, top_ref, total_ref, acc_ref)
    for n, s in enumerate(which):
        near, far = chunks[2 * n], chunks[2 * n + 1]
        for z in range(3):
            absorb(*state, (z + 1) * 256, (3 - z) * 256, [near[z], far[z]])

        @pl.when(flag_ref[s] > 0)
        def _(near=near, far=far):
            for z in range(4):
                absorb(*state, z * 256, 256, [near[z], far[z]])

    if last:
        mixed = acc_ref[...] / total_ref[...]
        low_lanes = lax.broadcasted_iota(jnp.int32, (1, 128), 1) < 64
        for z in range(4):
            upper = pltpu.roll(mixed[z * 256 : z * 256 + 128], 64, 1)
            lower = mixed[z * 256 + 128 : (z + 1) * 256]
            block = jnp.where(low_lanes, upper, lower).astype(bf16)
            for y in range(4):
                out_ref[z * 4 + y] = block


def feed_kernel(
    where_ref, heads_ref, short_ref, gain_ref, own_hbm, mine_hbm, other_hbm, up_hbm, down_hbm,
    part_ref, first_ref, mixed_ref, all_ref, co_ref, up_ref, down_ref, sems,
):
    head, core = where_ref[1], where_ref[2]
    pairs = [(own_hbm, co_ref.at[pl.ds(head * 256, 256)])]
    for s in range(1, 4):
        source = lax.rem(head - s + 4, 4) * 256
        pairs.append((mine_hbm.at[s - 1], co_ref.at[pl.ds(source + core * 128, 128)]))
        pairs.append((other_hbm.at[s - 1], co_ref.at[pl.ds(source + 128 - core * 128, 128)]))
    copies = begin_copies(pairs + [(up_hbm, up_ref), (down_hbm, down_ref)], sems)
    low_lanes = lax.broadcasted_iota(jnp.int32, (1, 128), 1) < 64
    for y in range(4):
        for pair in range(2):
            even = heads_ref[2 * pair * 4 + y].astype(f32)
            odd = heads_ref[(2 * pair + 1) * 4 + y].astype(f32)
            at = slice(y * 256 + pair * 128, y * 256 + (pair + 1) * 128)
            mixed_ref[0:128, at] = jnp.where(low_lanes, even, pltpu.roll(odd, 64, 1)).astype(bf16)
            mixed_ref[128:256, at] = jnp.where(low_lanes, pltpu.roll(even, 64, 1), odd).astype(bf16)
    finish_copies(copies[:7])
    first = short_ref[...].astype(f32) + dot(mixed_ref[...], co_ref[...])
    all_ref[...] = first
    first_ref[...] = all_ref[pl.ds(pl.multiple_of(head * 64, 64), 64), :]
    feed = norm_rows(first, gain_ref[...])
    finish_copies(copies[7:])
    inner = jax.nn.gelu(dot(feed, up_ref[...])).astype(bf16)
    part_ref[...] = dot(inner, down_ref[...]).astype(bf16).reshape(4, 64, D)


def final_kernel(where_ref, s0, s1, s2, s3, b0, b1, b2, b3, up_ref, out_ref):
    head = where_ref[1]
    rows = 256 + HALO
    second = jnp.concatenate([ref[...] for ref in (s0, s1, s2, s3)], axis=0)
    lifted = dot(second, up_ref[...])
    index = lax.broadcasted_iota(jnp.int32, (256, rows), 0)
    column = lax.broadcasted_iota(jnp.int32, (256, rows), 1)
    r, m = index // 64, index % 64
    source = jnp.where(r == 0, 192 + m, jnp.where(m == 63, 268 + r, (r - 1) * 64 + m + 1))
    choose = (source == column).astype(f32).astype(bf16)
    index = lax.broadcasted_iota(jnp.int32, (256, 256), 0)
    column = lax.broadcasted_iota(jnp.int32, (256, 256), 1)
    weave = ((index % 4) * 64 + index // 4 == column).astype(f32).astype(bf16)
    for s, block in enumerate((b0, b1, b2, b3)):
        mine = lifted[s * 64 : (s + 1) * 64]
        raised = jnp.concatenate([mine[:, q * SHARE : (q + 1) * SHARE] for q in range(4)], axis=0)
        value = (dot(choose, block[...]) + raised).astype(bf16)
        begin = pl.multiple_of(lax.rem(head - s + 4, 4) * 256, 256)
        out_ref[pl.ds(begin, 256), :] = dot(weave, value).astype(bf16)


def fetch_rest(weight, core):
    half = lax.dynamic_slice_in_dim(weight, core * 128, 128, 0)
    return [shift(half, "head", s, 4) for s in range(1, 4)]


def after(value, gate):
    return lax.optimization_barrier((value, gate))


def local(
    token_ids, embedding, fine_norm, fine_query, fine_key, fine_value, fine_output,
    shorten_weight, coarse_norm, coarse_query, coarse_key, coarse_value, coarse_output,
    ffn_norm, ffn_up, ffn_down, upsample_weight,
):
    place = lax.axis_index(SEQ).astype(jnp.int32)
    head = lax.axis_index("head").astype(jnp.int32)
    x_place = lax.axis_index("x").astype(jnp.int32)
    core = lax.axis_index("core").astype(jnp.int32)
    tables = [jnp.asarray(t) for t in angle_tables()]
    where = jnp.stack([place, head, core])

    prior = later(token_ids, SEQ, 1, 32)
    before = later(token_ids[ROWS - BLOCK :], SEQ, 2, 32)
    share = jax.ShapeDtypeStruct((ROWS, SHARE), bf16)
    tab, q, k_own, v_own = call(
        fine_own_kernel, "fine_own",
        [jax.ShapeDtypeStruct((9, 256, SHARE), bf16), share, share, share], [],
        [token_ids[:, None], embedding, fine_norm[None], *tables],
        [pltpu.VMEM((3, D, SHARE), bf16), pltpu.SemaphoreType.DMA((3,))],
        hbm=[fine_query, fine_key, fine_value], us=5,
    )
    past_ids = jnp.concatenate([before, prior])
    fine_output_held, tab = after(fine_output, tab)
    out_rest = fetch_rest(fine_output_held, core)

    mixed = call(
        fine_kernel, "fine_attention", jax.ShapeDtypeStruct((HALO + ROWS, SHARE), bf16),
        [where], [past_ids[:, None], tab, q, k_own, v_own, *tables],
        [pltpu.VMEM((KEYS, SHARE), bf16), pltpu.VMEM((KEYS, SHARE), bf16)], grid=(4,), us=12,
    )
    out_rest, mixed = after(out_rest, mixed)
    out_mine = jnp.stack(out_rest)
    out_other = shift(out_mine, "core", 1, 2)

    rows = 256 + HALO
    got = exchange(lambda d: lax.dynamic_slice_in_dim(mixed, d * 256, rows, 0), "head", 4)
    own_ids = lax.dynamic_slice_in_dim(
        jnp.concatenate([past_ids[PAST - HALO :], token_ids]), head * 256, rows, 0
    )
    sends = call(
        fine_rows_kernel, "fine_rows", jax.ShapeDtypeStruct((4, rows, SHARE), bf16),
        [where], [own_ids[:, None], embedding, *got],
        [pltpu.VMEM((D, D), bf16), pltpu.SemaphoreType.DMA((7,))],
        hbm=[fine_output, out_mine, out_other],
    )
    blocks = exchange(lambda d: lax.dynamic_index_in_dim(sends, d, 0, keepdims=False), "head", 4)

    terms = []
    for s, block in enumerate(blocks):
        part = call(
            short_part_kernel, "short_part", jax.ShapeDtypeStruct((64, D), bf16), [],
            [block, shorten_weight],
        )
        terms.append(part if s == 0 else shift(part, "head", 4 - s, 4))
    short_own = sum(t.astype(f32) for t in terms).astype(bf16)
    shorts = [short_own] + [shift(short_own, "head", s, 4) for s in range(1, 4)]
    packed, short = call(
        coarse_pack_kernel, "coarse_pack",
        [
            jax.ShapeDtypeStruct((4, COARSE_ROWS * 3 // 2, 128), bf16),
            jax.ShapeDtypeStruct((COARSE_ROWS, D), bf16),
        ],
        [where],
        [*shorts, coarse_norm[None], coarse_query, coarse_key, coarse_value, *tables],
    )

    turned = lax.all_to_all(packed, "z", 0, 0)
    coarse_output_held, turned = after(coarse_output, turned)
    kv = turned[:, :COARSE_ROWS]
    far = [shift(kv, "core", 1, 2)]
    near = [shift(kv, "x", s, 4) for s in range(1, 4)]
    far += [shift(part, "core", 1, 2) for part in near]
    steps = jnp.arange(4, dtype=jnp.int32)
    flags = ((x_place - steps + 4) % 4 < x_place).astype(jnp.int32) + (steps == 0) * core
    wide = jax.ShapeDtypeStruct((1024, 128), f32)
    q_all, *sums = call(
        coarse_first_kernel, "coarse_first",
        [jax.ShapeDtypeStruct((1024, 128), bf16), wide, wide, wide], [flags], [turned, far[0]],
        us=3,
    )
    co_rest = fetch_rest(coarse_output_held, core)
    sums = call(
        functools.partial(coarse_more_kernel, (1, 3), False), "coarse_more", [wide] * 3,
        [flags], [near[0], far[1], near[2], far[3], q_all, *sums], us=6,
    )
    wide_sends = call(
        functools.partial(coarse_more_kernel, (2,), True), "coarse_last",
        jax.ShapeDtypeStruct((16, 128, 128), bf16),
        [flags], [near[1], far[2], q_all, *sums], [pltpu.VMEM((1024, 128), f32)] * 3, us=3,
    )
    co_rest, wide_sends = after(co_rest, wide_sends)
    co_mine = jnp.stack(co_rest)
    co_other = shift(co_mine, "core", 1, 2)

    heads_in = lax.all_to_all(wide_sends, ("z", "head"), 0, 0)
    square = pltpu.VMEM((D, D), bf16)
    parts, first_own = call(
        feed_kernel, "feed",
        [jax.ShapeDtypeStruct((4, 64, D), bf16), jax.ShapeDtypeStruct((64, D), f32)],
        [where],
        [heads_in, short, ffn_norm[None]],
        [
            pltpu.VMEM((COARSE_ROWS, D), bf16), pltpu.VMEM((COARSE_ROWS, D), f32),
            square, square, square, pltpu.SemaphoreType.DMA((9,)),
        ],
        hbm=[coarse_output, co_mine, co_other, ffn_up, ffn_down], us=4,
    )
    sums = exchange(lambda d: lax.dynamic_index_in_dim(parts, d, 0, keepdims=False), "head", 4)
    second_own = (first_own + sum(t.astype(f32) for t in sums)).astype(bf16)
    seconds = [second_own] + [shift(second_own, "head", s, 4) for s in range(1, 4)]
    return call(
        final_kernel, "final", jax.ShapeDtypeStruct((ROWS, SHARE), bf16),
        [where], [*seconds, *blocks, upsample_weight.reshape(D, SHORTEN * SHARE)],
    )


def solution(mesh):
    split = Mesh(mesh.devices.reshape(4, 4, 2, 4), ("z", "x", "core", "head"))
    return jax.shard_map(
        local,
        mesh=split,
        in_specs=(
            P(SEQ), P(), P(), P(None, "head"), P(None, "head"), P(None, "head"), P("head", None),
            P(None, "head", None), P(), P(None, "head"), P(None, "head"), P(None, "head"),
            P("head", None), P(), P(None, "head"), P("head", None), P(None, None, "head"),
        ),
        out_specs=P(SEQ, "head"),
        check_vma=False,
    )
```

```python
import functools
import math

import jax
import jax.numpy as jnp
import numpy as np
from jax import lax
from jax.experimental import pallas as pl
from jax.experimental.pallas import tpu as pltpu
from jax.sharding import Mesh
from jax.sharding import PartitionSpec as P

D = 1024
HEAD_DIM = 64
SHORTEN = 4
WINDOW = 1024
BLOCK = 256
HALO = 16
ROWS = 1024
PAST = WINDOW + BLOCK
KEYS = PAST + ROWS
SHARE = 256
COARSE_ROWS = 256
SEQ = ("z", "x", "core")

epsilon = 1e-06
masked_low = -1e30
q_scale = HEAD_DIM ** (-0.5) * math.log2(math.e)
bf16 = jnp.bfloat16
f32 = jnp.float32


def angle_tables():
    lane = np.arange(128) % 32
    period = 2.0 ** (4 + lane * 14 // 32)
    coarse = (256.0 * np.arange(32)[:, None]) % period[None]
    near = np.arange(256)[:, None] % period[None]
    a = coarse * (2.0 * np.pi / period)[None]
    b = near * (2.0 * np.pi / period)[None]
    parts = [np.cos(a), np.sin(a), np.cos(b), np.sin(b)]
    return np.concatenate(parts, axis=0).astype(np.float32)


def shift(value, axis, steps, count):
    return lax.ppermute(value, axis, [(i, (i + steps) % count) for i in range(count)])


def later(value, axis, steps, count):
    return lax.ppermute(value, axis, [(i, i + steps) for i in range(count - steps)])


def exchange(block_for, axis, count):
    me = lax.axis_index(axis)
    got = [block_for(me)]
    for s in range(1, count):
        got.append(shift(block_for((me + s) % count), axis, s, count))
    return got


def dot(left, right):
    return jnp.dot(left, right, preferred_element_type=f32)


def dot_t(left, right):
    return lax.dot_general(left, right, (((1,), (1,)), ((), ())), preferred_element_type=f32)


def norm_rows(data, gain):
    power = jnp.mean(data * data, axis=-1, keepdims=True)
    return (data * lax.rsqrt(power + epsilon) * gain).astype(bf16)


def partner(values):
    width = values.shape[1]
    lane = lax.broadcasted_iota(jnp.int32, values.shape, 1)
    ahead = pltpu.roll(values, width - 32, 1)
    behind = pltpu.roll(values, 32, 1)
    return jnp.where(lane % 64 < 32, -ahead, behind)


def halves(table):
    high = table.astype(bf16)
    low = (table - high.astype(f32)).astype(bf16)
    return high, low


def turn_tables(turn_ref, far):
    ca = turn_ref[pl.ds(far, 1), :]
    sa = turn_ref[pl.ds(32 + far, 1), :]
    cb = turn_ref[64:320, :]
    sb = turn_ref[320:576, :]
    cosine = ca * cb - sa * sb
    sine = sa * cb + ca * sb
    return jnp.concatenate([cosine, cosine], axis=1), jnp.concatenate([sine, sine], axis=1)


def pick(ids, levels=256):
    columns = lax.broadcasted_iota(jnp.int32, (ids.shape[0], levels), 1)
    return (ids == columns).astype(f32).astype(bf16)


def turned_rows(hot, tab_ref, n, cosine, sine):
    plain = dot(hot, tab_ref[n]) + dot(hot, tab_ref[n + 1])
    other = dot(hot, tab_ref[n + 2]) + dot(hot, tab_ref[n + 3])
    return (plain * cosine + other * sine).astype(bf16)


def fine_kernel(
    where_ref, ids_ref, gain_ref, turn_hbm, emb_hbm, wq_hbm, wk_hbm, wv_hbm,
    o0, o1, o2, o3, tab_ref, q_ref, k_ref, v_ref, turn_ref, emb_ref, w_ref, sems,
):
    step = pl.program_id(0)
    head = where_ref[1]
    quarter = lax.rem(head + step, 4)
    outs = (o0, o1, o2, o3)
    lowest = jnp.maximum(PAST - where_ref[0] * ROWS, 0)
    head_lane = lax.broadcasted_iota(jnp.int32, (1, SHARE), 1) // HEAD_DIM

    @pl.when(step == 0)
    def _():
        pairs = [(emb_hbm, emb_ref), (turn_hbm, turn_ref)]
        for n, w in enumerate((wq_hbm, wk_hbm, wv_hbm)):
            for part in range(2):
                rows = pl.ds(part * 512, 512)
                pairs.append((w.at[rows], w_ref.at[n, rows]))
        copies = begin_copies(pairs, sems)
        finish_copies(copies[:1])
        fine_in = norm_rows(emb_ref[...].astype(f32), gain_ref[...])
        finish_copies(copies[1:])
        tq = dot(fine_in, w_ref[0]) * q_scale
        tk = dot(fine_in, w_ref[1])
        for n, table in enumerate((tq, partner(tq), tk, partner(tk))):
            high, low = halves(table)
            tab_ref[2 * n] = high
            tab_ref[2 * n + 1] = low
        tab_ref[8] = dot(fine_in, w_ref[2]).astype(bf16)

        def build(block, with_q):
            begin = pl.multiple_of(block * BLOCK, BLOCK)
            hot = pick(ids_ref[pl.ds(begin, BLOCK), :])
            cosine, sine = turn_tables(turn_ref, block)
            k_ref[pl.ds(begin, BLOCK), :] = turned_rows(hot, tab_ref, 4, cosine, sine)
            v_ref[pl.ds(begin, BLOCK), :] = dot(hot, tab_ref[8]).astype(bf16)
            if with_q:
                at = pl.multiple_of(begin - (PAST - BLOCK), BLOCK)
                q_ref[pl.ds(at, BLOCK), :] = turned_rows(hot, tab_ref, 0, cosine, sine)
            return 0

        early = PAST // BLOCK - 1
        lax.fori_loop(0, early, lambda block, _: build(block, False), 0)
        lax.fori_loop(early, KEYS // BLOCK, lambda block, _: build(block, True), 0)
        halo_q = q_ref[BLOCK - HALO : BLOCK, :]
        stacked = jnp.concatenate(
            [jnp.where(head_lane == h, halo_q, jnp.zeros_like(halo_q)) for h in range(4)], axis=0
        )
        scores = dot_t(stacked, k_ref[0:PAST, :])
        row = lax.broadcasted_iota(jnp.int32, scores.shape, 0) % HALO + (PAST - HALO)
        col = lax.broadcasted_iota(jnp.int32, scores.shape, 1)
        allowed = (col <= row) & (col > row - WINDOW) & (col >= lowest)
        scores = jnp.where(allowed, scores, masked_low)
        top = jnp.max(scores, axis=1, keepdims=True)
        weights = jnp.exp2(scores - top)
        total = jnp.sum(weights, axis=1, keepdims=True)
        mixed = dot(weights.astype(bf16), v_ref[0:PAST, :]) / total
        result = jnp.zeros((HALO, SHARE), f32)
        for h in range(4):
            result = jnp.where(head_lane == h, mixed[h * HALO : (h + 1) * HALO], result)
        for s, out_ref in enumerate(outs):

            @pl.when(lax.rem(head + s, 4) == 0)
            def _(out_ref=out_ref):
                out_ref[0:HALO, :] = result.astype(bf16)

    begin = pl.multiple_of((quarter + 1) * BLOCK, BLOCK)
    keys = k_ref[pl.ds(begin, PAST), :]
    values = v_ref[pl.ds(begin, PAST), :]
    query = q_ref[pl.ds(begin, BLOCK), :]
    row = lax.broadcasted_iota(jnp.int32, (BLOCK, BLOCK), 0)
    col = lax.broadcasted_iota(jnp.int32, (BLOCK, BLOCK), 1)
    biases = [
        jnp.where(begin + t * BLOCK >= lowest, 0.0, masked_low).astype(f32) for t in range(4)
    ]
    first_bias = jnp.where(col > row, 0.0, masked_low) + biases[0]
    last_bias = jnp.where(col <= row, 0.0, masked_low)
    ones = jnp.ones((PAST, 128), bf16)
    low_lanes = lax.broadcasted_iota(jnp.int32, (1, 128), 1) < 64
    results = []
    for h in range(4):
        scores = dot_t(jnp.where(head_lane == h, query, jnp.zeros_like(query)), keys)
        tiles = [scores[:, t * BLOCK : (t + 1) * BLOCK] for t in range(5)]
        tiles = (
            [tiles[0] + first_bias]
            + [tiles[t] + biases[t] for t in range(1, 4)]
            + [tiles[4] + last_bias]
        )
        peak = tiles[0]
        for t in range(1, 5):
            peak = jnp.maximum(peak, tiles[t])
        top = jnp.max(peak, axis=1, keepdims=True)
        weights = [jnp.exp2(tile - top).astype(bf16) for tile in tiles]
        pair = (h // 2) * 128
        wide = jnp.concatenate([values[:, pair : pair + 128], ones], axis=1)
        mixed = dot(jnp.concatenate(weights, axis=1), wide)
        results.append(mixed[:, :128] / mixed[:, 128:])
    result = jnp.concatenate(
        [jnp.where(low_lanes, results[2 * n], results[2 * n + 1]) for n in range(2)], axis=1
    )
    result = result.astype(bf16)
    for s in range(4):

        @pl.when(step == s)
        def _(s=s):
            outs[s][HALO:, :] = result

            @pl.when(quarter < 3)
            def _():
                outs[(s + 1) % 4][0:HALO, :] = result[BLOCK - HALO :]


def vmem():
    return pl.BlockSpec(memory_space=pltpu.VMEM)


def smem():
    return pl.BlockSpec(memory_space=pltpu.SMEM)


def call(kernel, name, shapes, scalars, arrays, scratch=(), grid=None, limit=16, us=2, hbm=(), free=()):
    one = not isinstance(shapes, (list, tuple))
    extra = {} if grid is None else {"grid": grid}
    return pl.pallas_call(
        kernel,
        out_shape=shapes,
        in_specs=[smem()] * len(scalars)
        + [vmem()] * len(arrays)
        + [pl.BlockSpec(memory_space=pltpu.HBM)] * len(hbm)
        + [pl.BlockSpec(memory_space=pl.ANY)] * len(free),
        out_specs=vmem() if one else [vmem()] * len(shapes),
        scratch_shapes=list(scratch),
        compiler_params=pltpu.CompilerParams(vmem_limit_bytes=limit << 20),
        cost_estimate=pl.CostEstimate(
            flops=us * 10**9, transcendentals=0, bytes_accessed=us * 2 * 10**6
        ),
        name=name,
        **extra,
    )(*scalars, *arrays, *(pltpu.with_memory_space_constraint(a, pltpu.HBM) for a in hbm), *free)


def begin_copies(pairs, sems):
    copies = [pltpu.make_async_copy(a, b, sems.at[n]) for n, (a, b) in enumerate(pairs)]
    for copy in copies:
        copy.start()
    return copies


def finish_copies(copies):
    for copy in copies:
        copy.wait()


def fine_rows_kernel(
    where_ref, ids_ref, emb_ref, g0, g1, g2, g3, f0, f1, f2, f3, out_ref, w_ref, sems
):
    place, head = where_ref[0], where_ref[1]
    pairs = []
    for s, f in enumerate((f0, f1, f2, f3)):
        for part in range(2):
            at = pl.ds(part * 128, 128)
            pairs.append((f.at[at], w_ref.at[pl.ds(s * 256 + part * 128, 128)]))
    copies = begin_copies(pairs, sems)
    merged = dot(pick(ids_ref[...]), emb_ref[...])
    finish_copies(copies)
    merged += dot(jnp.concatenate([g0[...], g1[...], g2[...], g3[...]], axis=1), w_ref[...])
    rows = 256 + HALO
    token = (
        place * ROWS + head * 256 - HALO + lax.broadcasted_iota(jnp.int32, (rows, D), 0)
    )
    fine = jnp.where(token >= 0, merged, 0.0).astype(bf16)
    index = lax.broadcasted_iota(jnp.int32, (256, rows), 0)
    column = lax.broadcasted_iota(jnp.int32, (256, rows), 1)
    source = 4 * (index % 64) + index // 64 + (HALO - 3)
    choose = (source == column).astype(f32).astype(bf16)
    grouped = dot(choose, fine).astype(bf16)
    for d in range(4):
        out_ref[d, 0:256, :] = grouped[:, d * SHARE : (d + 1) * SHARE]
        out_ref[d, 256:rows, :] = fine[256:rows, d * SHARE : (d + 1) * SHARE]


def short_part_kernel(group_ref, w_ref, out_ref):
    total = dot(group_ref[0:64, :], w_ref[0])
    for r in range(1, SHORTEN):
        total += dot(group_ref[r * 64 : (r + 1) * 64, :], w_ref[r])
    out_ref[...] = total.astype(bf16)


def coarse_pack_kernel(
    where_ref, s0, s1, s2, s3, gain_ref, wq_ref, wk_ref, wv_ref, turn_ref,
    out_ref, short_ref,
):
    place, head = where_ref[0], where_ref[1]
    for s, ref in enumerate((s0, s1, s2, s3)):
        begin = pl.multiple_of(lax.rem(head - s + 4, 4) * 64, 64)
        short_ref[pl.ds(begin, 64), :] = ref[...]
    x = norm_rows(short_ref[...].astype(f32), gain_ref[...])
    cosine, sine = turn_tables(turn_ref, place)

    def turned(values):
        return values * cosine + partner(values) * sine

    q = turned(dot(x, wq_ref[...])) * q_scale
    k = turned(dot(x, wk_ref[...]))
    v = dot(x, wv_ref[...])
    low_lanes = lax.broadcasted_iota(jnp.int32, (1, 128), 1) < 64
    half = COARSE_ROWS // 2
    for h in range(4):
        pair = (h // 2) * 128
        kp = k[:, pair : pair + 128]
        vp = v[:, pair : pair + 128]
        qp = q[:, pair : pair + 128]
        if h % 2 == 0:
            kv = jnp.where(low_lanes, kp, pltpu.roll(vp, 64, 1))
            qq = jnp.where(low_lanes, qp[:half], pltpu.roll(qp[half:], 64, 1))
        else:
            kv = jnp.where(low_lanes, pltpu.roll(kp, 64, 1), vp)
            qq = jnp.where(low_lanes, pltpu.roll(qp[:half], 64, 1), qp[half:])
        out_ref[h, 0:COARSE_ROWS, :] = kv.astype(bf16)
        out_ref[h, COARSE_ROWS : COARSE_ROWS + half, :] = qq.astype(bf16)


def with_ones(kv):
    return jnp.concatenate([kv, jnp.ones((kv.shape[0], 128), bf16)], axis=1)


def absorb(q_ref, top_ref, total_ref, acc_ref, begin, rows, parts):
    at = pl.ds(begin, rows)
    query = q_ref[at, :]
    scores = [dot_t(query, kv) for kv in parts]
    peak = scores[0]
    for s in scores[1:]:
        peak = jnp.maximum(peak, s)
    old = top_ref[at, :]
    top = jnp.maximum(old, jnp.max(peak, axis=1, keepdims=True))
    factor = jnp.exp2(old - top)
    both = jnp.concatenate([top, top], axis=1)
    contrib = dot(jnp.exp2(scores[0] - both).astype(bf16), with_ones(parts[0]))
    for s, kv in zip(scores[1:], parts[1:]):
        contrib = contrib + dot(jnp.exp2(s - both).astype(bf16), with_ones(kv))
    top_ref[at, :] = top
    total_ref[at, :] = total_ref[at, :] * factor + contrib[:, 128:]
    acc_ref[at, :] = acc_ref[at, :] * factor + contrib[:, :128]


def coarse_first_kernel(flag_ref, turned_ref, far_ref, q_ref, top_ref, total_ref, acc_ref):
    half = COARSE_ROWS // 2
    low_lanes = lax.broadcasted_iota(jnp.int32, (1, 128), 1) < 64
    row = lax.broadcasted_iota(jnp.int32, (256, 256), 0)
    col = lax.broadcasted_iota(jnp.int32, (256, 256), 1)
    for z in range(4):
        packed = turned_ref[z, COARSE_ROWS:, :].astype(f32)
        zero = jnp.zeros_like(packed)
        q_ref[z * 256 : z * 256 + half, :] = jnp.where(low_lanes, packed, zero).astype(bf16)
        q_ref[z * 256 + half : (z + 1) * 256, :] = jnp.where(
            low_lanes, pltpu.roll(packed, 64, 1), zero
        ).astype(bf16)
        kv = turned_ref[z, :COARSE_ROWS, :]
        at = pl.ds(z * 256, 256)
        scores = jnp.where(col <= row, dot_t(q_ref[at, :], kv), masked_low)
        top = jnp.max(scores, axis=1, keepdims=True)
        contrib = dot(jnp.exp2(scores - top).astype(bf16), with_ones(kv))
        top_ref[at, :] = jnp.broadcast_to(top, (256, 128))
        total_ref[at, :] = contrib[:, 128:]
        acc_ref[at, :] = contrib[:, :128]
    state = (q_ref, top_ref, total_ref, acc_ref)
    for z in range(3):
        absorb(
            *state, (z + 1) * 256, (3 - z) * 256, [turned_ref[z, :COARSE_ROWS, :], far_ref[z]]
        )

    @pl.when(flag_ref[0] > 0)
    def _():
        for z in range(4):
            absorb(*state, z * 256, 256, [far_ref[z]])


def coarse_more_kernel(which, last, flag_ref, *refs):
    count = 2 * len(which)
    chunks = refs[:count]
    q_ref, top_in, total_in, acc_in = refs[count : count + 4]
    out_ref = refs[count + 4] if last else None
    top_ref, total_ref, acc_ref = refs[-3:]
    top_ref[...] = top_in[...]
    total_ref[...] = total_in[...]
    acc_ref[...] = acc_in[...]
    state = (q_ref, top_ref, total_ref, acc_ref)
    for n, s in enumerate(which):
        near, far = chunks[2 * n], chunks[2 * n + 1]
        for z in range(3):
            absorb(*state, (z + 1) * 256, (3 - z) * 256, [near[z], far[z]])

        @pl.when(flag_ref[s] > 0)
        def _(near=near, far=far):
            for z in range(4):
                absorb(*state, z * 256, 256, [near[z], far[z]])

    if last:
        mixed = acc_ref[...] / total_ref[...]
        low_lanes = lax.broadcasted_iota(jnp.int32, (1, 128), 1) < 64
        for z in range(4):
            upper = pltpu.roll(mixed[z * 256 : z * 256 + 128], 64, 1)
            lower = mixed[z * 256 + 128 : (z + 1) * 256]
            block = jnp.where(low_lanes, upper, lower).astype(bf16)
            for y in range(4):
                out_ref[z * 4 + y] = block


def feed_kernel(
    where_ref, heads_ref, short_ref, gain_ref, c0, up_hbm, down_hbm, c1, c2, c3,
    part_ref, first_ref, mixed_ref, all_ref, co_ref, up_ref, down_ref, sems,
):
    head = where_ref[1]
    pairs = []
    for s, c in enumerate((c0, c1, c2, c3)):
        source = lax.rem(head - s + 4, 4) * 256
        for part in range(2):
            at = pl.ds(part * 128, 128)
            pairs.append((c.at[at], co_ref.at[pl.ds(source + part * 128, 128)]))
    for w, w_ref in ((up_hbm, up_ref), (down_hbm, down_ref)):
        for part in range(4):
            at = pl.ds(part * 256, 256)
            pairs.append((w.at[at], w_ref.at[at]))
    copies = begin_copies(pairs, sems)
    low_lanes = lax.broadcasted_iota(jnp.int32, (1, 128), 1) < 64
    for y in range(4):
        for pair in range(2):
            even = heads_ref[2 * pair * 4 + y].astype(f32)
            odd = heads_ref[(2 * pair + 1) * 4 + y].astype(f32)
            at = slice(y * 256 + pair * 128, y * 256 + (pair + 1) * 128)
            mixed_ref[0:128, at] = jnp.where(low_lanes, even, pltpu.roll(odd, 64, 1)).astype(bf16)
            mixed_ref[128:256, at] = jnp.where(low_lanes, pltpu.roll(even, 64, 1), odd).astype(bf16)
    finish_copies(copies[:8])
    first = short_ref[...].astype(f32) + dot(mixed_ref[...], co_ref[...])
    all_ref[...] = first
    first_ref[...] = all_ref[pl.ds(pl.multiple_of(head * 64, 64), 64), :]
    feed = norm_rows(first, gain_ref[...])
    finish_copies(copies[8:])
    inner = jax.nn.gelu(dot(feed, up_ref[...])).astype(bf16)
    part_ref[...] = dot(inner, down_ref[...]).astype(bf16).reshape(4, 64, D)


def final_kernel(where_ref, s0, s1, s2, s3, b0, b1, b2, b3, up_ref, out_ref):
    head = where_ref[1]
    rows = 256 + HALO
    second = jnp.concatenate([ref[...] for ref in (s0, s1, s2, s3)], axis=0)
    lifted = dot(second, up_ref[...])
    index = lax.broadcasted_iota(jnp.int32, (256, rows), 0)
    column = lax.broadcasted_iota(jnp.int32, (256, rows), 1)
    r, m = index // 64, index % 64
    source = jnp.where(r == 0, 192 + m, jnp.where(m == 63, 268 + r, (r - 1) * 64 + m + 1))
    choose = (source == column).astype(f32).astype(bf16)
    index = lax.broadcasted_iota(jnp.int32, (256, 256), 0)
    column = lax.broadcasted_iota(jnp.int32, (256, 256), 1)
    weave = ((index % 4) * 64 + index // 4 == column).astype(f32).astype(bf16)
    for s, block in enumerate((b0, b1, b2, b3)):
        mine = lifted[s * 64 : (s + 1) * 64]
        raised = jnp.concatenate([mine[:, q * SHARE : (q + 1) * SHARE] for q in range(4)], axis=0)
        value = (dot(choose, block[...]) + raised).astype(bf16)
        begin = pl.multiple_of(lax.rem(head - s + 4, 4) * 256, 256)
        out_ref[pl.ds(begin, 256), :] = dot(weave, value).astype(bf16)


def fetch_rest(weight):
    return [shift(weight, "head", s, 4) for s in range(1, 4)]


def after(value, gate):
    return lax.optimization_barrier((value, gate))


def local(
    token_ids, embedding, fine_norm, fine_query, fine_key, fine_value, fine_output,
    shorten_weight, coarse_norm, coarse_query, coarse_key, coarse_value, coarse_output,
    ffn_norm, ffn_up, ffn_down, upsample_weight,
):
    place = lax.axis_index(SEQ).astype(jnp.int32)
    head = lax.axis_index("head").astype(jnp.int32)
    x_place = lax.axis_index("x").astype(jnp.int32)
    core = lax.axis_index("core").astype(jnp.int32)
    tables = jnp.asarray(angle_tables())
    where = jnp.stack([place, head, core])

    prior = later(token_ids, SEQ, 1, 32)
    fine_output_held, last_ids = after(fine_output, token_ids[ROWS - BLOCK :])
    before = later(last_ids, SEQ, 2, 32)
    past_ids = jnp.concatenate([before, prior])
    out_rest = fetch_rest(fine_output_held)

    rows = 256 + HALO
    all_ids = jnp.concatenate([past_ids, token_ids])
    mixed = call(
        fine_kernel, "fine_attention", [jax.ShapeDtypeStruct((rows, SHARE), bf16)] * 4,
        [where],
        [all_ids[:, None], fine_norm[None]],
        [
            pltpu.VMEM((9, 256, SHARE), bf16), pltpu.VMEM((BLOCK + ROWS, SHARE), bf16),
            pltpu.VMEM((KEYS, SHARE), bf16), pltpu.VMEM((KEYS, SHARE), bf16),
            pltpu.VMEM((576, 128), f32), pltpu.VMEM((256, D), bf16),
            pltpu.VMEM((3, D, SHARE), bf16), pltpu.SemaphoreType.DMA((8,)),
        ],
        grid=(4,), us=15, limit=24,
        hbm=[tables, embedding, fine_query, fine_key, fine_value],
    )

    got = [mixed[0]] + [shift(mixed[s], "head", s, 4) for s in range(1, 4)]
    own_ids = lax.dynamic_slice_in_dim(
        jnp.concatenate([past_ids[PAST - HALO :], token_ids]), head * 256, rows, 0
    )
    sends = call(
        fine_rows_kernel, "fine_rows", jax.ShapeDtypeStruct((4, rows, SHARE), bf16),
        [where], [own_ids[:, None], embedding, *got],
        [pltpu.VMEM((D, D), bf16), pltpu.SemaphoreType.DMA((8,))],
        hbm=[fine_output], free=out_rest,
    )
    blocks = exchange(lambda d: lax.dynamic_index_in_dim(sends, d, 0, keepdims=False), "head", 4)

    terms = []
    for s, block in enumerate(blocks):
        part = call(
            short_part_kernel, "short_part", jax.ShapeDtypeStruct((64, D), bf16), [],
            [block, shorten_weight],
        )
        terms.append(part if s == 0 else shift(part, "head", 4 - s, 4))
    short_own = sum(t.astype(f32) for t in terms).astype(bf16)
    shorts = [short_own] + [shift(short_own, "head", s, 4) for s in range(1, 4)]
    packed, short = call(
        coarse_pack_kernel, "coarse_pack",
        [
            jax.ShapeDtypeStruct((4, COARSE_ROWS * 3 // 2, 128), bf16),
            jax.ShapeDtypeStruct((COARSE_ROWS, D), bf16),
        ],
        [where],
        [*shorts, coarse_norm[None], coarse_query, coarse_key, coarse_value, tables],
    )

    turned = lax.all_to_all(packed, "z", 0, 0)
    coarse_output_held, turned = after(coarse_output, turned)
    kv = turned[:, :COARSE_ROWS]
    far = [shift(kv, "core", 1, 2)]
    near = [shift(kv, "x", s, 4) for s in range(1, 4)]
    steps = jnp.arange(4, dtype=jnp.int32)
    flags = ((x_place - steps + 4) % 4 < x_place).astype(jnp.int32) + (steps == 0) * core
    wide = jax.ShapeDtypeStruct((1024, 128), f32)
    q_all, *sums = call(
        coarse_first_kernel, "coarse_first",
        [jax.ShapeDtypeStruct((1024, 128), bf16), wide, wide, wide], [flags], [turned, far[0]],
        us=3, limit=24,
    )
    co_rest = fetch_rest(coarse_output_held)
    near_held, q_all = after(near, q_all)
    far += [shift(part, "core", 1, 2) for part in near_held]
    sums = call(
        functools.partial(coarse_more_kernel, (1, 3), False), "coarse_more", [wide] * 3,
        [flags], [near[0], far[1], near[2], far[3], q_all, *sums], us=6, limit=24,
    )
    wide_sends = call(
        functools.partial(coarse_more_kernel, (2,), True), "coarse_last",
        jax.ShapeDtypeStruct((16, 128, 128), bf16),
        [flags], [near[1], far[2], q_all, *sums], [pltpu.VMEM((1024, 128), f32)] * 3, us=3, limit=24,
    )
    heads_in = lax.all_to_all(wide_sends, ("z", "head"), 0, 0)
    square = pltpu.VMEM((D, D), bf16)
    parts, first_own = call(
        feed_kernel, "feed",
        [jax.ShapeDtypeStruct((4, 64, D), bf16), jax.ShapeDtypeStruct((64, D), f32)],
        [where],
        [heads_in, short, ffn_norm[None]],
        [
            pltpu.VMEM((COARSE_ROWS, D), bf16), pltpu.VMEM((COARSE_ROWS, D), f32),
            square, square, square, pltpu.SemaphoreType.DMA((16,)),
        ],
        hbm=[coarse_output, ffn_up, ffn_down], free=co_rest, us=4, limit=24,
    )
    sums = exchange(lambda d: lax.dynamic_index_in_dim(parts, d, 0, keepdims=False), "head", 4)
    second_own = (first_own + sum(t.astype(f32) for t in sums)).astype(bf16)
    seconds = [second_own] + [shift(second_own, "head", s, 4) for s in range(1, 4)]
    return call(
        final_kernel, "final", jax.ShapeDtypeStruct((ROWS, SHARE), bf16),
        [where], [*seconds, *blocks, upsample_weight.reshape(D, SHORTEN * SHARE)],
    )


def solution(mesh):
    split = Mesh(mesh.devices.reshape(4, 4, 2, 4), ("z", "x", "core", "head"))
    return jax.shard_map(
        local,
        mesh=split,
        in_specs=(
            P(SEQ), P(), P(), P(None, "head"), P(None, "head"), P(None, "head"), P("head", None),
            P(None, "head", None), P(), P(None, "head"), P(None, "head"), P(None, "head"),
            P("head", None), P(), P(None, "head"), P("head", None), P(None, None, "head"),
        ),
        out_specs=P(SEQ, "head"),
        check_vma=False,
    )
```

```python
import functools
import math

import jax
import jax.numpy as jnp
import numpy as np
from jax import lax
from jax.experimental import pallas as pl
from jax.experimental.pallas import tpu as pltpu
from jax.sharding import Mesh
from jax.sharding import PartitionSpec as P

D = 1024
HEAD_DIM = 64
SHORTEN = 4
WINDOW = 1024
BLOCK = 256
HALO = 16
ROWS = 1024
PAST = WINDOW + BLOCK
KEYS = PAST + ROWS
SHARE = 256
COARSE_ROWS = 256
SEQ = ("z", "x", "core")

epsilon = 1e-06
masked_low = -1e30
q_scale = HEAD_DIM ** (-0.5) * math.log2(math.e)
bf16 = jnp.bfloat16
f32 = jnp.float32


def angle_tables():
    lane = np.arange(128) % 32
    period = 2.0 ** (4 + lane * 14 // 32)
    coarse = (256.0 * np.arange(32)[:, None]) % period[None]
    near = np.arange(256)[:, None] % period[None]
    a = coarse * (2.0 * np.pi / period)[None]
    b = near * (2.0 * np.pi / period)[None]
    parts = [np.cos(a), np.sin(a), np.cos(b), np.sin(b)]
    return np.concatenate(parts, axis=0).astype(np.float32)


def shift(value, axis, steps, count):
    return lax.ppermute(value, axis, [(i, (i + steps) % count) for i in range(count)])


def later(value, axis, steps, count):
    return lax.ppermute(value, axis, [(i, i + steps) for i in range(count - steps)])


def exchange(block_for, axis, count):
    me = lax.axis_index(axis)
    got = [block_for(me)]
    for s in range(1, count):
        got.append(shift(block_for((me + s) % count), axis, s, count))
    return got


def dot(left, right):
    return jnp.dot(left, right, preferred_element_type=f32)


def dot_t(left, right):
    return lax.dot_general(left, right, (((1,), (1,)), ((), ())), preferred_element_type=f32)


def norm_rows(data, gain):
    power = jnp.mean(data * data, axis=-1, keepdims=True)
    return (data * lax.rsqrt(power + epsilon) * gain).astype(bf16)


def partner(values):
    width = values.shape[1]
    lane = lax.broadcasted_iota(jnp.int32, values.shape, 1)
    ahead = pltpu.roll(values, width - 32, 1)
    behind = pltpu.roll(values, 32, 1)
    return jnp.where(lane % 64 < 32, -ahead, behind)


def halves(table):
    high = table.astype(bf16)
    low = (table - high.astype(f32)).astype(bf16)
    return high, low


def turn_tables(turn_ref, far):
    ca = turn_ref[pl.ds(far, 1), :]
    sa = turn_ref[pl.ds(32 + far, 1), :]
    cb = turn_ref[64:320, :]
    sb = turn_ref[320:576, :]
    cosine = ca * cb - sa * sb
    sine = sa * cb + ca * sb
    return jnp.concatenate([cosine, cosine], axis=1), jnp.concatenate([sine, sine], axis=1)


def pick(ids, levels=256):
    columns = lax.broadcasted_iota(jnp.int32, (ids.shape[0], levels), 1)
    return (ids == columns).astype(f32).astype(bf16)


def turned_rows(hot, tab_ref, n, cosine, sine):
    plain = dot(hot, tab_ref[n]) + dot(hot, tab_ref[n + 1])
    other = dot(hot, tab_ref[n + 2]) + dot(hot, tab_ref[n + 3])
    return (plain * cosine + other * sine).astype(bf16)


def fine_tables_kernel(gain_hbm, emb_hbm, wq_hbm, wk_hbm, wv_hbm, tab_hbm, tab_ref, gain_ref, emb_ref, w_ref, sems):
    pairs = [(emb_hbm, emb_ref), (gain_hbm, gain_ref)]
    for n, w in enumerate((wq_hbm, wk_hbm, wv_hbm)):
        for part in range(2):
            rows = pl.ds(part * 512, 512)
            pairs.append((w.at[rows], w_ref.at[n, rows]))
    copies = begin_copies(pairs, sems)
    finish_copies(copies[:2])
    fine_in = norm_rows(emb_ref[...].astype(f32), gain_ref[...])
    finish_copies(copies[2:])
    tq = dot(fine_in, w_ref[0]) * q_scale
    tk = dot(fine_in, w_ref[1])
    for n, table in enumerate((tq, partner(tq), tk, partner(tk))):
        high, low = halves(table)
        tab_ref[2 * n] = high
        tab_ref[2 * n + 1] = low
    tab_ref[8] = dot(fine_in, w_ref[2]).astype(bf16)
    finish_copies(begin_copies([(tab_ref.at[n], tab_hbm.at[n]) for n in range(9)], sems))


def fine_kernel(
    where_ref, before_ref, prior_ref, own_ref, tab_hbm, turn_hbm,
    o0, o1, o2, o3, q_ref, k_ref, v_ref, tab_ref, turn_ref, sems,
):
    step = pl.program_id(0)
    head = where_ref[1]
    quarter = lax.rem(head + step, 4)
    outs = (o0, o1, o2, o3)
    lowest = jnp.maximum(PAST - where_ref[0] * ROWS, 0)
    head_lane = lax.broadcasted_iota(jnp.int32, (1, SHARE), 1) // HEAD_DIM

    @pl.when(step == 0)
    def _():
        def build(block, ids, with_q):
            begin = pl.multiple_of(block * BLOCK, BLOCK)
            hot = pick(ids)
            cosine, sine = turn_tables(turn_ref, block)
            k_ref[pl.ds(begin, BLOCK), :] = turned_rows(hot, tab_ref, 4, cosine, sine)
            v_ref[pl.ds(begin, BLOCK), :] = dot(hot, tab_ref[8]).astype(bf16)
            if with_q:
                at = pl.multiple_of(begin - (PAST - BLOCK), BLOCK)
                q_ref[pl.ds(at, BLOCK), :] = turned_rows(hot, tab_ref, 0, cosine, sine)

        def build_from(ref, first, with_q):
            def body(n, _):
                ids = ref[pl.ds(pl.multiple_of(n * BLOCK, BLOCK), BLOCK), :]
                build(first + n, ids, with_q)
                return 0

            return body

        pairs = [(tab_hbm.at[n], tab_ref.at[n]) for n in range(9)] + [(turn_hbm, turn_ref)]
        finish_copies(begin_copies(pairs, sems))
        build(0, before_ref[...], False)
        lax.fori_loop(0, 3, build_from(prior_ref, 1, False), 0)
        build(4, prior_ref[3 * BLOCK :, :], True)
        lax.fori_loop(0, 4, build_from(own_ref, 5, True), 0)
        halo_q = q_ref[BLOCK - HALO : BLOCK, :]
        stacked = jnp.concatenate(
            [jnp.where(head_lane == h, halo_q, jnp.zeros_like(halo_q)) for h in range(4)], axis=0
        )
        scores = dot_t(stacked, k_ref[0:PAST, :])
        row = lax.broadcasted_iota(jnp.int32, scores.shape, 0) % HALO + (PAST - HALO)
        col = lax.broadcasted_iota(jnp.int32, scores.shape, 1)
        allowed = (col <= row) & (col > row - WINDOW) & (col >= lowest)
        scores = jnp.where(allowed, scores, masked_low)
        top = jnp.max(scores, axis=1, keepdims=True)
        weights = jnp.exp2(scores - top)
        total = jnp.sum(weights, axis=1, keepdims=True)
        mixed = dot(weights.astype(bf16), v_ref[0:PAST, :]) / total
        result = jnp.zeros((HALO, SHARE), f32)
        for h in range(4):
            result = jnp.where(head_lane == h, mixed[h * HALO : (h + 1) * HALO], result)
        for s, out_ref in enumerate(outs):

            @pl.when(lax.rem(head + s, 4) == 0)
            def _(out_ref=out_ref):
                out_ref[0:HALO, :] = result.astype(bf16)

    begin = pl.multiple_of((quarter + 1) * BLOCK, BLOCK)
    keys = k_ref[pl.ds(begin, PAST), :]
    values = v_ref[pl.ds(begin, PAST), :]
    query = q_ref[pl.ds(begin, BLOCK), :]
    row = lax.broadcasted_iota(jnp.int32, (BLOCK, BLOCK), 0)
    col = lax.broadcasted_iota(jnp.int32, (BLOCK, BLOCK), 1)
    biases = [
        jnp.where(begin + t * BLOCK >= lowest, 0.0, masked_low).astype(f32) for t in range(4)
    ]
    first_bias = jnp.where(col > row, 0.0, masked_low) + biases[0]
    last_bias = jnp.where(col <= row, 0.0, masked_low)
    ones = jnp.ones((PAST, 128), bf16)
    low_lanes = lax.broadcasted_iota(jnp.int32, (1, 128), 1) < 64
    results = []
    for h in range(4):
        scores = dot_t(jnp.where(head_lane == h, query, jnp.zeros_like(query)), keys)
        tiles = [scores[:, t * BLOCK : (t + 1) * BLOCK] for t in range(5)]
        tiles = (
            [tiles[0] + first_bias]
            + [tiles[t] + biases[t] for t in range(1, 4)]
            + [tiles[4] + last_bias]
        )
        peak = tiles[0]
        for t in range(1, 5):
            peak = jnp.maximum(peak, tiles[t])
        top = jnp.max(peak, axis=1, keepdims=True)
        weights = [jnp.exp2(tile - top).astype(bf16) for tile in tiles]
        pair = (h // 2) * 128
        wide = jnp.concatenate([values[:, pair : pair + 128], ones], axis=1)
        mixed = dot(jnp.concatenate(weights, axis=1), wide)
        results.append(mixed[:, :128] / mixed[:, 128:])
    result = jnp.concatenate(
        [jnp.where(low_lanes, results[2 * n], results[2 * n + 1]) for n in range(2)], axis=1
    )
    result = result.astype(bf16)
    for s in range(4):

        @pl.when(step == s)
        def _(s=s):
            outs[s][HALO:, :] = result

            @pl.when(quarter < 3)
            def _():
                outs[(s + 1) % 4][0:HALO, :] = result[BLOCK - HALO :]


def vmem():
    return pl.BlockSpec(memory_space=pltpu.VMEM)


def smem():
    return pl.BlockSpec(memory_space=pltpu.SMEM)


def call(kernel, name, shapes, scalars, arrays, scratch=(), grid=None, limit=16, us=2, hbm=(), out_hbm=False):
    one = not isinstance(shapes, (list, tuple))
    extra = {} if grid is None else {"grid": grid}
    return pl.pallas_call(
        kernel,
        out_shape=shapes,
        in_specs=[smem()] * len(scalars)
        + [vmem()] * len(arrays)
        + [pl.BlockSpec(memory_space=pltpu.HBM)] * len(hbm),
        out_specs=(pl.BlockSpec(memory_space=pltpu.HBM) if out_hbm else vmem())
        if one
        else [vmem()] * len(shapes),
        scratch_shapes=list(scratch),
        compiler_params=pltpu.CompilerParams(vmem_limit_bytes=limit << 20),
        cost_estimate=pl.CostEstimate(
            flops=us * 10**9, transcendentals=0, bytes_accessed=us * 2 * 10**6
        ),
        name=name,
        **extra,
    )(*scalars, *arrays, *(pltpu.with_memory_space_constraint(a, pltpu.HBM) for a in hbm))


def begin_copies(pairs, sems):
    copies = [pltpu.make_async_copy(a, b, sems.at[n]) for n, (a, b) in enumerate(pairs)]
    for copy in copies:
        copy.start()
    return copies


def finish_copies(copies):
    for copy in copies:
        copy.wait()


def fine_rows_kernel(
    where_ref, ids_ref, emb_ref, g0, g1, g2, g3, w_hbm, out_ref, w_ref, got_ref, sems
):
    place, head = where_ref[0], where_ref[1]
    pairs = []
    for part in range(8):
        at = pl.ds(part * 128, 128)
        pairs.append((w_hbm.at[at], w_ref.at[at]))
    copies = begin_copies(pairs, sems)
    for s, got in enumerate((g0, g1, g2, g3)):
        begin = pl.multiple_of(lax.rem(head - s + 4, 4) * SHARE, SHARE)
        got_ref[:, pl.ds(begin, SHARE)] = got[...]
    merged = dot(pick(ids_ref[...]), emb_ref[...])
    finish_copies(copies)
    merged += dot(got_ref[...], w_ref[...])
    rows = 256 + HALO
    token = (
        place * ROWS + head * 256 - HALO + lax.broadcasted_iota(jnp.int32, (rows, D), 0)
    )
    fine = jnp.where(token >= 0, merged, 0.0).astype(bf16)
    index = lax.broadcasted_iota(jnp.int32, (256, rows), 0)
    column = lax.broadcasted_iota(jnp.int32, (256, rows), 1)
    source = 4 * (index % 64) + index // 64 + (HALO - 3)
    choose = (source == column).astype(f32).astype(bf16)
    grouped = dot(choose, fine).astype(bf16)
    for d in range(4):
        out_ref[d, 0:256, :] = grouped[:, d * SHARE : (d + 1) * SHARE]
        out_ref[d, 256:rows, :] = fine[256:rows, d * SHARE : (d + 1) * SHARE]


def short_part_kernel(group_ref, w_ref, out_ref):
    total = dot(group_ref[0:64, :], w_ref[0])
    for r in range(1, SHORTEN):
        total += dot(group_ref[r * 64 : (r + 1) * 64, :], w_ref[r])
    out_ref[...] = total.astype(bf16)


def coarse_pack_kernel(
    where_ref, s0, s1, s2, s3, gain_ref, wq_ref, wk_ref, wv_ref, turn_ref,
    out_ref, short_ref,
):
    place, head = where_ref[0], where_ref[1]
    for s, ref in enumerate((s0, s1, s2, s3)):
        begin = pl.multiple_of(lax.rem(head - s + 4, 4) * 64, 64)
        short_ref[pl.ds(begin, 64), :] = ref[...]
    x = norm_rows(short_ref[...].astype(f32), gain_ref[...])
    cosine, sine = turn_tables(turn_ref, place)

    def turned(values):
        return values * cosine + partner(values) * sine

    q = turned(dot(x, wq_ref[...])) * q_scale
    k = turned(dot(x, wk_ref[...]))
    v = dot(x, wv_ref[...])
    low_lanes = lax.broadcasted_iota(jnp.int32, (1, 128), 1) < 64
    half = COARSE_ROWS // 2
    for h in range(4):
        pair = (h // 2) * 128
        kp = k[:, pair : pair + 128]
        vp = v[:, pair : pair + 128]
        qp = q[:, pair : pair + 128]
        if h % 2 == 0:
            kv = jnp.where(low_lanes, kp, pltpu.roll(vp, 64, 1))
            qq = jnp.where(low_lanes, qp[:half], pltpu.roll(qp[half:], 64, 1))
        else:
            kv = jnp.where(low_lanes, pltpu.roll(kp, 64, 1), vp)
            qq = jnp.where(low_lanes, pltpu.roll(qp[:half], 64, 1), qp[half:])
        out_ref[h, 0:COARSE_ROWS, :] = kv.astype(bf16)
        out_ref[h, COARSE_ROWS : COARSE_ROWS + half, :] = qq.astype(bf16)


def with_ones(kv):
    return jnp.concatenate([kv, jnp.ones((kv.shape[0], 128), bf16)], axis=1)


def absorb(q_ref, top_ref, total_ref, acc_ref, begin, rows, parts):
    at = pl.ds(begin, rows)
    query = q_ref[at, :]
    scores = [dot_t(query, kv) for kv in parts]
    peak = scores[0]
    for s in scores[1:]:
        peak = jnp.maximum(peak, s)
    old = top_ref[at, :]
    top = jnp.maximum(old, jnp.max(peak, axis=1, keepdims=True))
    factor = jnp.exp2(old - top)
    both = jnp.concatenate([top, top], axis=1)
    contrib = dot(jnp.exp2(scores[0] - both).astype(bf16), with_ones(parts[0]))
    for s, kv in zip(scores[1:], parts[1:]):
        contrib = contrib + dot(jnp.exp2(s - both).astype(bf16), with_ones(kv))
    top_ref[at, :] = top
    total_ref[at, :] = total_ref[at, :] * factor + contrib[:, 128:]
    acc_ref[at, :] = acc_ref[at, :] * factor + contrib[:, :128]


def coarse_first_kernel(flag_ref, turned_ref, far_ref, q_ref, top_ref, total_ref, acc_ref):
    half = COARSE_ROWS // 2
    low_lanes = lax.broadcasted_iota(jnp.int32, (1, 128), 1) < 64
    row = lax.broadcasted_iota(jnp.int32, (256, 256), 0)
    col = lax.broadcasted_iota(jnp.int32, (256, 256), 1)
    for z in range(4):
        packed = turned_ref[z, COARSE_ROWS:, :].astype(f32)
        zero = jnp.zeros_like(packed)
        q_ref[z * 256 : z * 256 + half, :] = jnp.where(low_lanes, packed, zero).astype(bf16)
        q_ref[z * 256 + half : (z + 1) * 256, :] = jnp.where(
            low_lanes, pltpu.roll(packed, 64, 1), zero
        ).astype(bf16)
        kv = turned_ref[z, :COARSE_ROWS, :]
        at = pl.ds(z * 256, 256)
        scores = jnp.where(col <= row, dot_t(q_ref[at, :], kv), masked_low)
        top = jnp.max(scores, axis=1, keepdims=True)
        contrib = dot(jnp.exp2(scores - top).astype(bf16), with_ones(kv))
        top_ref[at, :] = jnp.broadcast_to(top, (256, 128))
        total_ref[at, :] = contrib[:, 128:]
        acc_ref[at, :] = contrib[:, :128]
    state = (q_ref, top_ref, total_ref, acc_ref)
    for z in range(3):
        absorb(
            *state, (z + 1) * 256, (3 - z) * 256, [turned_ref[z, :COARSE_ROWS, :], far_ref[z]]
        )

    @pl.when(flag_ref[0] > 0)
    def _():
        for z in range(4):
            absorb(*state, z * 256, 256, [far_ref[z]])


def coarse_more_kernel(which, last, flag_ref, *refs):
    count = 2 * len(which)
    chunks = refs[:count]
    q_ref, top_in, total_in, acc_in = refs[count : count + 4]
    out_ref = refs[count + 4] if last else None
    top_ref, total_ref, acc_ref = refs[-3:]
    top_ref[...] = top_in[...]
    total_ref[...] = total_in[...]
    acc_ref[...] = acc_in[...]
    state = (q_ref, top_ref, total_ref, acc_ref)
    for n, s in enumerate(which):
        near, far = chunks[2 * n], chunks[2 * n + 1]
        for z in range(3):
            absorb(*state, (z + 1) * 256, (3 - z) * 256, [near[z], far[z]])

        @pl.when(flag_ref[s] > 0)
        def _(near=near, far=far):
            for z in range(4):
                absorb(*state, z * 256, 256, [near[z], far[z]])

    if last:
        mixed = acc_ref[...] / total_ref[...]
        low_lanes = lax.broadcasted_iota(jnp.int32, (1, 128), 1) < 64
        for z in range(4):
            upper = pltpu.roll(mixed[z * 256 : z * 256 + 128], 64, 1)
            lower = mixed[z * 256 + 128 : (z + 1) * 256]
            block = jnp.where(low_lanes, upper, lower).astype(bf16)
            for y in range(4):
                out_ref[z * 4 + y] = block


def feed_kernel(
    where_ref, heads_ref, short_ref, gain_ref, up_hbm, down_hbm, co_hbm,
    part_ref, first_ref, mixed_ref, all_ref, co_ref, up_ref, down_ref, sems,
):
    head = where_ref[1]
    pairs = []
    for w, w_ref in ((co_hbm, co_ref), (up_hbm, up_ref), (down_hbm, down_ref)):
        for part in range(4):
            at = pl.ds(part * 256, 256)
            pairs.append((w.at[at], w_ref.at[at]))
    copies = begin_copies(pairs, sems)
    low_lanes = lax.broadcasted_iota(jnp.int32, (1, 128), 1) < 64
    for y in range(4):
        for pair in range(2):
            even = heads_ref[2 * pair * 4 + y].astype(f32)
            odd = heads_ref[(2 * pair + 1) * 4 + y].astype(f32)
            at = slice(y * 256 + pair * 128, y * 256 + (pair + 1) * 128)
            mixed_ref[0:128, at] = jnp.where(low_lanes, even, pltpu.roll(odd, 64, 1)).astype(bf16)
            mixed_ref[128:256, at] = jnp.where(low_lanes, pltpu.roll(even, 64, 1), odd).astype(bf16)
    finish_copies(copies[:4])
    first = short_ref[...].astype(f32) + dot(mixed_ref[...], co_ref[...])
    all_ref[...] = first
    first_ref[...] = all_ref[pl.ds(pl.multiple_of(head * 64, 64), 64), :]
    feed = norm_rows(first, gain_ref[...])
    finish_copies(copies[4:])
    inner = jax.nn.gelu(dot(feed, up_ref[...])).astype(bf16)
    part_ref[...] = dot(inner, down_ref[...]).astype(bf16).reshape(4, 64, D)


def final_kernel(where_ref, s0, s1, s2, s3, b0, b1, b2, b3, up_ref, out_ref):
    head = where_ref[1]
    rows = 256 + HALO
    second = jnp.concatenate([ref[...] for ref in (s0, s1, s2, s3)], axis=0)
    lifted = dot(second, up_ref[...])
    index = lax.broadcasted_iota(jnp.int32, (256, rows), 0)
    column = lax.broadcasted_iota(jnp.int32, (256, rows), 1)
    r, m = index // 64, index % 64
    source = jnp.where(r == 0, 192 + m, jnp.where(m == 63, 268 + r, (r - 1) * 64 + m + 1))
    choose = (source == column).astype(f32).astype(bf16)
    index = lax.broadcasted_iota(jnp.int32, (256, 256), 0)
    column = lax.broadcasted_iota(jnp.int32, (256, 256), 1)
    weave = ((index % 4) * 64 + index // 4 == column).astype(f32).astype(bf16)
    for s, block in enumerate((b0, b1, b2, b3)):
        mine = lifted[s * 64 : (s + 1) * 64]
        raised = jnp.concatenate([mine[:, q * SHARE : (q + 1) * SHARE] for q in range(4)], axis=0)
        value = (dot(choose, block[...]) + raised).astype(bf16)
        begin = pl.multiple_of(lax.rem(head - s + 4, 4) * 256, 256)
        out_ref[pl.ds(begin, 256), :] = dot(weave, value).astype(bf16)


def fetch_all(weight, core):
    half = lax.dynamic_slice_in_dim(weight, core * 128, 128, 0)
    return lax.all_gather(half, ("head", "core"), axis=0, tiled=True)


def after(value, gate):
    return lax.optimization_barrier((value, gate))


def local(
    token_ids, embedding, fine_norm, fine_query, fine_key, fine_value, fine_output,
    shorten_weight, coarse_norm, coarse_query, coarse_key, coarse_value, coarse_output,
    ffn_norm, ffn_up, ffn_down, upsample_weight,
):
    place = lax.axis_index(SEQ).astype(jnp.int32)
    head = lax.axis_index("head").astype(jnp.int32)
    x_place = lax.axis_index("x").astype(jnp.int32)
    core = lax.axis_index("core").astype(jnp.int32)
    tables = jnp.asarray(angle_tables())
    where = jnp.stack([place, head, core])

    prior = later(token_ids, SEQ, 1, 32)
    last_ids = token_ids[ROWS - BLOCK :]
    before = later(last_ids, SEQ, 2, 32)
    tab = call(
        fine_tables_kernel, "fine_tables", pltpu.HBM((9, 256, SHARE), bf16), [], [],
        [
            pltpu.VMEM((9, 256, SHARE), bf16),
            pltpu.VMEM((1, D), f32), pltpu.VMEM((256, D), bf16),
            pltpu.VMEM((3, D, SHARE), bf16), pltpu.SemaphoreType.DMA((9,)),
        ],
        us=3, out_hbm=True, hbm=[fine_norm[None], embedding, fine_query, fine_key, fine_value],
    )
    fine_output_held, _ = after(fine_output, last_ids)
    fine_output_all = fetch_all(fine_output_held, core)
    rows = 256 + HALO
    mixed = call(
        fine_kernel, "fine_attention", [jax.ShapeDtypeStruct((rows, SHARE), bf16)] * 4,
        [where], [before[:, None], prior[:, None], token_ids[:, None]],
        [
            pltpu.VMEM((BLOCK + ROWS, SHARE), bf16),
            pltpu.VMEM((KEYS, SHARE), bf16), pltpu.VMEM((KEYS, SHARE), bf16),
            pltpu.VMEM((9, 256, SHARE), bf16), pltpu.VMEM((576, 128), f32),
            pltpu.SemaphoreType.DMA((10,)),
        ],
        grid=(4,), us=12, limit=24, hbm=[tab, tables],
    )

    got = [mixed[0]] + [shift(mixed[s], "head", s, 4) for s in range(1, 4)]
    own_ids = lax.dynamic_slice_in_dim(
        jnp.concatenate([prior[ROWS - HALO :], token_ids]), head * 256, rows, 0
    )
    sends = call(
        fine_rows_kernel, "fine_rows", jax.ShapeDtypeStruct((4, rows, SHARE), bf16),
        [where], [own_ids[:, None], embedding, *got],
        [
            pltpu.VMEM((D, D), bf16), pltpu.VMEM((rows, D), bf16),
            pltpu.SemaphoreType.DMA((8,)),
        ],
        hbm=[fine_output_all],
    )
    blocks = exchange(lambda d: lax.dynamic_index_in_dim(sends, d, 0, keepdims=False), "head", 4)

    terms = []
    for s, block in enumerate(blocks):
        part = call(
            short_part_kernel, "short_part", jax.ShapeDtypeStruct((64, D), bf16), [],
            [block, shorten_weight],
        )
        terms.append(part if s == 0 else shift(part, "head", 4 - s, 4))
    short_own = sum(t.astype(f32) for t in terms).astype(bf16)
    shorts = [short_own] + [shift(short_own, "head", s, 4) for s in range(1, 4)]
    packed, short = call(
        coarse_pack_kernel, "coarse_pack",
        [
            jax.ShapeDtypeStruct((4, COARSE_ROWS * 3 // 2, 128), bf16),
            jax.ShapeDtypeStruct((COARSE_ROWS, D), bf16),
        ],
        [where],
        [*shorts, coarse_norm[None], coarse_query, coarse_key, coarse_value, tables],
    )

    coarse_output_held, packed = after(coarse_output, packed)
    coarse_output_all = fetch_all(coarse_output_held, core)
    turned = lax.all_to_all(packed, "z", 0, 0)
    kv = turned[:, :COARSE_ROWS]
    far = [shift(kv, "core", 1, 2)]
    near = [shift(kv, "x", s, 4) for s in range(1, 4)]
    steps = jnp.arange(4, dtype=jnp.int32)
    flags = ((x_place - steps + 4) % 4 < x_place).astype(jnp.int32) + (steps == 0) * core
    wide = jax.ShapeDtypeStruct((1024, 128), f32)
    q_all, *sums = call(
        coarse_first_kernel, "coarse_first",
        [jax.ShapeDtypeStruct((1024, 128), bf16), wide, wide, wide], [flags], [turned, far[0]],
        us=3, limit=24,
    )
    near_held, q_all = after(near, q_all)
    far += [shift(part, "core", 1, 2) for part in near_held]
    sums = call(
        functools.partial(coarse_more_kernel, (1, 3), False), "coarse_more", [wide] * 3,
        [flags], [near[0], far[1], near[2], far[3], q_all, *sums], us=6, limit=24,
    )
    wide_sends = call(
        functools.partial(coarse_more_kernel, (2,), True), "coarse_last",
        jax.ShapeDtypeStruct((16, 128, 128), bf16),
        [flags], [near[1], far[2], q_all, *sums], [pltpu.VMEM((1024, 128), f32)] * 3, us=3, limit=24,
    )
    heads_in = lax.all_to_all(wide_sends, ("z", "head"), 0, 0)
    square = pltpu.VMEM((D, D), bf16)
    parts, first_own = call(
        feed_kernel, "feed",
        [jax.ShapeDtypeStruct((4, 64, D), bf16), jax.ShapeDtypeStruct((64, D), f32)],
        [where],
        [heads_in, short, ffn_norm[None]],
        [
            pltpu.VMEM((COARSE_ROWS, D), bf16), pltpu.VMEM((COARSE_ROWS, D), f32),
            square, square, square, pltpu.SemaphoreType.DMA((12,)),
        ],
        hbm=[ffn_up, ffn_down, coarse_output_all], us=4, limit=24,
    )
    sums = exchange(lambda d: lax.dynamic_index_in_dim(parts, d, 0, keepdims=False), "head", 4)
    second_own = (first_own + sum(t.astype(f32) for t in sums)).astype(bf16)
    seconds = [second_own] + [shift(second_own, "head", s, 4) for s in range(1, 4)]
    return call(
        final_kernel, "final", jax.ShapeDtypeStruct((ROWS, SHARE), bf16),
        [where], [*seconds, *blocks, upsample_weight.reshape(D, SHORTEN * SHARE)],
    )


def solution(mesh):
    split = Mesh(mesh.devices.reshape(4, 4, 2, 4), ("z", "x", "core", "head"))
    return jax.shard_map(
        local,
        mesh=split,
        in_specs=(
            P(SEQ), P(), P(), P(None, "head"), P(None, "head"), P(None, "head"), P("head", None),
            P(None, "head", None), P(), P(None, "head"), P(None, "head"), P(None, "head"),
            P("head", None), P(), P(None, "head"), P("head", None), P(None, None, "head"),
        ),
        out_specs=P(SEQ, "head"),
        check_vma=False,
    )
```

```python
import functools
import math

import jax
import jax.numpy as jnp
import numpy as np
from jax import lax
from jax.experimental import pallas as pl
from jax.experimental.pallas import tpu as pltpu
from jax.sharding import Mesh
from jax.sharding import PartitionSpec as P

D = 1024
HEAD_DIM = 64
SHORTEN = 4
WINDOW = 1024
BLOCK = 256
HALO = 16
ROWS = 1024
PAST = WINDOW + BLOCK
KEYS = PAST + ROWS
SHARE = 256
COARSE_ROWS = 256
SEQ = ("z", "x", "core")

epsilon = 1e-06
masked_low = -1e30
q_scale = HEAD_DIM ** (-0.5) * math.log2(math.e)
bf16 = jnp.bfloat16
f32 = jnp.float32


def angle_tables():
    lane = np.arange(128) % 32
    period = 2.0 ** (4 + lane * 14 // 32)
    coarse = (256.0 * np.arange(32)[:, None]) % period[None]
    near = np.arange(256)[:, None] % period[None]
    a = coarse * (2.0 * np.pi / period)[None]
    b = near * (2.0 * np.pi / period)[None]
    parts = [np.cos(a), np.sin(a), np.cos(b), np.sin(b)]
    return np.concatenate(parts, axis=0).astype(np.float32)


def shift(value, axis, steps, count):
    return lax.ppermute(value, axis, [(i, (i + steps) % count) for i in range(count)])


def later(value, axis, steps, count):
    return lax.ppermute(value, axis, [(i, i + steps) for i in range(count - steps)])


def exchange(block_for, axis, count):
    me = lax.axis_index(axis)
    got = [block_for(me)]
    for s in range(1, count):
        got.append(shift(block_for((me + s) % count), axis, s, count))
    return got


def dot(left, right):
    return jnp.dot(left, right, preferred_element_type=f32)


def dot_t(left, right):
    return lax.dot_general(left, right, (((1,), (1,)), ((), ())), preferred_element_type=f32)


def norm_rows(data, gain):
    power = jnp.mean(data * data, axis=-1, keepdims=True)
    return (data * lax.rsqrt(power + epsilon) * gain).astype(bf16)


def partner(values):
    width = values.shape[1]
    lane = lax.broadcasted_iota(jnp.int32, values.shape, 1)
    ahead = pltpu.roll(values, width - 32, 1)
    behind = pltpu.roll(values, 32, 1)
    return jnp.where(lane % 64 < 32, -ahead, behind)


def halves(table):
    high = table.astype(bf16)
    low = (table - high.astype(f32)).astype(bf16)
    return high, low


def turn_tables(turn_ref, far):
    ca = turn_ref[pl.ds(far, 1), :]
    sa = turn_ref[pl.ds(32 + far, 1), :]
    cb = turn_ref[64:320, :]
    sb = turn_ref[320:576, :]
    cosine = ca * cb - sa * sb
    sine = sa * cb + ca * sb
    return jnp.concatenate([cosine, cosine], axis=1), jnp.concatenate([sine, sine], axis=1)


def pick(ids, levels=256):
    columns = lax.broadcasted_iota(jnp.int32, (ids.shape[0], levels), 1)
    return (ids == columns).astype(f32).astype(bf16)


def turned_rows(hot, tab_ref, n, cosine, sine):
    return (dot(hot, tab_ref[n]) * cosine + dot(hot, tab_ref[n + 1]) * sine).astype(bf16)


def fine_tables_kernel(gain_hbm, emb_hbm, wq_hbm, wk_hbm, wv_hbm, tab_hbm, tab_ref, gain_ref, emb_ref, w_ref, sems):
    pairs = [(emb_hbm, emb_ref), (gain_hbm, gain_ref)]
    for n, w in enumerate((wq_hbm, wk_hbm, wv_hbm)):
        for part in range(2):
            rows = pl.ds(part * 512, 512)
            pairs.append((w.at[rows], w_ref.at[n, rows]))
    copies = begin_copies(pairs, sems)
    finish_copies(copies[:2])
    fine_in = norm_rows(emb_ref[...].astype(f32), gain_ref[...])
    finish_copies(copies[2:])
    tq = dot(fine_in, w_ref[0]) * q_scale
    tk = dot(fine_in, w_ref[1])
    tables = (tq, partner(tq), tk, partner(tk), dot(fine_in, w_ref[2]))
    for n, table in enumerate(tables):
        tab_ref[n] = table.astype(bf16)
    finish_copies(begin_copies([(tab_ref.at[n], tab_hbm.at[n]) for n in range(5)], sems))


def fine_kernel(
    where_ref, before_ref, prior_ref, own_ref, tab_hbm, turn_hbm,
    out_ref, q_ref, k_ref, v_ref, tab_ref, turn_ref, sems,
):
    step = pl.program_id(0)
    lowest = jnp.maximum(PAST - where_ref[0] * ROWS, 0)
    head_lane = lax.broadcasted_iota(jnp.int32, (1, SHARE), 1) // HEAD_DIM

    @pl.when(step == 0)
    def _():
        pairs = [(tab_hbm.at[n], tab_ref.at[n]) for n in range(5)] + [(turn_hbm, turn_ref)]
        finish_copies(begin_copies(pairs, sems))
        cosine, sine = turn_tables(turn_ref, 0)
        oldest = pick(before_ref[...])
        at = slice(BLOCK - HALO, BLOCK)
        k_ref[at, :] = turned_rows(oldest, tab_ref, 2, cosine[at], sine[at])
        v_ref[at, :] = dot(oldest, tab_ref[4]).astype(bf16)

        def build(block, ids, with_q):
            begin = pl.multiple_of(block * BLOCK, BLOCK)
            hot = pick(ids)
            cosine, sine = turn_tables(turn_ref, block)
            k_ref[pl.ds(begin, BLOCK), :] = turned_rows(hot, tab_ref, 2, cosine, sine)
            v_ref[pl.ds(begin, BLOCK), :] = dot(hot, tab_ref[4]).astype(bf16)
            if with_q:
                at = pl.multiple_of(begin - (PAST - BLOCK), BLOCK)
                q_ref[pl.ds(at, BLOCK), :] = turned_rows(hot, tab_ref, 0, cosine, sine)

        def build_from(ref, first, with_q):
            def body(n, _):
                ids = ref[pl.ds(pl.multiple_of(n * BLOCK, BLOCK), BLOCK), :]
                build(first + n, ids, with_q)
                return 0

            return body

        lax.fori_loop(0, 3, build_from(prior_ref, 1, False), 0)
        build(4, prior_ref[3 * BLOCK :, :], True)
        lax.fori_loop(0, 4, build_from(own_ref, 5, True), 0)
        halo_q = q_ref[BLOCK - HALO : BLOCK, :]
        stacked = jnp.concatenate(
            [jnp.where(head_lane == h, halo_q, jnp.zeros_like(halo_q)) for h in range(4)], axis=0
        )
        scores = dot_t(stacked, k_ref[BLOCK - HALO : PAST, :])
        row = lax.broadcasted_iota(jnp.int32, scores.shape, 0) % HALO + (PAST - HALO)
        col = lax.broadcasted_iota(jnp.int32, scores.shape, 1) + (BLOCK - HALO)
        allowed = (col <= row) & (col > row - WINDOW) & (col >= lowest)
        scores = jnp.where(allowed, scores, masked_low)
        top = jnp.max(scores, axis=1, keepdims=True)
        weights = jnp.exp2(scores - top)
        total = jnp.sum(weights, axis=1, keepdims=True)
        mixed = dot(weights.astype(bf16), v_ref[BLOCK - HALO : PAST, :]) / total
        result = jnp.zeros((HALO, SHARE), f32)
        for h in range(4):
            result = jnp.where(head_lane == h, mixed[h * HALO : (h + 1) * HALO], result)
        out_ref[0, 0:HALO, :] = result.astype(bf16)

    begin = pl.multiple_of((step + 1) * BLOCK, BLOCK)
    keys = k_ref[pl.ds(begin, PAST), :]
    values = v_ref[pl.ds(begin, PAST), :]
    query = q_ref[pl.ds(begin, BLOCK), :]
    row = lax.broadcasted_iota(jnp.int32, (BLOCK, BLOCK), 0)
    col = lax.broadcasted_iota(jnp.int32, (BLOCK, BLOCK), 1)
    biases = [
        jnp.where(begin + t * BLOCK >= lowest, 0.0, masked_low).astype(f32) for t in range(4)
    ]
    first_bias = jnp.where(col > row, 0.0, masked_low) + biases[0]
    last_bias = jnp.where(col <= row, 0.0, masked_low)
    ones = jnp.ones((PAST, 128), bf16)
    low_lanes = lax.broadcasted_iota(jnp.int32, (1, 128), 1) < 64
    results = []

    def score(h):
        return dot_t(jnp.where(head_lane == h, query, jnp.zeros_like(query)), keys)

    ahead = score(0)
    for h in range(4):
        scores = ahead
        if h < 3:
            ahead = score(h + 1)
        tiles = [scores[:, t * BLOCK : (t + 1) * BLOCK] for t in range(5)]
        tiles = (
            [tiles[0] + first_bias]
            + [tiles[t] + biases[t] for t in range(1, 4)]
            + [tiles[4] + last_bias]
        )
        peak = tiles[0]
        for t in range(1, 5):
            peak = jnp.maximum(peak, tiles[t])
        top = jnp.max(peak, axis=1, keepdims=True)
        weights = [jnp.exp2(tile - top).astype(bf16) for tile in tiles]
        pair = (h // 2) * 128
        wide = jnp.concatenate([values[:, pair : pair + 128], ones], axis=1)
        mixed = dot(jnp.concatenate(weights, axis=1), wide)
        results.append(mixed[:, :128] / mixed[:, 128:])
    result = jnp.concatenate(
        [jnp.where(low_lanes, results[2 * n], results[2 * n + 1]) for n in range(2)], axis=1
    )
    result = result.astype(bf16)
    out_ref[step, HALO:, :] = result

    @pl.when(step < 3)
    def _():
        out_ref[step + 1, 0:HALO, :] = result[BLOCK - HALO :]


def vmem():
    return pl.BlockSpec(memory_space=pltpu.VMEM)


def smem():
    return pl.BlockSpec(memory_space=pltpu.SMEM)


def call(kernel, name, shapes, scalars, arrays, scratch=(), grid=None, limit=16, us=2, hbm=(), out_hbm=False):
    one = not isinstance(shapes, (list, tuple))
    extra = {} if grid is None else {"grid": grid}
    return pl.pallas_call(
        kernel,
        out_shape=shapes,
        in_specs=[smem()] * len(scalars)
        + [vmem()] * len(arrays)
        + [pl.BlockSpec(memory_space=pltpu.HBM)] * len(hbm),
        out_specs=(pl.BlockSpec(memory_space=pltpu.HBM) if out_hbm else vmem())
        if one
        else [vmem()] * len(shapes),
        scratch_shapes=list(scratch),
        compiler_params=pltpu.CompilerParams(vmem_limit_bytes=limit << 20),
        cost_estimate=pl.CostEstimate(
            flops=us * 10**9, transcendentals=0, bytes_accessed=us * 2 * 10**6
        ),
        name=name,
        **extra,
    )(*scalars, *arrays, *(pltpu.with_memory_space_constraint(a, pltpu.HBM) for a in hbm))


def begin_copies(pairs, sems):
    copies = [pltpu.make_async_copy(a, b, sems.at[n]) for n, (a, b) in enumerate(pairs)]
    for copy in copies:
        copy.start()
    return copies


def finish_copies(copies):
    for copy in copies:
        copy.wait()


def fine_rows_kernel(
    where_ref, ids_ref, emb_ref, got_ref, own_ref, m1, m2, m3, t1, t2, t3, w_hbm,
    out_ref, w_ref, sems,
):
    place, head, core = where_ref[0], where_ref[1], where_ref[2]
    copies = begin_copies([(w_hbm.at[n], w_ref.at[n]) for n in range(4)], sems)
    merged = dot(pick(ids_ref[...]), emb_ref[...]) + dot(got_ref[head], own_ref[...])
    near = pl.ds(pl.multiple_of(core * 128, 128), 128)
    far = pl.ds(pl.multiple_of(128 - core * 128, 128), 128)
    for s, mine, other in ((1, m1, t1), (2, m2, t2), (3, m3, t3)):
        source = lax.rem(head - s + 4, 4)
        merged += dot(got_ref[source, :, near], mine[...])
        merged += dot(got_ref[source, :, far], other[...])
    rows = 256 + HALO
    token = (
        place * ROWS + head * 256 - HALO + lax.broadcasted_iota(jnp.int32, (rows, D), 0)
    )
    fine = jnp.where(token >= 0, merged, 0.0).astype(bf16)
    index = lax.broadcasted_iota(jnp.int32, (256, rows), 0)
    column = lax.broadcasted_iota(jnp.int32, (256, rows), 1)
    source = 4 * (index % 64) + index // 64 + (HALO - 3)
    choose = (source == column).astype(f32).astype(bf16)
    grouped = dot(choose, fine).astype(bf16)
    for d in range(4):
        out_ref[d, 0:256, :] = grouped[:, d * SHARE : (d + 1) * SHARE]
        out_ref[d, 256:rows, :] = fine[256:rows, d * SHARE : (d + 1) * SHARE]
    finish_copies(copies)


def short_part_kernel(group_ref, w_ref, out_ref):
    total = dot(group_ref[0:64, :], w_ref[0])
    for r in range(1, SHORTEN):
        total += dot(group_ref[r * 64 : (r + 1) * 64, :], w_ref[r])
    out_ref[...] = total.astype(bf16)


def coarse_pack_kernel(
    where_ref, s0, s1, s2, s3, gain_ref, wq_ref, wk_ref, wv_ref, turn_ref,
    out_ref, short_ref,
):
    place, head = where_ref[0], where_ref[1]
    for s, ref in enumerate((s0, s1, s2, s3)):
        begin = pl.multiple_of(lax.rem(head - s + 4, 4) * 64, 64)
        short_ref[pl.ds(begin, 64), :] = ref[...]
    x = norm_rows(short_ref[...].astype(f32), gain_ref[...])
    cosine, sine = turn_tables(turn_ref, place)

    def turned(values):
        return values * cosine + partner(values) * sine

    q = turned(dot(x, wq_ref[...])) * q_scale
    k = turned(dot(x, wk_ref[...]))
    v = dot(x, wv_ref[...])
    low_lanes = lax.broadcasted_iota(jnp.int32, (1, 128), 1) < 64
    half = COARSE_ROWS // 2
    for h in range(4):
        pair = (h // 2) * 128
        kp = k[:, pair : pair + 128]
        vp = v[:, pair : pair + 128]
        qp = q[:, pair : pair + 128]
        if h % 2 == 0:
            kv = jnp.where(low_lanes, kp, pltpu.roll(vp, 64, 1))
            qq = jnp.where(low_lanes, qp[:half], pltpu.roll(qp[half:], 64, 1))
        else:
            kv = jnp.where(low_lanes, pltpu.roll(kp, 64, 1), vp)
            qq = jnp.where(low_lanes, pltpu.roll(qp[:half], 64, 1), qp[half:])
        out_ref[h, 0:COARSE_ROWS, :] = kv.astype(bf16)
        out_ref[h, COARSE_ROWS : COARSE_ROWS + half, :] = qq.astype(bf16)


def with_ones(kv):
    return jnp.concatenate([kv, jnp.ones((kv.shape[0], 128), bf16)], axis=1)


def absorb(q_ref, top_ref, total_ref, acc_ref, begin, rows, parts):
    at = pl.ds(begin, rows)
    query = q_ref[at, :]
    scores = [dot_t(query, kv) for kv in parts]
    peak = scores[0]
    for s in scores[1:]:
        peak = jnp.maximum(peak, s)
    old = top_ref[at, :]
    top = jnp.maximum(old, jnp.max(peak, axis=1, keepdims=True))
    factor = jnp.exp2(old - top)
    both = jnp.concatenate([top, top], axis=1)
    contrib = dot(jnp.exp2(scores[0] - both).astype(bf16), with_ones(parts[0]))
    for s, kv in zip(scores[1:], parts[1:]):
        contrib = contrib + dot(jnp.exp2(s - both).astype(bf16), with_ones(kv))
    top_ref[at, :] = top
    total_ref[at, :] = total_ref[at, :] * factor + contrib[:, 128:]
    acc_ref[at, :] = acc_ref[at, :] * factor + contrib[:, :128]


def coarse_first_kernel(flag_ref, turned_ref, far_ref, q_ref, top_ref, total_ref, acc_ref):
    half = COARSE_ROWS // 2
    low_lanes = lax.broadcasted_iota(jnp.int32, (1, 128), 1) < 64
    row = lax.broadcasted_iota(jnp.int32, (256, 256), 0)
    col = lax.broadcasted_iota(jnp.int32, (256, 256), 1)
    for z in range(4):
        packed = turned_ref[z, COARSE_ROWS:, :].astype(f32)
        zero = jnp.zeros_like(packed)
        q_ref[z * 256 : z * 256 + half, :] = jnp.where(low_lanes, packed, zero).astype(bf16)
        q_ref[z * 256 + half : (z + 1) * 256, :] = jnp.where(
            low_lanes, pltpu.roll(packed, 64, 1), zero
        ).astype(bf16)
        kv = turned_ref[z, :COARSE_ROWS, :]
        at = pl.ds(z * 256, 256)
        scores = jnp.where(col <= row, dot_t(q_ref[at, :], kv), masked_low)
        top = jnp.max(scores, axis=1, keepdims=True)
        contrib = dot(jnp.exp2(scores - top).astype(bf16), with_ones(kv))
        top_ref[at, :] = jnp.broadcast_to(top, (256, 128))
        total_ref[at, :] = contrib[:, 128:]
        acc_ref[at, :] = contrib[:, :128]
    state = (q_ref, top_ref, total_ref, acc_ref)
    for z in range(3):
        absorb(
            *state, (z + 1) * 256, (3 - z) * 256, [turned_ref[z, :COARSE_ROWS, :], far_ref[z]]
        )

    @pl.when(flag_ref[0] > 0)
    def _():
        for z in range(4):
            absorb(*state, z * 256, 256, [far_ref[z]])


def coarse_more_kernel(which, last, flag_ref, *refs):
    count = 2 * len(which)
    chunks = refs[:count]
    q_ref, top_in, total_in, acc_in = refs[count : count + 4]
    out_ref = refs[count + 4] if last else None
    top_ref, total_ref, acc_ref = refs[-3:]
    top_ref[...] = top_in[...]
    total_ref[...] = total_in[...]
    acc_ref[...] = acc_in[...]
    state = (q_ref, top_ref, total_ref, acc_ref)
    for n, s in enumerate(which):
        near, far = chunks[2 * n], chunks[2 * n + 1]
        for z in range(3):
            absorb(*state, (z + 1) * 256, (3 - z) * 256, [near[z], far[z]])

        @pl.when(flag_ref[s] > 0)
        def _(near=near, far=far):
            for z in range(4):
                absorb(*state, z * 256, 256, [near[z], far[z]])

    if last:
        mixed = acc_ref[...] / total_ref[...]
        low_lanes = lax.broadcasted_iota(jnp.int32, (1, 128), 1) < 64
        for z in range(4):
            upper = pltpu.roll(mixed[z * 256 : z * 256 + 128], 64, 1)
            lower = mixed[z * 256 + 128 : (z + 1) * 256]
            block = jnp.where(low_lanes, upper, lower).astype(bf16)
            for y in range(4):
                out_ref[z * 4 + y] = block


def feed_kernel(
    where_ref, heads_ref, short_ref, gain_ref, own, mine, other, up_hbm, down_hbm,
    part_ref, first_ref, mixed_ref, all_ref, co_ref, up_ref, down_ref, sems,
):
    head = where_ref[1]
    pairs = place_copies(head, where_ref[2], own, mine, other, co_ref)
    for w, w_ref in ((up_hbm, up_ref), (down_hbm, down_ref)):
        for part in range(4):
            at = pl.ds(part * 256, 256)
            pairs.append((w.at[at], w_ref.at[at]))
    copies = begin_copies(pairs, sems)
    low_lanes = lax.broadcasted_iota(jnp.int32, (1, 128), 1) < 64
    for y in range(4):
        for pair in range(2):
            even = heads_ref[2 * pair * 4 + y].astype(f32)
            odd = heads_ref[(2 * pair + 1) * 4 + y].astype(f32)
            at = slice(y * 256 + pair * 128, y * 256 + (pair + 1) * 128)
            mixed_ref[0:128, at] = jnp.where(low_lanes, even, pltpu.roll(odd, 64, 1)).astype(bf16)
            mixed_ref[128:256, at] = jnp.where(low_lanes, pltpu.roll(even, 64, 1), odd).astype(bf16)
    finish_copies(copies[:7])
    first = short_ref[...].astype(f32) + dot(mixed_ref[...], co_ref[...])
    all_ref[...] = first
    first_ref[...] = all_ref[pl.ds(pl.multiple_of(head * 64, 64), 64), :]
    feed = norm_rows(first, gain_ref[...])
    finish_copies(copies[7:])
    inner = jax.nn.gelu(dot(feed, up_ref[...])).astype(bf16)
    part_ref[...] = dot(inner, down_ref[...]).astype(bf16).reshape(4, 64, D)


def final_kernel(where_ref, s0, s1, s2, s3, b0, b1, b2, b3, up_ref, out_ref):
    head = where_ref[1]
    rows = 256 + HALO
    second = jnp.concatenate([ref[...] for ref in (s0, s1, s2, s3)], axis=0)
    lifted = dot(second, up_ref[...])
    index = lax.broadcasted_iota(jnp.int32, (256, rows), 0)
    column = lax.broadcasted_iota(jnp.int32, (256, rows), 1)
    r, m = index // 64, index % 64
    source = jnp.where(r == 0, 192 + m, jnp.where(m == 63, 268 + r, (r - 1) * 64 + m + 1))
    choose = (source == column).astype(f32).astype(bf16)
    index = lax.broadcasted_iota(jnp.int32, (256, 256), 0)
    column = lax.broadcasted_iota(jnp.int32, (256, 256), 1)
    weave = ((index % 4) * 64 + index // 4 == column).astype(f32).astype(bf16)
    for s, block in enumerate((b0, b1, b2, b3)):
        mine = lifted[s * 64 : (s + 1) * 64]
        raised = jnp.concatenate([mine[:, q * SHARE : (q + 1) * SHARE] for q in range(4)], axis=0)
        value = (dot(choose, block[...]) + raised).astype(bf16)
        begin = pl.multiple_of(lax.rem(head - s + 4, 4) * 256, 256)
        out_ref[pl.ds(begin, 256), :] = dot(weave, value).astype(bf16)


def fetch_half(weight, core):
    half = lax.dynamic_slice_in_dim(weight, core * 128, 128, 0)
    return [shift(half, "head", s, 4) for s in range(1, 4)]


def place_copies(head, core, own, mine, other, target):
    pairs = [(own, target.at[pl.ds(pl.multiple_of(head * 256, 256), 256)])]
    for s in range(1, 4):
        source = lax.rem(head - s + 4, 4) * 256
        at = pl.multiple_of(source + core * 128, 128)
        pairs.append((mine.at[s - 1], target.at[pl.ds(at, 128)]))
        at = pl.multiple_of(source + 128 - core * 128, 128)
        pairs.append((other.at[s - 1], target.at[pl.ds(at, 128)]))
    return pairs


def after(value, gate):
    return lax.optimization_barrier((value, gate))


def local(
    token_ids, embedding, fine_norm, fine_query, fine_key, fine_value, fine_output,
    shorten_weight, coarse_norm, coarse_query, coarse_key, coarse_value, coarse_output,
    ffn_norm, ffn_up, ffn_down, upsample_weight,
):
    place = lax.axis_index(SEQ).astype(jnp.int32)
    head = lax.axis_index("head").astype(jnp.int32)
    x_place = lax.axis_index("x").astype(jnp.int32)
    core = lax.axis_index("core").astype(jnp.int32)
    tables = jnp.asarray(angle_tables())
    where = jnp.stack([place, head, core])

    prior = later(token_ids, SEQ, 1, 32)
    last_ids = token_ids[ROWS - HALO :]
    before = later(last_ids, SEQ, 2, 32)
    tab = call(
        fine_tables_kernel, "fine_tables", pltpu.HBM((5, 256, SHARE), bf16), [], [],
        [
            pltpu.VMEM((5, 256, SHARE), bf16),
            pltpu.VMEM((1, D), f32), pltpu.VMEM((256, D), bf16),
            pltpu.VMEM((3, D, SHARE), bf16), pltpu.SemaphoreType.DMA((9,)),
        ],
        us=3, out_hbm=True, hbm=[fine_norm[None], embedding, fine_query, fine_key, fine_value],
    )
    fine_output_held, _ = after(fine_output, last_ids)
    out_mine = fetch_half(fine_output_held, core)
    rows = 256 + HALO
    mixed = call(
        fine_kernel, "fine_attention", jax.ShapeDtypeStruct((4, rows, SHARE), bf16),
        [where], [before[:, None], prior[:, None], token_ids[:, None]],
        [
            pltpu.VMEM((BLOCK + ROWS, SHARE), bf16),
            pltpu.VMEM((KEYS, SHARE), bf16), pltpu.VMEM((KEYS, SHARE), bf16),
            pltpu.VMEM((5, 256, SHARE), bf16), pltpu.VMEM((576, 128), f32),
            pltpu.SemaphoreType.DMA((10,)),
        ],
        grid=(4,), us=12, limit=24, hbm=[tab, tables],
    )

    out_mine, mixed = after(out_mine, mixed)
    got = lax.all_to_all(mixed, "head", 0, 0)
    out_other = [shift(part, "core", 1, 2) for part in out_mine]
    own_ids = lax.dynamic_slice_in_dim(
        jnp.concatenate([prior[ROWS - HALO :], token_ids]), head * 256, rows, 0
    )
    sends, shorten_near = call(
        fine_rows_kernel, "fine_rows",
        [
            jax.ShapeDtypeStruct((4, rows, SHARE), bf16),
            jax.ShapeDtypeStruct((SHORTEN, SHARE, D), bf16),
        ],
        [where],
        [own_ids[:, None], embedding, got, fine_output, *out_mine, *out_other],
        [pltpu.SemaphoreType.DMA((4,))], hbm=[shorten_weight],
    )
    blocks = exchange(lambda d: lax.dynamic_index_in_dim(sends, d, 0, keepdims=False), "head", 4)

    terms = []
    for s, block in enumerate(blocks):
        part = call(
            short_part_kernel, "short_part", jax.ShapeDtypeStruct((64, D), bf16), [],
            [block, shorten_near],
        )
        terms.append(part if s == 0 else shift(part, "head", 4 - s, 4))
    short_own = sum(t.astype(f32) for t in terms).astype(bf16)
    shorts = [short_own] + [shift(short_own, "head", s, 4) for s in range(1, 4)]
    packed, short = call(
        coarse_pack_kernel, "coarse_pack",
        [
            jax.ShapeDtypeStruct((4, COARSE_ROWS * 3 // 2, 128), bf16),
            jax.ShapeDtypeStruct((COARSE_ROWS, D), bf16),
        ],
        [where],
        [*shorts, coarse_norm[None], coarse_query, coarse_key, coarse_value, tables],
    )

    turned = lax.all_to_all(packed, "z", 0, 0)
    coarse_output_held, turned = after(coarse_output, turned)
    co_mine = fetch_half(coarse_output_held, core)
    kv = turned[:, :COARSE_ROWS]
    far = [shift(kv, "core", 1, 2)]
    near = [shift(kv, "x", s, 4) for s in range(1, 4)]
    steps = jnp.arange(4, dtype=jnp.int32)
    flags = ((x_place - steps + 4) % 4 < x_place).astype(jnp.int32) + (steps == 0) * core
    wide = jax.ShapeDtypeStruct((1024, 128), f32)
    q_all, *sums = call(
        coarse_first_kernel, "coarse_first",
        [jax.ShapeDtypeStruct((1024, 128), bf16), wide, wide, wide], [flags], [turned, far[0]],
        us=3, limit=24,
    )
    near_held, q_all = after(near, q_all)
    far += [shift(part, "core", 1, 2) for part in near_held]
    sums = call(
        functools.partial(coarse_more_kernel, (1, 3), False), "coarse_more", [wide] * 3,
        [flags], [near[0], far[1], near[2], far[3], q_all, *sums], us=6, limit=24,
    )
    wide_sends = call(
        functools.partial(coarse_more_kernel, (2,), True), "coarse_last",
        jax.ShapeDtypeStruct((16, 128, 128), bf16),
        [flags], [near[1], far[2], q_all, *sums], [pltpu.VMEM((1024, 128), f32)] * 3, us=3, limit=24,
    )
    co_mine, wide_sends = after(co_mine, wide_sends)
    co_mine = jnp.stack(co_mine)
    co_other = shift(co_mine, "core", 1, 2)

    heads_in = lax.all_to_all(wide_sends, ("z", "head"), 0, 0)
    parts, first_own = call(
        feed_kernel, "feed",
        [jax.ShapeDtypeStruct((4, 64, D), bf16), jax.ShapeDtypeStruct((64, D), f32)],
        [where],
        [heads_in, short, ffn_norm[None]],
        [
            pltpu.VMEM((COARSE_ROWS, D), bf16), pltpu.VMEM((COARSE_ROWS, D), f32),
            *[pltpu.VMEM((D, D), bf16)] * 3, pltpu.SemaphoreType.DMA((15,)),
        ],
        hbm=[coarse_output, co_mine, co_other, ffn_up, ffn_down], us=4, limit=24,
    )
    sums = exchange(lambda d: lax.dynamic_index_in_dim(parts, d, 0, keepdims=False), "head", 4)
    second_own = (first_own + sum(t.astype(f32) for t in sums)).astype(bf16)
    seconds = [second_own] + [shift(second_own, "head", s, 4) for s in range(1, 4)]
    return call(
        final_kernel, "final", jax.ShapeDtypeStruct((ROWS, SHARE), bf16),
        [where], [*seconds, *blocks, upsample_weight.reshape(D, SHORTEN * SHARE)],
    )


def solution(mesh):
    split = Mesh(mesh.devices.reshape(4, 4, 2, 4), ("z", "x", "core", "head"))
    return jax.shard_map(
        local,
        mesh=split,
        in_specs=(
            P(SEQ), P(), P(), P(None, "head"), P(None, "head"), P(None, "head"), P("head", None),
            P(None, "head", None), P(), P(None, "head"), P(None, "head"), P(None, "head"),
            P("head", None), P(), P(None, "head"), P("head", None), P(None, None, "head"),
        ),
        out_specs=P(SEQ, "head"),
        check_vma=False,
    )
```

```python
import functools
import math

import jax
import jax.numpy as jnp
import numpy as np
from jax import lax
from jax.experimental import pallas as pl
from jax.experimental.pallas import tpu as pltpu
from jax.sharding import Mesh
from jax.sharding import PartitionSpec as P

D = 1024
HEAD_DIM = 64
SHORTEN = 4
WINDOW = 1024
BLOCK = 256
HALO = 16
ROWS = 1024
PAST = WINDOW + BLOCK
KEYS = PAST + ROWS
SHARE = 256
COARSE_ROWS = 256
SEQ = ("z", "x", "core")

epsilon = 1e-06
masked_low = -1e30
q_scale = HEAD_DIM ** (-0.5) * math.log2(math.e)
bf16 = jnp.bfloat16
f32 = jnp.float32


def angle_tables():
    lane = np.arange(128) % 32
    period = 2.0 ** (4 + lane * 14 // 32)
    coarse = (256.0 * np.arange(32)[:, None]) % period[None]
    near = np.arange(256)[:, None] % period[None]
    a = coarse * (2.0 * np.pi / period)[None]
    b = near * (2.0 * np.pi / period)[None]
    parts = [np.cos(a), np.sin(a), np.cos(b), np.sin(b)]
    return np.concatenate(parts, axis=0).astype(np.float32)


def shift(value, axis, steps, count):
    return lax.ppermute(value, axis, [(i, (i + steps) % count) for i in range(count)])


def later(value, axis, steps, count):
    return lax.ppermute(value, axis, [(i, i + steps) for i in range(count - steps)])


def exchange(block_for, axis, count):
    me = lax.axis_index(axis)
    got = [block_for(me)]
    for s in range(1, count):
        got.append(shift(block_for((me + s) % count), axis, s, count))
    return got


def dot(left, right):
    return jnp.dot(left, right, preferred_element_type=f32)


def dot_t(left, right):
    return lax.dot_general(left, right, (((1,), (1,)), ((), ())), preferred_element_type=f32)


def norm_rows(data, gain):
    power = jnp.mean(data * data, axis=-1, keepdims=True)
    return (data * lax.rsqrt(power + epsilon) * gain).astype(bf16)


def partner(values):
    width = values.shape[1]
    lane = lax.broadcasted_iota(jnp.int32, values.shape, 1)
    ahead = pltpu.roll(values, width - 32, 1)
    behind = pltpu.roll(values, 32, 1)
    return jnp.where(lane % 64 < 32, -ahead, behind)


def halves(table):
    high = table.astype(bf16)
    low = (table - high.astype(f32)).astype(bf16)
    return high, low


def turn_tables(turn_ref, far):
    ca = turn_ref[pl.ds(far, 1), :]
    sa = turn_ref[pl.ds(32 + far, 1), :]
    cb = turn_ref[64:320, :]
    sb = turn_ref[320:576, :]
    cosine = ca * cb - sa * sb
    sine = sa * cb + ca * sb
    return jnp.concatenate([cosine, cosine], axis=1), jnp.concatenate([sine, sine], axis=1)


def pick(ids, levels=256):
    columns = lax.broadcasted_iota(jnp.int32, (ids.shape[0], levels), 1)
    return (ids == columns).astype(f32).astype(bf16)


def turned_rows(hot, tab_ref, n, cosine, sine):
    return (dot(hot, tab_ref[n]) * cosine + dot(hot, tab_ref[n + 1]) * sine).astype(bf16)


def fine_tables_kernel(gain_hbm, emb_hbm, wq_hbm, wk_hbm, wv_hbm, tab_hbm, tab_ref, gain_ref, emb_ref, w_ref, sems):
    pairs = [(emb_hbm, emb_ref), (gain_hbm, gain_ref)]
    for n, w in enumerate((wq_hbm, wk_hbm, wv_hbm)):
        for part in range(2):
            rows = pl.ds(part * 512, 512)
            pairs.append((w.at[rows], w_ref.at[n, rows]))
    copies = begin_copies(pairs, sems)
    finish_copies(copies[:2])
    fine_in = norm_rows(emb_ref[...].astype(f32), gain_ref[...])
    finish_copies(copies[2:])
    tq = dot(fine_in, w_ref[0]) * q_scale
    tk = dot(fine_in, w_ref[1])
    tables = (tq, partner(tq), tk, partner(tk), dot(fine_in, w_ref[2]))
    for n, table in enumerate(tables):
        tab_ref[n] = table.astype(bf16)
    finish_copies(begin_copies([(tab_ref.at[n], tab_hbm.at[n]) for n in range(5)], sems))


def fine_kernel(
    where_ref, before_ref, prior_ref, own_ref, tab_hbm, turn_hbm,
    out_ref, q_ref, k_ref, v_ref, tab_ref, turn_ref, sems,
):
    step = pl.program_id(0)
    lowest = jnp.maximum(PAST - where_ref[0] * ROWS, 0)
    head_lane = lax.broadcasted_iota(jnp.int32, (1, SHARE), 1) // HEAD_DIM

    @pl.when(step == 0)
    def _():
        pairs = [(tab_hbm.at[n], tab_ref.at[n]) for n in range(5)] + [(turn_hbm, turn_ref)]
        finish_copies(begin_copies(pairs, sems))
        cosine, sine = turn_tables(turn_ref, 0)
        oldest = pick(before_ref[...])
        at = slice(BLOCK - HALO, BLOCK)
        k_ref[at, :] = turned_rows(oldest, tab_ref, 2, cosine[at], sine[at])
        v_ref[at, :] = dot(oldest, tab_ref[4]).astype(bf16)

        def build(block, ids, with_q):
            begin = pl.multiple_of(block * BLOCK, BLOCK)
            hot = pick(ids)
            cosine, sine = turn_tables(turn_ref, block)
            k_ref[pl.ds(begin, BLOCK), :] = turned_rows(hot, tab_ref, 2, cosine, sine)
            v_ref[pl.ds(begin, BLOCK), :] = dot(hot, tab_ref[4]).astype(bf16)
            if with_q:
                at = pl.multiple_of(begin - (PAST - BLOCK), BLOCK)
                q_ref[pl.ds(at, BLOCK), :] = turned_rows(hot, tab_ref, 0, cosine, sine)

        def build_from(ref, first, with_q):
            def body(n, _):
                ids = ref[pl.ds(pl.multiple_of(n * BLOCK, BLOCK), BLOCK), :]
                build(first + n, ids, with_q)
                return 0

            return body

        lax.fori_loop(0, 3, build_from(prior_ref, 1, False), 0)
        build(4, prior_ref[3 * BLOCK :, :], True)
        lax.fori_loop(0, 4, build_from(own_ref, 5, True), 0)
        halo_q = q_ref[BLOCK - HALO : BLOCK, :]
        stacked = jnp.concatenate(
            [jnp.where(head_lane == h, halo_q, jnp.zeros_like(halo_q)) for h in range(4)], axis=0
        )
        scores = dot_t(stacked, k_ref[BLOCK - HALO : PAST, :])
        row = lax.broadcasted_iota(jnp.int32, scores.shape, 0) % HALO + (PAST - HALO)
        col = lax.broadcasted_iota(jnp.int32, scores.shape, 1) + (BLOCK - HALO)
        allowed = (col <= row) & (col > row - WINDOW) & (col >= lowest)
        scores = jnp.where(allowed, scores, masked_low)
        top = jnp.max(scores, axis=1, keepdims=True)
        weights = jnp.exp2(scores - top)
        total = jnp.sum(weights, axis=1, keepdims=True)
        mixed = dot(weights.astype(bf16), v_ref[BLOCK - HALO : PAST, :]) / total
        result = jnp.zeros((HALO, SHARE), f32)
        for h in range(4):
            result = jnp.where(head_lane == h, mixed[h * HALO : (h + 1) * HALO], result)
        out_ref[0, 0:HALO, :] = result.astype(bf16)

    begin = pl.multiple_of((step + 1) * BLOCK, BLOCK)
    keys = k_ref[pl.ds(begin, PAST), :]
    values = v_ref[pl.ds(begin, PAST), :]
    query = q_ref[pl.ds(begin, BLOCK), :]
    row = lax.broadcasted_iota(jnp.int32, (BLOCK, BLOCK), 0)
    col = lax.broadcasted_iota(jnp.int32, (BLOCK, BLOCK), 1)
    biases = [
        jnp.where(begin + t * BLOCK >= lowest, 0.0, masked_low).astype(f32) for t in range(4)
    ]
    first_bias = jnp.where(col > row, 0.0, masked_low) + biases[0]
    last_bias = jnp.where(col <= row, 0.0, masked_low)
    ones = jnp.ones((PAST, 128), bf16)
    low_lanes = lax.broadcasted_iota(jnp.int32, (1, 128), 1) < 64
    results = []

    def score(h):
        return dot_t(jnp.where(head_lane == h, query, jnp.zeros_like(query)), keys)

    ahead = score(0)
    for h in range(4):
        scores = ahead
        if h < 3:
            ahead = score(h + 1)
        tiles = [scores[:, t * BLOCK : (t + 1) * BLOCK] for t in range(5)]
        tiles = (
            [tiles[0] + first_bias]
            + [tiles[t] + biases[t] for t in range(1, 4)]
            + [tiles[4] + last_bias]
        )
        peak = tiles[0]
        for t in range(1, 5):
            peak = jnp.maximum(peak, tiles[t])
        top = jnp.max(peak, axis=1, keepdims=True)
        weights = [jnp.exp2(tile - top).astype(bf16) for tile in tiles]
        pair = (h // 2) * 128
        wide = jnp.concatenate([values[:, pair : pair + 128], ones], axis=1)
        mixed = dot(jnp.concatenate(weights, axis=1), wide)
        results.append(mixed[:, :128] / mixed[:, 128:])
    result = jnp.concatenate(
        [jnp.where(low_lanes, results[2 * n], results[2 * n + 1]) for n in range(2)], axis=1
    )
    result = result.astype(bf16)
    out_ref[step, HALO:, :] = result

    @pl.when(step < 3)
    def _():
        out_ref[step + 1, 0:HALO, :] = result[BLOCK - HALO :]


def vmem():
    return pl.BlockSpec(memory_space=pltpu.VMEM)


def smem():
    return pl.BlockSpec(memory_space=pltpu.SMEM)


def space(shape):
    plain = isinstance(shape, jax.ShapeDtypeStruct)
    return vmem() if plain else pl.BlockSpec(memory_space=pltpu.HBM)


def call(kernel, name, shapes, scalars, arrays, scratch=(), grid=None, limit=16, us=2, hbm=(), free=()):
    one = not isinstance(shapes, (list, tuple))
    extra = {} if grid is None else {"grid": grid}
    return pl.pallas_call(
        kernel,
        out_shape=shapes,
        in_specs=[smem()] * len(scalars)
        + [vmem()] * len(arrays)
        + [pl.BlockSpec(memory_space=pltpu.HBM)] * len(hbm)
        + [pl.BlockSpec(memory_space=pl.ANY)] * len(free),
        out_specs=space(shapes) if one else [space(shape) for shape in shapes],
        scratch_shapes=list(scratch),
        compiler_params=pltpu.CompilerParams(vmem_limit_bytes=limit << 20),
        cost_estimate=pl.CostEstimate(
            flops=us * 10**9, transcendentals=0, bytes_accessed=us * 2 * 10**6
        ),
        name=name,
        **extra,
    )(*scalars, *arrays, *(pltpu.with_memory_space_constraint(a, pltpu.HBM) for a in hbm), *free)


def begin_copies(pairs, sems):
    copies = [pltpu.make_async_copy(a, b, sems.at[n]) for n, (a, b) in enumerate(pairs)]
    for copy in copies:
        copy.start()
    return copies


def finish_copies(copies):
    for copy in copies:
        copy.wait()


def fine_rows_kernel(
    where_ref, ids_ref, emb_ref, got_ref, own_ref, m1, m2, t1, t2, w_hbm,
    out_ref, w_ref, sems,
):
    place, head, core = where_ref[0], where_ref[1], where_ref[2]
    copies = begin_copies([(w_hbm.at[n], w_ref.at[n]) for n in range(4)], sems)
    merged = dot(pick(ids_ref[...]), emb_ref[...]) + dot(got_ref[head], own_ref[...])
    near, far, apart = sources(head, core)
    merged += dot(got_ref[near], m1[...]) + dot(got_ref[far], t1[...])
    at = pl.ds(pl.multiple_of(core * 128, 128), 128)
    merged += dot(got_ref[apart, :, at], m2[...])
    at = pl.ds(pl.multiple_of(128 - core * 128, 128), 128)
    merged += dot(got_ref[apart, :, at], t2[...])
    rows = 256 + HALO
    token = (
        place * ROWS + head * 256 - HALO + lax.broadcasted_iota(jnp.int32, (rows, D), 0)
    )
    fine = jnp.where(token >= 0, merged, 0.0).astype(bf16)
    index = lax.broadcasted_iota(jnp.int32, (256, rows), 0)
    column = lax.broadcasted_iota(jnp.int32, (256, rows), 1)
    source = 4 * (index % 64) + index // 64 + (HALO - 3)
    choose = (source == column).astype(f32).astype(bf16)
    grouped = dot(choose, fine).astype(bf16)
    for d in range(4):
        out_ref[d, 0:256, :] = grouped[:, d * SHARE : (d + 1) * SHARE]
        out_ref[d, 256:rows, :] = fine[256:rows, d * SHARE : (d + 1) * SHARE]
    finish_copies(copies)


def short_part_kernel(group_ref, w_ref, out_ref):
    total = dot(group_ref[0:64, :], w_ref[0])
    for r in range(1, SHORTEN):
        total += dot(group_ref[r * 64 : (r + 1) * 64, :], w_ref[r])
    out_ref[...] = total.astype(bf16)


def coarse_pack_kernel(
    where_ref, s0, s1, s2, s3, gain_ref, wq_ref, wk_ref, wv_ref, turn_ref,
    out_ref, short_ref,
):
    place, head = where_ref[0], where_ref[1]
    for s, ref in enumerate((s0, s1, s2, s3)):
        begin = pl.multiple_of(lax.rem(head - s + 4, 4) * 64, 64)
        short_ref[pl.ds(begin, 64), :] = ref[...]
    x = norm_rows(short_ref[...].astype(f32), gain_ref[...])
    cosine, sine = turn_tables(turn_ref, place)

    def turned(values):
        return values * cosine + partner(values) * sine

    q = turned(dot(x, wq_ref[...])) * q_scale
    k = turned(dot(x, wk_ref[...]))
    v = dot(x, wv_ref[...])
    low_lanes = lax.broadcasted_iota(jnp.int32, (1, 128), 1) < 64
    half = COARSE_ROWS // 2
    for h in range(4):
        pair = (h // 2) * 128
        kp = k[:, pair : pair + 128]
        vp = v[:, pair : pair + 128]
        qp = q[:, pair : pair + 128]
        if h % 2 == 0:
            kv = jnp.where(low_lanes, kp, pltpu.roll(vp, 64, 1))
            qq = jnp.where(low_lanes, qp[:half], pltpu.roll(qp[half:], 64, 1))
        else:
            kv = jnp.where(low_lanes, pltpu.roll(kp, 64, 1), vp)
            qq = jnp.where(low_lanes, pltpu.roll(qp[:half], 64, 1), qp[half:])
        out_ref[h, 0:COARSE_ROWS, :] = kv.astype(bf16)
        out_ref[h, COARSE_ROWS : COARSE_ROWS + half, :] = qq.astype(bf16)


def with_ones(kv):
    return jnp.concatenate([kv, jnp.ones((kv.shape[0], 128), bf16)], axis=1)


def absorb(q_ref, top_ref, total_ref, acc_ref, begin, rows, parts):
    at = pl.ds(begin, rows)
    query = q_ref[at, :]
    scores = [dot_t(query, kv) for kv in parts]
    peak = scores[0]
    for s in scores[1:]:
        peak = jnp.maximum(peak, s)
    old = top_ref[at, :]
    top = jnp.maximum(old, jnp.max(peak, axis=1, keepdims=True))
    factor = jnp.exp2(old - top)
    both = jnp.concatenate([top, top], axis=1)
    contrib = dot(jnp.exp2(scores[0] - both).astype(bf16), with_ones(parts[0]))
    for s, kv in zip(scores[1:], parts[1:]):
        contrib = contrib + dot(jnp.exp2(s - both).astype(bf16), with_ones(kv))
    top_ref[at, :] = top
    total_ref[at, :] = total_ref[at, :] * factor + contrib[:, 128:]
    acc_ref[at, :] = acc_ref[at, :] * factor + contrib[:, :128]


def coarse_first_kernel(flag_ref, turned_ref, far_ref, q_ref, top_ref, total_ref, acc_ref):
    half = COARSE_ROWS // 2
    low_lanes = lax.broadcasted_iota(jnp.int32, (1, 128), 1) < 64
    row = lax.broadcasted_iota(jnp.int32, (256, 256), 0)
    col = lax.broadcasted_iota(jnp.int32, (256, 256), 1)
    for z in range(4):
        packed = turned_ref[z, COARSE_ROWS:, :].astype(f32)
        zero = jnp.zeros_like(packed)
        q_ref[z * 256 : z * 256 + half, :] = jnp.where(low_lanes, packed, zero).astype(bf16)
        q_ref[z * 256 + half : (z + 1) * 256, :] = jnp.where(
            low_lanes, pltpu.roll(packed, 64, 1), zero
        ).astype(bf16)
        kv = turned_ref[z, :COARSE_ROWS, :]
        at = pl.ds(z * 256, 256)
        scores = jnp.where(col <= row, dot_t(q_ref[at, :], kv), masked_low)
        top = jnp.max(scores, axis=1, keepdims=True)
        contrib = dot(jnp.exp2(scores - top).astype(bf16), with_ones(kv))
        top_ref[at, :] = jnp.broadcast_to(top, (256, 128))
        total_ref[at, :] = contrib[:, 128:]
        acc_ref[at, :] = contrib[:, :128]
    state = (q_ref, top_ref, total_ref, acc_ref)
    for z in range(3):
        absorb(
            *state, (z + 1) * 256, (3 - z) * 256, [turned_ref[z, :COARSE_ROWS, :], far_ref[z]]
        )

    @pl.when(flag_ref[0] > 0)
    def _():
        for z in range(4):
            absorb(*state, z * 256, 256, [far_ref[z]])


def coarse_more_kernel(which, last, flag_ref, *refs):
    count = 2 * len(which)
    sems = refs[-1]
    refs = refs[:-1]
    chunks = refs[:count]
    q_ref, top_in, total_in, acc_in = refs[count : count + 4]
    refs = refs[count + 4 :]
    top_ref, total_ref, acc_ref = refs[-3:]
    if last:
        own, m1, m2, t1, t2, target, out_ref = refs[:-3]
        pairs = place_copies(flag_ref[4], flag_ref[5], own, (m1, m2), (t1, t2), target)
    else:
        pairs = []
        for a, b in zip(refs[:2], refs[2:4]):
            for part in range(4):
                at = pl.ds(part * 256, 256)
                pairs.append((a.at[at], b.at[at]))
    copies = begin_copies(pairs, sems)
    top_ref[...] = top_in[...]
    total_ref[...] = total_in[...]
    acc_ref[...] = acc_in[...]
    state = (q_ref, top_ref, total_ref, acc_ref)
    for n, s in enumerate(which):
        near, far = chunks[2 * n], chunks[2 * n + 1]
        for z in range(3):
            absorb(*state, (z + 1) * 256, (3 - z) * 256, [near[z], far[z]])

        @pl.when(flag_ref[s] > 0)
        def _(near=near, far=far):
            for z in range(4):
                absorb(*state, z * 256, 256, [near[z], far[z]])

    if last:
        mixed = acc_ref[...] / total_ref[...]
        low_lanes = lax.broadcasted_iota(jnp.int32, (1, 128), 1) < 64
        for z in range(4):
            upper = pltpu.roll(mixed[z * 256 : z * 256 + 128], 64, 1)
            lower = mixed[z * 256 + 128 : (z + 1) * 256]
            block = jnp.where(low_lanes, upper, lower).astype(bf16)
            for y in range(4):
                out_ref[z * 4 + y] = block
    finish_copies(copies)


def feed_kernel(
    where_ref, heads_ref, short_ref, gain_ref, co_ref, up_ref, down_ref,
    part_ref, first_ref, mixed_ref, all_ref,
):
    head = where_ref[1]
    low_lanes = lax.broadcasted_iota(jnp.int32, (1, 128), 1) < 64
    for y in range(4):
        for pair in range(2):
            even = heads_ref[2 * pair * 4 + y].astype(f32)
            odd = heads_ref[(2 * pair + 1) * 4 + y].astype(f32)
            at = slice(y * 256 + pair * 128, y * 256 + (pair + 1) * 128)
            mixed_ref[0:128, at] = jnp.where(low_lanes, even, pltpu.roll(odd, 64, 1)).astype(bf16)
            mixed_ref[128:256, at] = jnp.where(low_lanes, pltpu.roll(even, 64, 1), odd).astype(bf16)
    first = short_ref[...].astype(f32) + dot(mixed_ref[...], co_ref[...])
    all_ref[...] = first
    first_ref[...] = all_ref[pl.ds(pl.multiple_of(head * 64, 64), 64), :]
    feed = norm_rows(first, gain_ref[...])
    inner = jax.nn.gelu(dot(feed, up_ref[...])).astype(bf16)
    part_ref[...] = dot(inner, down_ref[...]).astype(bf16).reshape(4, 64, D)


def final_kernel(where_ref, s0, s1, s2, s3, b0, b1, b2, b3, up_ref, out_ref):
    head = where_ref[1]
    rows = 256 + HALO
    second = jnp.concatenate([ref[...] for ref in (s0, s1, s2, s3)], axis=0)
    lifted = dot(second, up_ref[...])
    index = lax.broadcasted_iota(jnp.int32, (256, rows), 0)
    column = lax.broadcasted_iota(jnp.int32, (256, rows), 1)
    r, m = index // 64, index % 64
    source = jnp.where(r == 0, 192 + m, jnp.where(m == 63, 268 + r, (r - 1) * 64 + m + 1))
    choose = (source == column).astype(f32).astype(bf16)
    index = lax.broadcasted_iota(jnp.int32, (256, 256), 0)
    column = lax.broadcasted_iota(jnp.int32, (256, 256), 1)
    weave = ((index % 4) * 64 + index // 4 == column).astype(f32).astype(bf16)
    for s, block in enumerate((b0, b1, b2, b3)):
        mine = lifted[s * 64 : (s + 1) * 64]
        raised = jnp.concatenate([mine[:, q * SHARE : (q + 1) * SHARE] for q in range(4)], axis=0)
        value = (dot(choose, block[...]) + raised).astype(bf16)
        begin = pl.multiple_of(lax.rem(head - s + 4, 4) * 256, 256)
        out_ref[pl.ds(begin, 256), :] = dot(weave, value).astype(bf16)


def fetch_rest(weight, core):
    pairs = []
    for c, step in ((0, 1), (1, 3)):
        pairs += [(4 * c + y, 4 * c + (y + step) % 4) for y in range(4)]
    whole = lax.ppermute(weight, ("core", "head"), pairs)
    half = shift(lax.dynamic_slice_in_dim(weight, core * 128, 128, 0), "head", 2, 4)
    return [whole, half]


def swap_cores(parts):
    return [shift(part, "core", 1, 2) for part in parts]


def sources(head, core):
    mine = lax.rem(head + 3 - 2 * core, 4)
    other = lax.rem(head + 1 + 2 * core, 4)
    return mine, other, lax.rem(head + 2, 4)


def place_copies(head, core, own, mine, other, target):
    near, far, apart = sources(head, core)
    halves_at = apart * 256
    return [
        (own, target.at[pl.ds(pl.multiple_of(head * 256, 256), 256)]),
        (mine[0], target.at[pl.ds(pl.multiple_of(near * 256, 256), 256)]),
        (other[0], target.at[pl.ds(pl.multiple_of(far * 256, 256), 256)]),
        (mine[1], target.at[pl.ds(pl.multiple_of(halves_at + core * 128, 128), 128)]),
        (other[1], target.at[pl.ds(pl.multiple_of(halves_at + 128 - core * 128, 128), 128)]),
    ]


def after(value, gate):
    return lax.optimization_barrier((value, gate))


def local(
    token_ids, embedding, fine_norm, fine_query, fine_key, fine_value, fine_output,
    shorten_weight, coarse_norm, coarse_query, coarse_key, coarse_value, coarse_output,
    ffn_norm, ffn_up, ffn_down, upsample_weight,
):
    place = lax.axis_index(SEQ).astype(jnp.int32)
    head = lax.axis_index("head").astype(jnp.int32)
    x_place = lax.axis_index("x").astype(jnp.int32)
    core = lax.axis_index("core").astype(jnp.int32)
    tables = jnp.asarray(angle_tables())
    where = jnp.stack([place, head, core])

    prior = later(token_ids, SEQ, 1, 32)
    before = later(token_ids, SEQ, 2, 32)[ROWS - HALO :]
    tab = call(
        fine_tables_kernel, "fine_tables", pltpu.HBM((5, 256, SHARE), bf16), [], [],
        [
            pltpu.VMEM((5, 256, SHARE), bf16),
            pltpu.VMEM((1, D), f32), pltpu.VMEM((256, D), bf16),
            pltpu.VMEM((3, D, SHARE), bf16), pltpu.SemaphoreType.DMA((9,)),
        ],
        us=3, hbm=[fine_norm[None], embedding, fine_query, fine_key, fine_value],
    )
    own_ids_column = token_ids[:, None]
    fine_output_held, own_ids_column = after(fine_output, own_ids_column)
    out_mine = fetch_rest(fine_output_held, core)
    rows = 256 + HALO
    mixed = call(
        fine_kernel, "fine_attention", jax.ShapeDtypeStruct((4, rows, SHARE), bf16),
        [where], [before[:, None], prior[:, None], own_ids_column],
        [
            pltpu.VMEM((BLOCK + ROWS, SHARE), bf16),
            pltpu.VMEM((KEYS, SHARE), bf16), pltpu.VMEM((KEYS, SHARE), bf16),
            pltpu.VMEM((5, 256, SHARE), bf16), pltpu.VMEM((576, 128), f32),
            pltpu.SemaphoreType.DMA((10,)),
        ],
        grid=(4,), us=12, limit=24, hbm=[tab, tables],
    )

    out_mine, mixed = after(out_mine, mixed)
    got = lax.all_to_all(mixed, "head", 0, 0)
    out_other = swap_cores(out_mine)
    own_ids = lax.dynamic_slice_in_dim(
        jnp.concatenate([prior[ROWS - HALO :], token_ids]), head * 256, rows, 0
    )
    sends, shorten_near = call(
        fine_rows_kernel, "fine_rows",
        [
            jax.ShapeDtypeStruct((4, rows, SHARE), bf16),
            jax.ShapeDtypeStruct((SHORTEN, SHARE, D), bf16),
        ],
        [where],
        [own_ids[:, None], embedding, got, fine_output, *out_mine, *out_other],
        [pltpu.SemaphoreType.DMA((4,))], hbm=[shorten_weight],
    )
    blocks = exchange(lambda d: lax.dynamic_index_in_dim(sends, d, 0, keepdims=False), "head", 4)

    terms = []
    for s, block in enumerate(blocks):
        part = call(
            short_part_kernel, "short_part", jax.ShapeDtypeStruct((64, D), bf16), [],
            [block, shorten_near],
        )
        terms.append(part if s == 0 else shift(part, "head", 4 - s, 4))
    short_own = sum(t.astype(f32) for t in terms).astype(bf16)
    shorts = [short_own] + [shift(short_own, "head", s, 4) for s in range(1, 4)]
    packed, short = call(
        coarse_pack_kernel, "coarse_pack",
        [
            jax.ShapeDtypeStruct((4, COARSE_ROWS * 3 // 2, 128), bf16),
            jax.ShapeDtypeStruct((COARSE_ROWS, D), bf16),
        ],
        [where],
        [*shorts, coarse_norm[None], coarse_query, coarse_key, coarse_value, tables],
    )

    coarse_output_held, packed = after(coarse_output, packed)
    co_mine = fetch_rest(coarse_output_held, core)
    turned = lax.all_to_all(packed, "z", 0, 0)
    kv = turned[:, :COARSE_ROWS]
    far = [shift(kv, "core", 1, 2)]
    near = [shift(kv, "x", s, 4) for s in range(1, 4)]
    steps = jnp.arange(4, dtype=jnp.int32)
    flags = ((x_place - steps + 4) % 4 < x_place).astype(jnp.int32) + (steps == 0) * core
    flags = jnp.concatenate([flags, where[1:]])
    wide = jax.ShapeDtypeStruct((1024, 128), f32)
    q_all, *sums = call(
        coarse_first_kernel, "coarse_first",
        [jax.ShapeDtypeStruct((1024, 128), bf16), wide, wide, wide], [flags], [turned, far[0]],
        us=3, limit=24,
    )
    near_held, co_held, q_all = lax.optimization_barrier((near, co_mine, q_all))
    far += [shift(part, "core", 1, 2) for part in near_held]
    co_other = swap_cores(co_held)
    square = jax.ShapeDtypeStruct((D, D), bf16)
    up_near, down_near, *sums = call(
        functools.partial(coarse_more_kernel, (1, 3), False), "coarse_more",
        [square, square, wide, wide, wide],
        [flags], [near[0], far[1], near[2], far[3], q_all, *sums],
        [pltpu.SemaphoreType.DMA((8,))], us=6, limit=24, hbm=[ffn_up, ffn_down],
    )
    output_near, wide_sends = call(
        functools.partial(coarse_more_kernel, (2,), True), "coarse_last",
        [square, jax.ShapeDtypeStruct((16, 128, 128), bf16)],
        [flags], [near[1], far[2], q_all, *sums],
        [pltpu.VMEM((1024, 128), f32)] * 3 + [pltpu.SemaphoreType.DMA((5,))],
        us=3, limit=24, hbm=[coarse_output], free=[*co_mine, *co_other],
    )

    heads_in = lax.all_to_all(wide_sends, ("z", "head"), 0, 0)
    parts, first_own = call(
        feed_kernel, "feed",
        [jax.ShapeDtypeStruct((4, 64, D), bf16), jax.ShapeDtypeStruct((64, D), f32)],
        [where],
        [heads_in, short, ffn_norm[None], output_near, up_near, down_near],
        [
            pltpu.VMEM((COARSE_ROWS, D), bf16), pltpu.VMEM((COARSE_ROWS, D), f32),
        ],
        us=4,
    )
    sums = exchange(lambda d: lax.dynamic_index_in_dim(parts, d, 0, keepdims=False), "head", 4)
    second_own = (first_own + sum(t.astype(f32) for t in sums)).astype(bf16)
    seconds = [second_own] + [shift(second_own, "head", s, 4) for s in range(1, 4)]
    return call(
        final_kernel, "final", jax.ShapeDtypeStruct((ROWS, SHARE), bf16),
        [where], [*seconds, *blocks, upsample_weight.reshape(D, SHORTEN * SHARE)],
    )


def solution(mesh):
    split = Mesh(mesh.devices.reshape(4, 4, 2, 4), ("z", "x", "core", "head"))
    return jax.shard_map(
        local,
        mesh=split,
        in_specs=(
            P(SEQ), P(), P(), P(None, "head"), P(None, "head"), P(None, "head"), P("head", None),
            P(None, "head", None), P(), P(None, "head"), P(None, "head"), P(None, "head"),
            P("head", None), P(), P(None, "head"), P("head", None), P(None, None, "head"),
        ),
        out_specs=P(SEQ, "head"),
        check_vma=False,
    )
```

```python
import functools
import math

import jax
import jax.numpy as jnp
import numpy as np
from jax import lax
from jax.experimental import pallas as pl
from jax.experimental.pallas import tpu as pltpu
from jax.sharding import Mesh
from jax.sharding import PartitionSpec as P

D = 1024
HEAD_DIM = 64
SHORTEN = 4
WINDOW = 1024
BLOCK = 256
HALO = 16
ROWS = 1024
PAST = WINDOW + BLOCK
KEYS = PAST + ROWS
SHARE = 256
COARSE_ROWS = 256
SEQ = ("z", "x", "core")

epsilon = 1e-06
masked_low = -1e30
q_scale = HEAD_DIM ** (-0.5) * math.log2(math.e)
bf16 = jnp.bfloat16
f32 = jnp.float32


def angle_tables():
    lane = np.arange(128) % 32
    period = 2.0 ** (4 + lane * 14 // 32)
    coarse = (256.0 * np.arange(32)[:, None]) % period[None]
    near = np.arange(256)[:, None] % period[None]
    a = coarse * (2.0 * np.pi / period)[None]
    b = near * (2.0 * np.pi / period)[None]
    parts = [np.cos(a), np.sin(a), np.cos(b), np.sin(b)]
    return np.concatenate(parts, axis=0).astype(np.float32)


def shift(value, axis, steps, count):
    return lax.ppermute(value, axis, [(i, (i + steps) % count) for i in range(count)])


def later(value, axis, steps, count):
    return lax.ppermute(value, axis, [(i, i + steps) for i in range(count - steps)])


def exchange(block_for, axis, count):
    me = lax.axis_index(axis)
    got = [block_for(me)]
    for s in range(1, count):
        got.append(shift(block_for((me + s) % count), axis, s, count))
    return got


def dot(left, right):
    return jnp.dot(left, right, preferred_element_type=f32)


def dot_t(left, right):
    return lax.dot_general(left, right, (((1,), (1,)), ((), ())), preferred_element_type=f32)


def norm_rows(data, gain):
    power = jnp.mean(data * data, axis=-1, keepdims=True)
    return (data * lax.rsqrt(power + epsilon) * gain).astype(bf16)


def partner(values):
    width = values.shape[1]
    lane = lax.broadcasted_iota(jnp.int32, values.shape, 1)
    ahead = pltpu.roll(values, width - 32, 1)
    behind = pltpu.roll(values, 32, 1)
    return jnp.where(lane % 64 < 32, -ahead, behind)


def halves(table):
    high = table.astype(bf16)
    low = (table - high.astype(f32)).astype(bf16)
    return high, low


def turn_tables(turn_ref, far):
    ca = turn_ref[pl.ds(far, 1), :]
    sa = turn_ref[pl.ds(32 + far, 1), :]
    cb = turn_ref[64:320, :]
    sb = turn_ref[320:576, :]
    cosine = ca * cb - sa * sb
    sine = sa * cb + ca * sb
    return jnp.concatenate([cosine, cosine], axis=1), jnp.concatenate([sine, sine], axis=1)


def pick(ids, levels=256):
    columns = lax.broadcasted_iota(jnp.int32, (ids.shape[0], levels), 1)
    return (ids == columns).astype(f32).astype(bf16)


def turned_rows(hot, tab_ref, n, cosine, sine):
    return (dot(hot, tab_ref[n]) * cosine + dot(hot, tab_ref[n + 1]) * sine).astype(bf16)


def fine_tables_kernel(gain_hbm, emb_hbm, wq_hbm, wk_hbm, wv_hbm, tab_hbm, tab_ref, gain_ref, emb_ref, w_ref, sems):
    pairs = [(emb_hbm, emb_ref), (gain_hbm, gain_ref)]
    for n, w in enumerate((wq_hbm, wk_hbm, wv_hbm)):
        for part in range(2):
            rows = pl.ds(part * 512, 512)
            pairs.append((w.at[rows], w_ref.at[n, rows]))
    copies = begin_copies(pairs, sems)
    finish_copies(copies[:2])
    fine_in = norm_rows(emb_ref[...].astype(f32), gain_ref[...])
    finish_copies(copies[2:])
    tq = dot(fine_in, w_ref[0]) * q_scale
    tk = dot(fine_in, w_ref[1])
    tables = (tq, partner(tq), tk, partner(tk), dot(fine_in, w_ref[2]))
    for n, table in enumerate(tables):
        tab_ref[n] = table.astype(bf16)
    finish_copies(begin_copies([(tab_ref.at[n], tab_hbm.at[n]) for n in range(5)], sems))


def fine_kernel(
    where_ref, before_ref, prior_ref, own_ref, tab_hbm, turn_hbm,
    o0, o1, o2, o3, q_ref, k_ref, v_ref, tab_ref, turn_ref, sems,
):
    step = pl.program_id(0)
    head = where_ref[1]
    quarter = lax.rem(head + step, 4)
    outs = (o0, o1, o2, o3)
    lowest = jnp.maximum(PAST - where_ref[0] * ROWS, 0)
    head_lane = lax.broadcasted_iota(jnp.int32, (1, SHARE), 1) // HEAD_DIM

    @pl.when(step == 0)
    def _():
        pairs = [(tab_hbm.at[n], tab_ref.at[n]) for n in range(5)] + [(turn_hbm, turn_ref)]
        finish_copies(begin_copies(pairs, sems))
        cosine, sine = turn_tables(turn_ref, 0)
        oldest = pick(before_ref[...])
        at = slice(BLOCK - HALO, BLOCK)
        k_ref[at, :] = turned_rows(oldest, tab_ref, 2, cosine[at], sine[at])
        v_ref[at, :] = dot(oldest, tab_ref[4]).astype(bf16)

        def build(block, ids, with_q):
            begin = pl.multiple_of(block * BLOCK, BLOCK)
            hot = pick(ids)
            cosine, sine = turn_tables(turn_ref, block)
            k_ref[pl.ds(begin, BLOCK), :] = turned_rows(hot, tab_ref, 2, cosine, sine)
            v_ref[pl.ds(begin, BLOCK), :] = dot(hot, tab_ref[4]).astype(bf16)
            if with_q:
                at = pl.multiple_of(begin - (PAST - BLOCK), BLOCK)
                q_ref[pl.ds(at, BLOCK), :] = turned_rows(hot, tab_ref, 0, cosine, sine)

        def build_from(ref, first, with_q):
            def body(n, _):
                ids = ref[pl.ds(pl.multiple_of(n * BLOCK, BLOCK), BLOCK), :]
                build(first + n, ids, with_q)
                return 0

            return body

        lax.fori_loop(0, 3, build_from(prior_ref, 1, False), 0)
        build(4, prior_ref[3 * BLOCK :, :], True)
        lax.fori_loop(0, 4, build_from(own_ref, 5, True), 0)
        halo_q = q_ref[BLOCK - HALO : BLOCK, :]
        stacked = jnp.concatenate(
            [jnp.where(head_lane == h, halo_q, jnp.zeros_like(halo_q)) for h in range(4)], axis=0
        )
        scores = dot_t(stacked, k_ref[BLOCK - HALO : PAST, :])
        row = lax.broadcasted_iota(jnp.int32, scores.shape, 0) % HALO + (PAST - HALO)
        col = lax.broadcasted_iota(jnp.int32, scores.shape, 1) + (BLOCK - HALO)
        allowed = (col <= row) & (col > row - WINDOW) & (col >= lowest)
        scores = jnp.where(allowed, scores, masked_low)
        top = jnp.max(scores, axis=1, keepdims=True)
        weights = jnp.exp2(scores - top)
        total = jnp.sum(weights, axis=1, keepdims=True)
        mixed = dot(weights.astype(bf16), v_ref[BLOCK - HALO : PAST, :]) / total
        result = jnp.zeros((HALO, SHARE), f32)
        for h in range(4):
            result = jnp.where(head_lane == h, mixed[h * HALO : (h + 1) * HALO], result)
        for s, out_ref in enumerate(outs):

            @pl.when(lax.rem(head + s, 4) == 0)
            def _(out_ref=out_ref):
                out_ref[0:HALO, :] = result.astype(bf16)

    begin = pl.multiple_of((quarter + 1) * BLOCK, BLOCK)
    keys = k_ref[pl.ds(begin, PAST), :]
    values = v_ref[pl.ds(begin, PAST), :]
    query = q_ref[pl.ds(begin, BLOCK), :]
    row = lax.broadcasted_iota(jnp.int32, (BLOCK, BLOCK), 0)
    col = lax.broadcasted_iota(jnp.int32, (BLOCK, BLOCK), 1)
    biases = [
        jnp.where(begin + t * BLOCK >= lowest, 0.0, masked_low).astype(f32) for t in range(4)
    ]
    first_bias = jnp.where(col > row, 0.0, masked_low) + biases[0]
    last_bias = jnp.where(col <= row, 0.0, masked_low)
    ones = jnp.ones((PAST, 128), bf16)
    low_lanes = lax.broadcasted_iota(jnp.int32, (1, 128), 1) < 64
    results = []

    def score(h):
        return dot_t(jnp.where(head_lane == h, query, jnp.zeros_like(query)), keys)

    ahead = score(0)
    for h in range(4):
        scores = ahead
        if h < 3:
            ahead = score(h + 1)
        tiles = [scores[:, t * BLOCK : (t + 1) * BLOCK] for t in range(5)]
        tiles = (
            [tiles[0] + first_bias]
            + [tiles[t] + biases[t] for t in range(1, 4)]
            + [tiles[4] + last_bias]
        )
        peak = tiles[0]
        for t in range(1, 5):
            peak = jnp.maximum(peak, tiles[t])
        top = jnp.max(peak, axis=1, keepdims=True)
        weights = [jnp.exp2(tile - top).astype(bf16) for tile in tiles]
        pair = (h // 2) * 128
        wide = jnp.concatenate([values[:, pair : pair + 128], ones], axis=1)
        mixed = dot(jnp.concatenate(weights, axis=1), wide)
        results.append(mixed[:, :128] / mixed[:, 128:])
    result = jnp.concatenate(
        [jnp.where(low_lanes, results[2 * n], results[2 * n + 1]) for n in range(2)], axis=1
    )
    result = result.astype(bf16)
    for s in range(4):

        @pl.when(step == s)
        def _(s=s):
            outs[s][HALO:, :] = result

            @pl.when(quarter < 3)
            def _():
                outs[(s + 1) % 4][0:HALO, :] = result[BLOCK - HALO :]


def vmem():
    return pl.BlockSpec(memory_space=pltpu.VMEM)


def smem():
    return pl.BlockSpec(memory_space=pltpu.SMEM)


def space(shape):
    plain = isinstance(shape, jax.ShapeDtypeStruct)
    return vmem() if plain else pl.BlockSpec(memory_space=pltpu.HBM)


def call(kernel, name, shapes, scalars, arrays, scratch=(), grid=None, limit=16, us=2, hbm=(), free=()):
    one = not isinstance(shapes, (list, tuple))
    extra = {} if grid is None else {"grid": grid}
    return pl.pallas_call(
        kernel,
        out_shape=shapes,
        in_specs=[smem()] * len(scalars)
        + [vmem()] * len(arrays)
        + [pl.BlockSpec(memory_space=pltpu.HBM)] * len(hbm)
        + [pl.BlockSpec(memory_space=pl.ANY)] * len(free),
        out_specs=space(shapes) if one else [space(shape) for shape in shapes],
        scratch_shapes=list(scratch),
        compiler_params=pltpu.CompilerParams(vmem_limit_bytes=limit << 20),
        cost_estimate=pl.CostEstimate(
            flops=us * 10**9, transcendentals=0, bytes_accessed=us * 2 * 10**6
        ),
        name=name,
        **extra,
    )(*scalars, *arrays, *(pltpu.with_memory_space_constraint(a, pltpu.HBM) for a in hbm), *free)


def begin_copies(pairs, sems):
    copies = [pltpu.make_async_copy(a, b, sems.at[n]) for n, (a, b) in enumerate(pairs)]
    for copy in copies:
        copy.start()
    return copies


def finish_copies(copies):
    for copy in copies:
        copy.wait()


def fine_rows_kernel(
    where_ref, ids_ref, emb_ref, g0, g1, g2, g3, own_ref, m1, m2, t1, t2, w_hbm,
    out_ref, w_ref, sems,
):
    place, head, core = where_ref[0], where_ref[1], where_ref[2]
    copies = begin_copies([(w_hbm.at[n], w_ref.at[n]) for n in range(4)], sems)
    merged = dot(pick(ids_ref[...]), emb_ref[...]) + dot(g0[...], own_ref[...])
    near = jnp.where(core == 0, g1[...], g3[...])
    far = jnp.where(core == 0, g3[...], g1[...])
    merged += dot(near, m1[...]) + dot(far, t1[...])
    at = pl.ds(pl.multiple_of(core * 128, 128), 128)
    merged += dot(g2[:, at], m2[...])
    at = pl.ds(pl.multiple_of(128 - core * 128, 128), 128)
    merged += dot(g2[:, at], t2[...])
    rows = 256 + HALO
    token = (
        place * ROWS + head * 256 - HALO + lax.broadcasted_iota(jnp.int32, (rows, D), 0)
    )
    fine = jnp.where(token >= 0, merged, 0.0).astype(bf16)
    index = lax.broadcasted_iota(jnp.int32, (256, rows), 0)
    column = lax.broadcasted_iota(jnp.int32, (256, rows), 1)
    source = 4 * (index % 64) + index // 64 + (HALO - 3)
    choose = (source == column).astype(f32).astype(bf16)
    grouped = dot(choose, fine).astype(bf16)
    for d in range(4):
        out_ref[d, 0:256, :] = grouped[:, d * SHARE : (d + 1) * SHARE]
        out_ref[d, 256:rows, :] = fine[256:rows, d * SHARE : (d + 1) * SHARE]
    finish_copies(copies)


def short_part_kernel(group_ref, w_ref, out_ref):
    total = dot(group_ref[0:64, :], w_ref[0])
    for r in range(1, SHORTEN):
        total += dot(group_ref[r * 64 : (r + 1) * 64, :], w_ref[r])
    out_ref[...] = total.astype(bf16)


def coarse_pack_kernel(
    where_ref, s0, s1, s2, s3, gain_ref, wq_ref, wk_ref, wv_ref, turn_ref,
    out_ref, short_ref,
):
    place, head = where_ref[0], where_ref[1]
    for s, ref in enumerate((s0, s1, s2, s3)):
        begin = pl.multiple_of(lax.rem(head - s + 4, 4) * 64, 64)
        short_ref[pl.ds(begin, 64), :] = ref[...]
    x = norm_rows(short_ref[...].astype(f32), gain_ref[...])
    cosine, sine = turn_tables(turn_ref, place)

    def turned(values):
        return values * cosine + partner(values) * sine

    q = turned(dot(x, wq_ref[...])) * q_scale
    k = turned(dot(x, wk_ref[...]))
    v = dot(x, wv_ref[...])
    low_lanes = lax.broadcasted_iota(jnp.int32, (1, 128), 1) < 64
    half = COARSE_ROWS // 2
    for h in range(4):
        pair = (h // 2) * 128
        kp = k[:, pair : pair + 128]
        vp = v[:, pair : pair + 128]
        qp = q[:, pair : pair + 128]
        if h % 2 == 0:
            kv = jnp.where(low_lanes, kp, pltpu.roll(vp, 64, 1))
            qq = jnp.where(low_lanes, qp[:half], pltpu.roll(qp[half:], 64, 1))
        else:
            kv = jnp.where(low_lanes, pltpu.roll(kp, 64, 1), vp)
            qq = jnp.where(low_lanes, pltpu.roll(qp[:half], 64, 1), qp[half:])
        out_ref[h, 0:COARSE_ROWS, :] = kv.astype(bf16)
        out_ref[h, COARSE_ROWS : COARSE_ROWS + half, :] = qq.astype(bf16)


def with_ones(kv):
    return jnp.concatenate([kv, jnp.ones((kv.shape[0], 128), bf16)], axis=1)


def absorb(q_ref, top_ref, total_ref, acc_ref, begin, rows, parts):
    at = pl.ds(begin, rows)
    query = q_ref[at, :]
    scores = [dot_t(query, kv) for kv in parts]
    peak = scores[0]
    for s in scores[1:]:
        peak = jnp.maximum(peak, s)
    old = top_ref[at, :]
    top = jnp.maximum(old, jnp.max(peak, axis=1, keepdims=True))
    factor = jnp.exp2(old - top)
    both = jnp.concatenate([top, top], axis=1)
    contrib = dot(jnp.exp2(scores[0] - both).astype(bf16), with_ones(parts[0]))
    for s, kv in zip(scores[1:], parts[1:]):
        contrib = contrib + dot(jnp.exp2(s - both).astype(bf16), with_ones(kv))
    top_ref[at, :] = top
    total_ref[at, :] = total_ref[at, :] * factor + contrib[:, 128:]
    acc_ref[at, :] = acc_ref[at, :] * factor + contrib[:, :128]


def coarse_first_kernel(turned_ref, q_ref, top_ref, total_ref, acc_ref):
    half = COARSE_ROWS // 2
    low_lanes = lax.broadcasted_iota(jnp.int32, (1, 128), 1) < 64
    row = lax.broadcasted_iota(jnp.int32, (256, 256), 0)
    col = lax.broadcasted_iota(jnp.int32, (256, 256), 1)
    for z in range(4):
        packed = turned_ref[z, COARSE_ROWS:, :].astype(f32)
        zero = jnp.zeros_like(packed)
        q_ref[z * 256 : z * 256 + half, :] = jnp.where(low_lanes, packed, zero).astype(bf16)
        q_ref[z * 256 + half : (z + 1) * 256, :] = jnp.where(
            low_lanes, pltpu.roll(packed, 64, 1), zero
        ).astype(bf16)
        kv = turned_ref[z, :COARSE_ROWS, :]
        at = pl.ds(z * 256, 256)
        scores = jnp.where(col <= row, dot_t(q_ref[at, :], kv), masked_low)
        top = jnp.max(scores, axis=1, keepdims=True)
        contrib = dot(jnp.exp2(scores - top).astype(bf16), with_ones(kv))
        top_ref[at, :] = jnp.broadcast_to(top, (256, 128))
        total_ref[at, :] = contrib[:, 128:]
        acc_ref[at, :] = contrib[:, :128]
    state = (q_ref, top_ref, total_ref, acc_ref)
    for z in range(3):
        absorb(*state, (z + 1) * 256, (3 - z) * 256, [turned_ref[z, :COARSE_ROWS, :]])


def coarse_far_kernel(
    flag_ref, far_ref, q_ref, top_in, total_in, acc_in, top_ref, total_ref, acc_ref
):
    top_ref[...] = top_in[...]
    total_ref[...] = total_in[...]
    acc_ref[...] = acc_in[...]
    state = (q_ref, top_ref, total_ref, acc_ref)
    for z in range(3):
        absorb(*state, (z + 1) * 256, (3 - z) * 256, [far_ref[z]])

    @pl.when(flag_ref[0] > 0)
    def _():
        for z in range(4):
            absorb(*state, z * 256, 256, [far_ref[z]])


def coarse_more_kernel(which, last, flag_ref, *refs):
    count = 2 * len(which)
    sems = refs[-1]
    refs = refs[:-1]
    chunks = refs[:count]
    q_ref, top_in, total_in, acc_in = refs[count : count + 4]
    refs = refs[count + 4 :]
    top_ref, total_ref, acc_ref = refs[-3:]
    if last:
        own, m1, m2, t1, t2, target, out_ref = refs[:-3]
        pairs = place_copies(flag_ref[4], flag_ref[5], own, (m1, m2), (t1, t2), target)
    else:
        pairs = []
        for a, b in zip(refs[:2], refs[2:4]):
            for part in range(4):
                at = pl.ds(part * 256, 256)
                pairs.append((a.at[at], b.at[at]))
    copies = begin_copies(pairs, sems)
    top_ref[...] = top_in[...]
    total_ref[...] = total_in[...]
    acc_ref[...] = acc_in[...]
    state = (q_ref, top_ref, total_ref, acc_ref)
    for n, s in enumerate(which):
        near, far = chunks[2 * n], chunks[2 * n + 1]
        for z in range(3):
            absorb(*state, (z + 1) * 256, (3 - z) * 256, [near[z], far[z]])

        @pl.when(flag_ref[s] > 0)
        def _(near=near, far=far):
            for z in range(4):
                absorb(*state, z * 256, 256, [near[z], far[z]])

    if last:
        mixed = acc_ref[...] / total_ref[...]
        low_lanes = lax.broadcasted_iota(jnp.int32, (1, 128), 1) < 64
        for z in range(4):
            upper = pltpu.roll(mixed[z * 256 : z * 256 + 128], 64, 1)
            lower = mixed[z * 256 + 128 : (z + 1) * 256]
            block = jnp.where(low_lanes, upper, lower).astype(bf16)
            for y in range(4):
                out_ref[z * 4 + y] = block
    finish_copies(copies)


def feed_kernel(
    where_ref, heads_ref, short_ref, gain_ref, co_ref, up_ref, down_ref,
    part_ref, first_ref, mixed_ref, all_ref,
):
    head = where_ref[1]
    low_lanes = lax.broadcasted_iota(jnp.int32, (1, 128), 1) < 64
    for y in range(4):
        for pair in range(2):
            even = heads_ref[2 * pair * 4 + y].astype(f32)
            odd = heads_ref[(2 * pair + 1) * 4 + y].astype(f32)
            at = slice(y * 256 + pair * 128, y * 256 + (pair + 1) * 128)
            mixed_ref[0:128, at] = jnp.where(low_lanes, even, pltpu.roll(odd, 64, 1)).astype(bf16)
            mixed_ref[128:256, at] = jnp.where(low_lanes, pltpu.roll(even, 64, 1), odd).astype(bf16)
    first = short_ref[...].astype(f32) + dot(mixed_ref[...], co_ref[...])
    all_ref[...] = first
    first_ref[...] = all_ref[pl.ds(pl.multiple_of(head * 64, 64), 64), :]
    feed = norm_rows(first, gain_ref[...])
    inner = jax.nn.gelu(dot(feed, up_ref[...])).astype(bf16)
    part_ref[...] = dot(inner, down_ref[...]).astype(bf16).reshape(4, 64, D)


def final_kernel(where_ref, s0, s1, s2, s3, b0, b1, b2, b3, up_ref, out_ref):
    head = where_ref[1]
    rows = 256 + HALO
    second = jnp.concatenate([ref[...] for ref in (s0, s1, s2, s3)], axis=0)
    lifted = dot(second, up_ref[...])
    index = lax.broadcasted_iota(jnp.int32, (256, rows), 0)
    column = lax.broadcasted_iota(jnp.int32, (256, rows), 1)
    r, m = index // 64, index % 64
    source = jnp.where(r == 0, 192 + m, jnp.where(m == 63, 268 + r, (r - 1) * 64 + m + 1))
    choose = (source == column).astype(f32).astype(bf16)
    index = lax.broadcasted_iota(jnp.int32, (256, 256), 0)
    column = lax.broadcasted_iota(jnp.int32, (256, 256), 1)
    weave = ((index % 4) * 64 + index // 4 == column).astype(f32).astype(bf16)
    for s, block in enumerate((b0, b1, b2, b3)):
        mine = lifted[s * 64 : (s + 1) * 64]
        raised = jnp.concatenate([mine[:, q * SHARE : (q + 1) * SHARE] for q in range(4)], axis=0)
        value = (dot(choose, block[...]) + raised).astype(bf16)
        begin = pl.multiple_of(lax.rem(head - s + 4, 4) * 256, 256)
        out_ref[pl.ds(begin, 256), :] = dot(weave, value).astype(bf16)


def fetch_rest(weight, core):
    pairs = []
    for c, step in ((0, 1), (1, 3)):
        pairs += [(4 * c + y, 4 * c + (y + step) % 4) for y in range(4)]
    whole = lax.ppermute(weight, ("core", "head"), pairs)
    half = shift(lax.dynamic_slice_in_dim(weight, core * 128, 128, 0), "head", 2, 4)
    return [whole, half]


def swap_cores(parts):
    return [shift(part, "core", 1, 2) for part in parts]


def sources(head, core):
    mine = lax.rem(head + 3 - 2 * core, 4)
    other = lax.rem(head + 1 + 2 * core, 4)
    return mine, other, lax.rem(head + 2, 4)


def place_copies(head, core, own, mine, other, target):
    near, far, apart = sources(head, core)
    halves_at = apart * 256
    return [
        (own, target.at[pl.ds(pl.multiple_of(head * 256, 256), 256)]),
        (mine[0], target.at[pl.ds(pl.multiple_of(near * 256, 256), 256)]),
        (other[0], target.at[pl.ds(pl.multiple_of(far * 256, 256), 256)]),
        (mine[1], target.at[pl.ds(pl.multiple_of(halves_at + core * 128, 128), 128)]),
        (other[1], target.at[pl.ds(pl.multiple_of(halves_at + 128 - core * 128, 128), 128)]),
    ]


def after(value, gate):
    return lax.optimization_barrier((value, gate))


def local(
    token_ids, embedding, fine_norm, fine_query, fine_key, fine_value, fine_output,
    shorten_weight, coarse_norm, coarse_query, coarse_key, coarse_value, coarse_output,
    ffn_norm, ffn_up, ffn_down, upsample_weight,
):
    place = lax.axis_index(SEQ).astype(jnp.int32)
    head = lax.axis_index("head").astype(jnp.int32)
    x_place = lax.axis_index("x").astype(jnp.int32)
    core = lax.axis_index("core").astype(jnp.int32)
    tables = jnp.asarray(angle_tables())
    where = jnp.stack([place, head, core])

    prior = later(token_ids, SEQ, 1, 32)
    before = later(prior, SEQ, 1, 32)[ROWS - HALO :]
    norm_held, prior = after(fine_norm, prior)
    tab = call(
        fine_tables_kernel, "fine_tables", pltpu.HBM((5, 256, SHARE), bf16), [], [],
        [
            pltpu.VMEM((5, 256, SHARE), bf16),
            pltpu.VMEM((1, D), f32), pltpu.VMEM((256, D), bf16),
            pltpu.VMEM((3, D, SHARE), bf16), pltpu.SemaphoreType.DMA((9,)),
        ],
        us=3, hbm=[norm_held[None], embedding, fine_query, fine_key, fine_value],
    )
    own_ids_column = token_ids[:, None]
    fine_output_held, own_ids_column = after(fine_output, own_ids_column)
    out_mine = fetch_rest(fine_output_held, core)
    rows = 256 + HALO
    mixed = call(
        fine_kernel, "fine_attention", [jax.ShapeDtypeStruct((rows, SHARE), bf16)] * 4,
        [where], [before[:, None], prior[:, None], own_ids_column],
        [
            pltpu.VMEM((BLOCK + ROWS, SHARE), bf16),
            pltpu.VMEM((KEYS, SHARE), bf16), pltpu.VMEM((KEYS, SHARE), bf16),
            pltpu.VMEM((5, 256, SHARE), bf16), pltpu.VMEM((576, 128), f32),
            pltpu.SemaphoreType.DMA((10,)),
        ],
        grid=(4,), us=12, limit=24, hbm=[tab, tables],
    )

    out_mine, mixed = after(out_mine, mixed)
    got = [mixed[0]] + [shift(mixed[s], "head", s, 4) for s in range(1, 4)]
    out_other = swap_cores(out_mine)
    own_ids = lax.dynamic_slice_in_dim(
        jnp.concatenate([prior[ROWS - HALO :], token_ids]), head * 256, rows, 0
    )
    sends, shorten_near = call(
        fine_rows_kernel, "fine_rows",
        [
            jax.ShapeDtypeStruct((4, rows, SHARE), bf16),
            jax.ShapeDtypeStruct((SHORTEN, SHARE, D), bf16),
        ],
        [where],
        [own_ids[:, None], embedding, *got, fine_output, *out_mine, *out_other],
        [pltpu.SemaphoreType.DMA((4,))], hbm=[shorten_weight],
    )
    blocks = exchange(lambda d: lax.dynamic_index_in_dim(sends, d, 0, keepdims=False), "head", 4)

    terms = []
    for s, block in enumerate(blocks):
        part = call(
            short_part_kernel, "short_part", jax.ShapeDtypeStruct((64, D), bf16), [],
            [block, shorten_near],
        )
        terms.append(part if s == 0 else shift(part, "head", 4 - s, 4))
    short_own = sum(t.astype(f32) for t in terms).astype(bf16)
    shorts = [short_own] + [shift(short_own, "head", s, 4) for s in range(1, 4)]
    packed, short = call(
        coarse_pack_kernel, "coarse_pack",
        [
            jax.ShapeDtypeStruct((4, COARSE_ROWS * 3 // 2, 128), bf16),
            jax.ShapeDtypeStruct((COARSE_ROWS, D), bf16),
        ],
        [where],
        [*shorts, coarse_norm[None], coarse_query, coarse_key, coarse_value, tables],
    )

    coarse_output_held, packed = after(coarse_output, packed)
    co_mine = fetch_rest(coarse_output_held, core)
    turned = lax.all_to_all(packed, "z", 0, 0)
    co_mine[1], turned = after(co_mine[1], turned)
    kv = turned[:, :COARSE_ROWS]
    far = [shift(kv, "core", 1, 2)]
    near = [shift(kv, "x", s, 4) for s in range(1, 4)]
    steps = jnp.arange(4, dtype=jnp.int32)
    flags = ((x_place - steps + 4) % 4 < x_place).astype(jnp.int32) + (steps == 0) * core
    flags = jnp.concatenate([flags, where[1:]])
    wide = jax.ShapeDtypeStruct((1024, 128), f32)
    q_all, *sums = call(
        coarse_first_kernel, "coarse_first",
        [jax.ShapeDtypeStruct((1024, 128), bf16), wide, wide, wide], [], [turned],
        us=2, limit=24,
    )
    sums = call(
        coarse_far_kernel, "coarse_far", [wide, wide, wide], [flags], [far[0], q_all, *sums],
        us=2, limit=24,
    )
    near_held, co_held, sums = lax.optimization_barrier((near, co_mine, sums))
    far += [shift(part, "core", 1, 2) for part in near_held]
    co_other = swap_cores(co_held)
    square = jax.ShapeDtypeStruct((D, D), bf16)
    up_near, down_near, *sums = call(
        functools.partial(coarse_more_kernel, (1, 3), False), "coarse_more",
        [square, square, wide, wide, wide],
        [flags], [near[0], far[1], near[2], far[3], q_all, *sums],
        [pltpu.SemaphoreType.DMA((8,))], us=6, limit=24, hbm=[ffn_up, ffn_down],
    )
    output_near, wide_sends = call(
        functools.partial(coarse_more_kernel, (2,), True), "coarse_last",
        [square, jax.ShapeDtypeStruct((16, 128, 128), bf16)],
        [flags], [near[1], far[2], q_all, *sums],
        [pltpu.VMEM((1024, 128), f32)] * 3 + [pltpu.SemaphoreType.DMA((5,))],
        us=3, limit=24, hbm=[coarse_output], free=[*co_mine, *co_other],
    )

    heads_in = lax.all_to_all(wide_sends, ("z", "head"), 0, 0)
    parts, first_own = call(
        feed_kernel, "feed",
        [jax.ShapeDtypeStruct((4, 64, D), bf16), jax.ShapeDtypeStruct((64, D), f32)],
        [where],
        [heads_in, short, ffn_norm[None], output_near, up_near, down_near],
        [
            pltpu.VMEM((COARSE_ROWS, D), bf16), pltpu.VMEM((COARSE_ROWS, D), f32),
        ],
        us=4,
    )
    sums = exchange(lambda d: lax.dynamic_index_in_dim(parts, d, 0, keepdims=False), "head", 4)
    second_own = (first_own + sum(t.astype(f32) for t in sums)).astype(bf16)
    seconds = [second_own] + [shift(second_own, "head", s, 4) for s in range(1, 4)]
    return call(
        final_kernel, "final", jax.ShapeDtypeStruct((ROWS, SHARE), bf16),
        [where], [*seconds, *blocks, upsample_weight.reshape(D, SHORTEN * SHARE)],
    )


def solution(mesh):
    split = Mesh(mesh.devices.reshape(4, 4, 2, 4), ("z", "x", "core", "head"))
    return jax.shard_map(
        local,
        mesh=split,
        in_specs=(
            P(SEQ), P(), P(), P(None, "head"), P(None, "head"), P(None, "head"), P("head", None),
            P(None, "head", None), P(), P(None, "head"), P(None, "head"), P(None, "head"),
            P("head", None), P(), P(None, "head"), P("head", None), P(None, None, "head"),
        ),
        out_specs=P(SEQ, "head"),
        check_vma=False,
    )
```

```python
import functools
import math

import jax
import jax.numpy as jnp
import numpy as np
from jax import lax
from jax.experimental import pallas as pl
from jax.experimental.pallas import tpu as pltpu
from jax.sharding import Mesh
from jax.sharding import PartitionSpec as P

D = 1024
HEAD_DIM = 64
SHORTEN = 4
WINDOW = 1024
BLOCK = 256
HALO = 16
ROWS = 1024
PAST = WINDOW + BLOCK
KEYS = PAST + ROWS
SHARE = 256
COARSE_ROWS = 256
SEQ = ("z", "x", "core")

epsilon = 1e-06
masked_low = -1e30
q_scale = HEAD_DIM ** (-0.5) * math.log2(math.e)
bf16 = jnp.bfloat16
f32 = jnp.float32


def angle_tables():
    lane = np.arange(128) % 32
    period = 2.0 ** (4 + lane * 14 // 32)
    coarse = (256.0 * np.arange(32)[:, None]) % period[None]
    near = np.arange(256)[:, None] % period[None]
    a = coarse * (2.0 * np.pi / period)[None]
    b = near * (2.0 * np.pi / period)[None]
    parts = [np.cos(a), np.sin(a), np.cos(b), np.sin(b)]
    return np.concatenate(parts, axis=0).astype(np.float32)


def shift(value, axis, steps, count):
    return lax.ppermute(value, axis, [(i, (i + steps) % count) for i in range(count)])


def later(value, axis, steps, count):
    return lax.ppermute(value, axis, [(i, i + steps) for i in range(count - steps)])


def exchange(block_for, axis, count):
    me = lax.axis_index(axis)
    got = [block_for(me)]
    for s in range(1, count):
        got.append(shift(block_for((me + s) % count), axis, s, count))
    return got


def dot(left, right):
    return jnp.dot(left, right, preferred_element_type=f32)


def dot_t(left, right):
    return lax.dot_general(left, right, (((1,), (1,)), ((), ())), preferred_element_type=f32)


def norm_rows(data, gain):
    power = jnp.mean(data * data, axis=-1, keepdims=True)
    return (data * lax.rsqrt(power + epsilon) * gain).astype(bf16)


def partner(values):
    width = values.shape[1]
    lane = lax.broadcasted_iota(jnp.int32, values.shape, 1)
    ahead = pltpu.roll(values, width - 32, 1)
    behind = pltpu.roll(values, 32, 1)
    return jnp.where(lane % 64 < 32, -ahead, behind)


def halves(table):
    high = table.astype(bf16)
    low = (table - high.astype(f32)).astype(bf16)
    return high, low


def turn_tables(turn_ref, far):
    ca = turn_ref[pl.ds(far, 1), :]
    sa = turn_ref[pl.ds(32 + far, 1), :]
    cb = turn_ref[64:320, :]
    sb = turn_ref[320:576, :]
    cosine = ca * cb - sa * sb
    sine = sa * cb + ca * sb
    return jnp.concatenate([cosine, cosine], axis=1), jnp.concatenate([sine, sine], axis=1)


def pick(ids, levels=256):
    columns = lax.broadcasted_iota(jnp.int32, (ids.shape[0], levels), 1)
    return (ids == columns).astype(f32).astype(bf16)


def turned_rows(hot, tab_ref, n, cosine, sine):
    return (dot(hot, tab_ref[n]) * cosine + dot(hot, tab_ref[n + 1]) * sine).astype(bf16)


def fine_tables_kernel(gain_hbm, emb_hbm, wq_hbm, wk_hbm, wv_hbm, tab_hbm, tab_ref, gain_ref, emb_ref, w_ref, sems):
    pairs = [(emb_hbm, emb_ref), (gain_hbm, gain_ref)]
    for n, w in enumerate((wq_hbm, wk_hbm, wv_hbm)):
        for part in range(2):
            rows = pl.ds(part * 512, 512)
            pairs.append((w.at[rows], w_ref.at[n, rows]))
    copies = begin_copies(pairs, sems)
    finish_copies(copies[:2])
    fine_in = norm_rows(emb_ref[...].astype(f32), gain_ref[...])
    finish_copies(copies[2:])
    tq = dot(fine_in, w_ref[0]) * q_scale
    tk = dot(fine_in, w_ref[1])
    tables = (tq, partner(tq), tk, partner(tk), dot(fine_in, w_ref[2]))
    for n, table in enumerate(tables):
        tab_ref[n] = table.astype(bf16)
    finish_copies(begin_copies([(tab_ref.at[n], tab_hbm.at[n]) for n in range(5)], sems))


def fine_kernel(
    where_ref, before_ref, prior_ref, own_ref, tab_hbm, turn_hbm,
    out_ref, q_ref, k_ref, v_ref, tab_ref, turn_ref, sems,
):
    step = pl.program_id(0)
    lowest = jnp.maximum(PAST - where_ref[0] * ROWS, 0)
    head_lane = lax.broadcasted_iota(jnp.int32, (1, SHARE), 1) // HEAD_DIM

    @pl.when(step == 0)
    def _():
        pairs = [(tab_hbm.at[n], tab_ref.at[n]) for n in range(5)] + [(turn_hbm, turn_ref)]
        finish_copies(begin_copies(pairs, sems))
        cosine, sine = turn_tables(turn_ref, 0)
        oldest = pick(before_ref[...])
        at = slice(BLOCK - HALO, BLOCK)
        k_ref[at, :] = turned_rows(oldest, tab_ref, 2, cosine[at], sine[at])
        v_ref[at, :] = dot(oldest, tab_ref[4]).astype(bf16)

        def build(block, ids, with_q):
            begin = pl.multiple_of(block * BLOCK, BLOCK)
            hot = pick(ids)
            cosine, sine = turn_tables(turn_ref, block)
            k_ref[pl.ds(begin, BLOCK), :] = turned_rows(hot, tab_ref, 2, cosine, sine)
            v_ref[pl.ds(begin, BLOCK), :] = dot(hot, tab_ref[4]).astype(bf16)
            if with_q:
                at = pl.multiple_of(begin - (PAST - BLOCK), BLOCK)
                q_ref[pl.ds(at, BLOCK), :] = turned_rows(hot, tab_ref, 0, cosine, sine)

        def build_from(ref, first, with_q):
            def body(n, _):
                ids = ref[pl.ds(pl.multiple_of(n * BLOCK, BLOCK), BLOCK), :]
                build(first + n, ids, with_q)
                return 0

            return body

        for n in range(3):
            build(1 + n, prior_ref[n * BLOCK : (n + 1) * BLOCK, :], False)
        build(4, prior_ref[3 * BLOCK :, :], True)
        for n in range(4):
            build(5 + n, own_ref[n * BLOCK : (n + 1) * BLOCK, :], True)
        halo_q = q_ref[BLOCK - HALO : BLOCK, :]
        stacked = jnp.concatenate(
            [jnp.where(head_lane == h, halo_q, jnp.zeros_like(halo_q)) for h in range(4)], axis=0
        )
        scores = dot_t(stacked, k_ref[BLOCK - HALO : PAST, :])
        row = lax.broadcasted_iota(jnp.int32, scores.shape, 0) % HALO + (PAST - HALO)
        col = lax.broadcasted_iota(jnp.int32, scores.shape, 1) + (BLOCK - HALO)
        allowed = (col <= row) & (col > row - WINDOW) & (col >= lowest)
        scores = jnp.where(allowed, scores, masked_low)
        top = jnp.max(scores, axis=1, keepdims=True)
        weights = jnp.exp2(scores - top)
        total = jnp.sum(weights, axis=1, keepdims=True)
        mixed = dot(weights.astype(bf16), v_ref[BLOCK - HALO : PAST, :]) / total
        result = jnp.zeros((HALO, SHARE), f32)
        for h in range(4):
            result = jnp.where(head_lane == h, mixed[h * HALO : (h + 1) * HALO], result)
        out_ref[0, 0:HALO, :] = result.astype(bf16)

    begin = pl.multiple_of((step + 1) * BLOCK, BLOCK)
    keys = k_ref[pl.ds(begin, PAST), :]
    values = v_ref[pl.ds(begin, PAST), :]
    query = q_ref[pl.ds(begin, BLOCK), :]
    row = lax.broadcasted_iota(jnp.int32, (BLOCK, BLOCK), 0)
    col = lax.broadcasted_iota(jnp.int32, (BLOCK, BLOCK), 1)
    biases = [
        jnp.where(begin + t * BLOCK >= lowest, 0.0, masked_low).astype(f32) for t in range(4)
    ]
    first_bias = jnp.where(col > row, 0.0, masked_low) + biases[0]
    last_bias = jnp.where(col <= row, 0.0, masked_low)
    ones = jnp.ones((PAST, 128), bf16)
    low_lanes = lax.broadcasted_iota(jnp.int32, (1, 128), 1) < 64
    results = []

    def score(h):
        return dot_t(jnp.where(head_lane == h, query, jnp.zeros_like(query)), keys)

    ahead = score(0)
    for h in range(4):
        scores = ahead
        if h < 3:
            ahead = score(h + 1)
        tiles = [scores[:, t * BLOCK : (t + 1) * BLOCK] for t in range(5)]
        tiles = (
            [tiles[0] + first_bias]
            + [tiles[t] + biases[t] for t in range(1, 4)]
            + [tiles[4] + last_bias]
        )
        peak = tiles[0]
        for t in range(1, 5):
            peak = jnp.maximum(peak, tiles[t])
        top = jnp.max(peak, axis=1, keepdims=True)
        weights = [jnp.exp2(tile - top).astype(bf16) for tile in tiles]
        pair = (h // 2) * 128
        wide = jnp.concatenate([values[:, pair : pair + 128], ones], axis=1)
        mixed = dot(jnp.concatenate(weights, axis=1), wide)
        results.append(mixed[:, :128] / mixed[:, 128:])
    result = jnp.concatenate(
        [jnp.where(low_lanes, results[2 * n], results[2 * n + 1]) for n in range(2)], axis=1
    )
    result = result.astype(bf16)
    out_ref[step, HALO:, :] = result

    @pl.when(step < 3)
    def _():
        out_ref[step + 1, 0:HALO, :] = result[BLOCK - HALO :]


def vmem():
    return pl.BlockSpec(memory_space=pltpu.VMEM)


def smem():
    return pl.BlockSpec(memory_space=pltpu.SMEM)


def space(shape):
    plain = isinstance(shape, jax.ShapeDtypeStruct)
    return vmem() if plain else pl.BlockSpec(memory_space=pltpu.HBM)


def call(kernel, name, shapes, scalars, arrays, scratch=(), grid=None, limit=16, us=2, hbm=(), free=()):
    one = not isinstance(shapes, (list, tuple))
    extra = {} if grid is None else {"grid": grid}
    return pl.pallas_call(
        kernel,
        out_shape=shapes,
        in_specs=[smem()] * len(scalars)
        + [vmem()] * len(arrays)
        + [pl.BlockSpec(memory_space=pltpu.HBM)] * len(hbm)
        + [pl.BlockSpec(memory_space=pl.ANY)] * len(free),
        out_specs=space(shapes) if one else [space(shape) for shape in shapes],
        scratch_shapes=list(scratch),
        compiler_params=pltpu.CompilerParams(vmem_limit_bytes=limit << 20),
        cost_estimate=pl.CostEstimate(
            flops=us * 10**9, transcendentals=0, bytes_accessed=us * 2 * 10**6
        ),
        name=name,
        **extra,
    )(*scalars, *arrays, *(pltpu.with_memory_space_constraint(a, pltpu.HBM) for a in hbm), *free)


def begin_copies(pairs, sems):
    copies = [pltpu.make_async_copy(a, b, sems.at[n]) for n, (a, b) in enumerate(pairs)]
    for copy in copies:
        copy.start()
    return copies


def finish_copies(copies):
    for copy in copies:
        copy.wait()


def fine_rows_kernel(
    where_ref, ids_ref, emb_ref, got_ref, own_ref, m1, m2, t1, t2, w_hbm,
    out_ref, w_ref, sems,
):
    place, head, core = where_ref[0], where_ref[1], where_ref[2]
    copies = begin_copies([(w_hbm.at[n], w_ref.at[n]) for n in range(4)], sems)
    merged = dot(pick(ids_ref[...]), emb_ref[...]) + dot(got_ref[head], own_ref[...])
    near, far, apart = sources(head, core)
    merged += dot(got_ref[near], m1[...]) + dot(got_ref[far], t1[...])
    at = pl.ds(pl.multiple_of(core * 128, 128), 128)
    merged += dot(got_ref[apart, :, at], m2[...])
    at = pl.ds(pl.multiple_of(128 - core * 128, 128), 128)
    merged += dot(got_ref[apart, :, at], t2[...])
    rows = 256 + HALO
    token = (
        place * ROWS + head * 256 - HALO + lax.broadcasted_iota(jnp.int32, (rows, D), 0)
    )
    fine = jnp.where(token >= 0, merged, 0.0).astype(bf16)
    index = lax.broadcasted_iota(jnp.int32, (256, rows), 0)
    column = lax.broadcasted_iota(jnp.int32, (256, rows), 1)
    source = 4 * (index % 64) + index // 64 + (HALO - 3)
    choose = (source == column).astype(f32).astype(bf16)
    grouped = dot(choose, fine).astype(bf16)
    for d in range(4):
        out_ref[d, 0:256, :] = grouped[:, d * SHARE : (d + 1) * SHARE]
        out_ref[d, 256:rows, :] = fine[256:rows, d * SHARE : (d + 1) * SHARE]
    finish_copies(copies)


def short_part_kernel(group_ref, w_ref, out_ref):
    total = dot(group_ref[0:64, :], w_ref[0])
    for r in range(1, SHORTEN):
        total += dot(group_ref[r * 64 : (r + 1) * 64, :], w_ref[r])
    out_ref[...] = total.astype(bf16)


def coarse_pack_kernel(
    where_ref, s0, s1, s2, s3, gain_ref, wq_ref, wk_ref, wv_ref, turn_ref,
    out_ref, short_ref,
):
    place, head = where_ref[0], where_ref[1]
    for s, ref in enumerate((s0, s1, s2, s3)):
        begin = pl.multiple_of(lax.rem(head - s + 4, 4) * 64, 64)
        short_ref[pl.ds(begin, 64), :] = ref[...]
    x = norm_rows(short_ref[...].astype(f32), gain_ref[...])
    cosine, sine = turn_tables(turn_ref, place)

    def turned(values):
        return values * cosine + partner(values) * sine

    q = turned(dot(x, wq_ref[...])) * q_scale
    k = turned(dot(x, wk_ref[...]))
    v = dot(x, wv_ref[...])
    low_lanes = lax.broadcasted_iota(jnp.int32, (1, 128), 1) < 64
    half = COARSE_ROWS // 2
    for h in range(4):
        pair = (h // 2) * 128
        kp = k[:, pair : pair + 128]
        vp = v[:, pair : pair + 128]
        qp = q[:, pair : pair + 128]
        if h % 2 == 0:
            kv = jnp.where(low_lanes, kp, pltpu.roll(vp, 64, 1))
            qq = jnp.where(low_lanes, qp[:half], pltpu.roll(qp[half:], 64, 1))
        else:
            kv = jnp.where(low_lanes, pltpu.roll(kp, 64, 1), vp)
            qq = jnp.where(low_lanes, pltpu.roll(qp[:half], 64, 1), qp[half:])
        out_ref[h, 0:COARSE_ROWS, :] = kv.astype(bf16)
        out_ref[h, COARSE_ROWS : COARSE_ROWS + half, :] = qq.astype(bf16)


def with_ones(kv):
    return jnp.concatenate([kv, jnp.ones((kv.shape[0], 128), bf16)], axis=1)


def absorb(state, jobs):
    q_ref, top_ref, total_ref, acc_ref = state

    def score(job):
        query = q_ref[pl.ds(job[0], job[1]), :]
        return [dot_t(query, kv) for kv in job[2]]

    ahead = score(jobs[0])
    for n, (begin, rows, parts) in enumerate(jobs):
        scores = ahead
        if n + 1 < len(jobs):
            ahead = score(jobs[n + 1])
        at = pl.ds(begin, rows)
        peak = scores[0]
        for s in scores[1:]:
            peak = jnp.maximum(peak, s)
        old = top_ref[at, :]
        top = jnp.maximum(old, jnp.max(peak, axis=1, keepdims=True))
        factor = jnp.exp2(old - top)
        both = jnp.concatenate([top, top], axis=1)
        contrib = dot(jnp.exp2(scores[0] - both).astype(bf16), with_ones(parts[0]))
        for s, kv in zip(scores[1:], parts[1:]):
            contrib = contrib + dot(jnp.exp2(s - both).astype(bf16), with_ones(kv))
        top_ref[at, :] = top
        total_ref[at, :] = total_ref[at, :] * factor + contrib[:, 128:]
        acc_ref[at, :] = acc_ref[at, :] * factor + contrib[:, :128]


def coarse_first_kernel(flag_ref, turned_ref, far_ref, q_ref, top_ref, total_ref, acc_ref):
    half = COARSE_ROWS // 2
    low_lanes = lax.broadcasted_iota(jnp.int32, (1, 128), 1) < 64
    row = lax.broadcasted_iota(jnp.int32, (256, 256), 0)
    col = lax.broadcasted_iota(jnp.int32, (256, 256), 1)
    for z in range(4):
        packed = turned_ref[z, COARSE_ROWS:, :].astype(f32)
        zero = jnp.zeros_like(packed)
        q_ref[z * 256 : z * 256 + half, :] = jnp.where(low_lanes, packed, zero).astype(bf16)
        q_ref[z * 256 + half : (z + 1) * 256, :] = jnp.where(
            low_lanes, pltpu.roll(packed, 64, 1), zero
        ).astype(bf16)
        kv = turned_ref[z, :COARSE_ROWS, :]
        at = pl.ds(z * 256, 256)
        scores = jnp.where(col <= row, dot_t(q_ref[at, :], kv), masked_low)
        top = jnp.max(scores, axis=1, keepdims=True)
        contrib = dot(jnp.exp2(scores - top).astype(bf16), with_ones(kv))
        top_ref[at, :] = jnp.broadcast_to(top, (256, 128))
        total_ref[at, :] = contrib[:, 128:]
        acc_ref[at, :] = contrib[:, :128]
    state = (q_ref, top_ref, total_ref, acc_ref)
    absorb(
        state,
        [
            ((z + 1) * 256, (3 - z) * 256, [turned_ref[z, :COARSE_ROWS, :], far_ref[z]])
            for z in range(3)
        ],
    )

    @pl.when(flag_ref[0] > 0)
    def _():
        absorb(state, [(z * 256, 256, [far_ref[z]]) for z in range(4)])


def coarse_more_kernel(which, last, flag_ref, *refs):
    count = 2 * len(which)
    sems = refs[-1]
    refs = refs[:-1]
    chunks = refs[:count]
    q_ref, top_in, total_in, acc_in = refs[count : count + 4]
    refs = refs[count + 4 :]
    top_ref, total_ref, acc_ref = refs[-3:]
    if last:
        own, m1, m2, t1, t2, target, out_ref = refs[:-3]
        pairs = place_copies(flag_ref[4], flag_ref[5], own, (m1, m2), (t1, t2), target)
    else:
        pairs = []
        for a, b in zip(refs[:2], refs[2:4]):
            for part in range(4):
                at = pl.ds(part * 256, 256)
                pairs.append((a.at[at], b.at[at]))
    copies = begin_copies(pairs, sems)
    top_ref[...] = top_in[...]
    total_ref[...] = total_in[...]
    acc_ref[...] = acc_in[...]
    state = (q_ref, top_ref, total_ref, acc_ref)
    pairs_of = [(chunks[2 * n], chunks[2 * n + 1]) for n in range(len(which))]
    absorb(
        state,
        [
            ((z + 1) * 256, (3 - z) * 256, [near[z], far[z]])
            for near, far in pairs_of
            for z in range(3)
        ],
    )
    for s, (near, far) in zip(which, pairs_of):

        @pl.when(flag_ref[s] > 0)
        def _(near=near, far=far):
            absorb(state, [(z * 256, 256, [near[z], far[z]]) for z in range(4)])

    if last:
        mixed = acc_ref[...] / total_ref[...]
        low_lanes = lax.broadcasted_iota(jnp.int32, (1, 128), 1) < 64
        for z in range(4):
            upper = pltpu.roll(mixed[z * 256 : z * 256 + 128], 64, 1)
            lower = mixed[z * 256 + 128 : (z + 1) * 256]
            block = jnp.where(low_lanes, upper, lower).astype(bf16)
            for y in range(4):
                out_ref[z * 4 + y] = block
    finish_copies(copies)


def feed_kernel(
    where_ref, heads_ref, short_ref, gain_ref, co_ref, up_ref, down_ref,
    part_ref, first_ref, mixed_ref, all_ref,
):
    head = where_ref[1]
    low_lanes = lax.broadcasted_iota(jnp.int32, (1, 128), 1) < 64
    for y in range(4):
        for pair in range(2):
            even = heads_ref[2 * pair * 4 + y].astype(f32)
            odd = heads_ref[(2 * pair + 1) * 4 + y].astype(f32)
            at = slice(y * 256 + pair * 128, y * 256 + (pair + 1) * 128)
            mixed_ref[0:128, at] = jnp.where(low_lanes, even, pltpu.roll(odd, 64, 1)).astype(bf16)
            mixed_ref[128:256, at] = jnp.where(low_lanes, pltpu.roll(even, 64, 1), odd).astype(bf16)
    first = short_ref[...].astype(f32) + dot(mixed_ref[...], co_ref[...])
    all_ref[...] = first
    first_ref[...] = all_ref[pl.ds(pl.multiple_of(head * 64, 64), 64), :]
    feed = norm_rows(first, gain_ref[...])
    inner = jax.nn.gelu(dot(feed, up_ref[...])).astype(bf16)
    part_ref[...] = dot(inner, down_ref[...]).astype(bf16).reshape(4, 64, D)


def final_kernel(where_ref, s0, s1, s2, s3, b0, b1, b2, b3, up_ref, out_ref):
    head = where_ref[1]
    rows = 256 + HALO
    second = jnp.concatenate([ref[...] for ref in (s0, s1, s2, s3)], axis=0)
    lifted = dot(second, up_ref[...])
    index = lax.broadcasted_iota(jnp.int32, (256, rows), 0)
    column = lax.broadcasted_iota(jnp.int32, (256, rows), 1)
    r, m = index // 64, index % 64
    source = jnp.where(r == 0, 192 + m, jnp.where(m == 63, 268 + r, (r - 1) * 64 + m + 1))
    choose = (source == column).astype(f32).astype(bf16)
    index = lax.broadcasted_iota(jnp.int32, (256, 256), 0)
    column = lax.broadcasted_iota(jnp.int32, (256, 256), 1)
    weave = ((index % 4) * 64 + index // 4 == column).astype(f32).astype(bf16)
    for s, block in enumerate((b0, b1, b2, b3)):
        mine = lifted[s * 64 : (s + 1) * 64]
        raised = jnp.concatenate([mine[:, q * SHARE : (q + 1) * SHARE] for q in range(4)], axis=0)
        value = (dot(choose, block[...]) + raised).astype(bf16)
        begin = pl.multiple_of(lax.rem(head - s + 4, 4) * 256, 256)
        out_ref[pl.ds(begin, 256), :] = dot(weave, value).astype(bf16)


def fetch_rest(weight, core):
    pairs = []
    for c, step in ((0, 1), (1, 3)):
        pairs += [(4 * c + y, 4 * c + (y + step) % 4) for y in range(4)]
    whole = lax.ppermute(weight, ("core", "head"), pairs)
    half = shift(lax.dynamic_slice_in_dim(weight, core * 128, 128, 0), "head", 2, 4)
    return [whole, half]


def swap_cores(parts):
    return [shift(part, "core", 1, 2) for part in parts]


def sources(head, core):
    mine = lax.rem(head + 3 - 2 * core, 4)
    other = lax.rem(head + 1 + 2 * core, 4)
    return mine, other, lax.rem(head + 2, 4)


def place_copies(head, core, own, mine, other, target):
    near, far, apart = sources(head, core)
    halves_at = apart * 256
    return [
        (own, target.at[pl.ds(pl.multiple_of(head * 256, 256), 256)]),
        (mine[0], target.at[pl.ds(pl.multiple_of(near * 256, 256), 256)]),
        (other[0], target.at[pl.ds(pl.multiple_of(far * 256, 256), 256)]),
        (mine[1], target.at[pl.ds(pl.multiple_of(halves_at + core * 128, 128), 128)]),
        (other[1], target.at[pl.ds(pl.multiple_of(halves_at + 128 - core * 128, 128), 128)]),
    ]


def after(value, gate):
    return lax.optimization_barrier((value, gate))


def local(
    token_ids, embedding, fine_norm, fine_query, fine_key, fine_value, fine_output,
    shorten_weight, coarse_norm, coarse_query, coarse_key, coarse_value, coarse_output,
    ffn_norm, ffn_up, ffn_down, upsample_weight,
):
    place = lax.axis_index(SEQ).astype(jnp.int32)
    head = lax.axis_index("head").astype(jnp.int32)
    x_place = lax.axis_index("x").astype(jnp.int32)
    core = lax.axis_index("core").astype(jnp.int32)
    tables = jnp.asarray(angle_tables())
    where = jnp.stack([place, head, core])

    prior = later(token_ids, SEQ, 1, 32)
    before = later(token_ids, SEQ, 2, 32)[ROWS - HALO :]
    tab = call(
        fine_tables_kernel, "fine_tables", pltpu.HBM((5, 256, SHARE), bf16), [], [],
        [
            pltpu.VMEM((5, 256, SHARE), bf16),
            pltpu.VMEM((1, D), f32), pltpu.VMEM((256, D), bf16),
            pltpu.VMEM((3, D, SHARE), bf16), pltpu.SemaphoreType.DMA((9,)),
        ],
        us=3, hbm=[fine_norm[None], embedding, fine_query, fine_key, fine_value],
    )
    own_ids_column = token_ids[:, None]
    fine_output_held, own_ids_column = after(fine_output, own_ids_column)
    out_mine = fetch_rest(fine_output_held, core)
    rows = 256 + HALO
    mixed = call(
        fine_kernel, "fine_attention", jax.ShapeDtypeStruct((4, rows, SHARE), bf16),
        [where], [before[:, None], prior[:, None], own_ids_column],
        [
            pltpu.VMEM((BLOCK + ROWS, SHARE), bf16),
            pltpu.VMEM((KEYS, SHARE), bf16), pltpu.VMEM((KEYS, SHARE), bf16),
            pltpu.VMEM((5, 256, SHARE), bf16), pltpu.VMEM((576, 128), f32),
            pltpu.SemaphoreType.DMA((10,)),
        ],
        grid=(4,), us=12, limit=24, hbm=[tab, tables],
    )

    out_mine, mixed = after(out_mine, mixed)
    got = lax.all_to_all(mixed, "head", 0, 0)
    out_other = swap_cores(out_mine)
    own_ids = lax.dynamic_slice_in_dim(
        jnp.concatenate([prior[ROWS - HALO :], token_ids]), head * 256, rows, 0
    )
    sends, shorten_near = call(
        fine_rows_kernel, "fine_rows",
        [
            jax.ShapeDtypeStruct((4, rows, SHARE), bf16),
            jax.ShapeDtypeStruct((SHORTEN, SHARE, D), bf16),
        ],
        [where],
        [own_ids[:, None], embedding, got, fine_output, *out_mine, *out_other],
        [pltpu.SemaphoreType.DMA((4,))], hbm=[shorten_weight],
    )
    blocks = exchange(lambda d: lax.dynamic_index_in_dim(sends, d, 0, keepdims=False), "head", 4)

    terms = []
    for s, block in enumerate(blocks):
        part = call(
            short_part_kernel, "short_part", jax.ShapeDtypeStruct((64, D), bf16), [],
            [block, shorten_near],
        )
        terms.append(part if s == 0 else shift(part, "head", 4 - s, 4))
    short_own = sum(t.astype(f32) for t in terms).astype(bf16)
    shorts = [short_own] + [shift(short_own, "head", s, 4) for s in range(1, 4)]
    packed, short = call(
        coarse_pack_kernel, "coarse_pack",
        [
            jax.ShapeDtypeStruct((4, COARSE_ROWS * 3 // 2, 128), bf16),
            jax.ShapeDtypeStruct((COARSE_ROWS, D), bf16),
        ],
        [where],
        [*shorts, coarse_norm[None], coarse_query, coarse_key, coarse_value, tables],
    )

    coarse_output_held, packed = after(coarse_output, packed)
    co_mine = fetch_rest(coarse_output_held, core)
    turned = lax.all_to_all(packed, "z", 0, 0)
    kv = turned[:, :COARSE_ROWS]
    far = [shift(kv, "core", 1, 2)]
    near = [shift(kv, "x", s, 4) for s in range(1, 4)]
    steps = jnp.arange(4, dtype=jnp.int32)
    flags = ((x_place - steps + 4) % 4 < x_place).astype(jnp.int32) + (steps == 0) * core
    flags = jnp.concatenate([flags, where[1:]])
    wide = jax.ShapeDtypeStruct((1024, 128), f32)
    q_all, *sums = call(
        coarse_first_kernel, "coarse_first",
        [jax.ShapeDtypeStruct((1024, 128), bf16), wide, wide, wide], [flags], [turned, far[0]],
        us=3, limit=24,
    )
    near_held, co_held, q_all = lax.optimization_barrier((near, co_mine, q_all))
    far += [shift(part, "core", 1, 2) for part in near_held]
    co_other = swap_cores(co_held)
    square = jax.ShapeDtypeStruct((D, D), bf16)
    up_near, down_near, *sums = call(
        functools.partial(coarse_more_kernel, (1, 3), False), "coarse_more",
        [square, square, wide, wide, wide],
        [flags], [near[0], far[1], near[2], far[3], q_all, *sums],
        [pltpu.SemaphoreType.DMA((8,))], us=6, limit=24, hbm=[ffn_up, ffn_down],
    )
    output_near, wide_sends = call(
        functools.partial(coarse_more_kernel, (2,), True), "coarse_last",
        [square, jax.ShapeDtypeStruct((16, 128, 128), bf16)],
        [flags], [near[1], far[2], q_all, *sums],
        [pltpu.VMEM((1024, 128), f32)] * 3 + [pltpu.SemaphoreType.DMA((5,))],
        us=3, limit=24, hbm=[coarse_output], free=[*co_mine, *co_other],
    )

    heads_in = lax.all_to_all(wide_sends, ("z", "head"), 0, 0)
    parts, first_own = call(
        feed_kernel, "feed",
        [jax.ShapeDtypeStruct((4, 64, D), bf16), jax.ShapeDtypeStruct((64, D), f32)],
        [where],
        [heads_in, short, ffn_norm[None], output_near, up_near, down_near],
        [
            pltpu.VMEM((COARSE_ROWS, D), bf16), pltpu.VMEM((COARSE_ROWS, D), f32),
        ],
        us=4,
    )
    sums = exchange(lambda d: lax.dynamic_index_in_dim(parts, d, 0, keepdims=False), "head", 4)
    second_own = (first_own + sum(t.astype(f32) for t in sums)).astype(bf16)
    seconds = [second_own] + [shift(second_own, "head", s, 4) for s in range(1, 4)]
    return call(
        final_kernel, "final", jax.ShapeDtypeStruct((ROWS, SHARE), bf16),
        [where], [*seconds, *blocks, upsample_weight.reshape(D, SHORTEN * SHARE)],
    )


def solution(mesh):
    split = Mesh(mesh.devices.reshape(4, 4, 2, 4), ("z", "x", "core", "head"))
    return jax.shard_map(
        local,
        mesh=split,
        in_specs=(
            P(SEQ), P(), P(), P(None, "head"), P(None, "head"), P(None, "head"), P("head", None),
            P(None, "head", None), P(), P(None, "head"), P(None, "head"), P(None, "head"),
            P("head", None), P(), P(None, "head"), P("head", None), P(None, None, "head"),
        ),
        out_specs=P(SEQ, "head"),
        check_vma=False,
    )
```

```python
import functools
import math

import jax
import jax.numpy as jnp
import numpy as np
from jax import lax
from jax.experimental import pallas as pl
from jax.experimental.pallas import tpu as pltpu
from jax.sharding import Mesh
from jax.sharding import PartitionSpec as P

D = 1024
HEAD_DIM = 64
SHORTEN = 4
WINDOW = 1024
BLOCK = 256
HALO = 16
ROWS = 1024
PAST = WINDOW + BLOCK
KEYS = PAST + ROWS
SHARE = 256
COARSE_ROWS = 256
SEQ = ("z", "x", "core")

epsilon = 1e-06
masked_low = -1e30
q_scale = HEAD_DIM ** (-0.5) * math.log2(math.e)
bf16 = jnp.bfloat16
f32 = jnp.float32


def angle_tables():
    lane = np.arange(128) % 32
    period = 2.0 ** (4 + lane * 14 // 32)
    coarse = (256.0 * np.arange(32)[:, None]) % period[None]
    near = np.arange(256)[:, None] % period[None]
    a = coarse * (2.0 * np.pi / period)[None]
    b = near * (2.0 * np.pi / period)[None]
    parts = [np.cos(a), np.sin(a), np.cos(b), np.sin(b)]
    return np.concatenate(parts, axis=0).astype(np.float32)


def shift(value, axis, steps, count):
    return lax.ppermute(value, axis, [(i, (i + steps) % count) for i in range(count)])


def later(value, axis, steps, count):
    return lax.ppermute(value, axis, [(i, i + steps) for i in range(count - steps)])


def exchange(block_for, axis, count):
    me = lax.axis_index(axis)
    got = [block_for(me)]
    for s in range(1, count):
        got.append(shift(block_for((me + s) % count), axis, s, count))
    return got


def dot(left, right):
    return jnp.dot(left, right, preferred_element_type=f32)


def dot_t(left, right):
    return lax.dot_general(left, right, (((1,), (1,)), ((), ())), preferred_element_type=f32)


def norm_rows(data, gain):
    power = jnp.mean(data * data, axis=-1, keepdims=True)
    return (data * lax.rsqrt(power + epsilon) * gain).astype(bf16)


def partner(values):
    width = values.shape[1]
    lane = lax.broadcasted_iota(jnp.int32, values.shape, 1)
    ahead = pltpu.roll(values, width - 32, 1)
    behind = pltpu.roll(values, 32, 1)
    return jnp.where(lane % 64 < 32, -ahead, behind)


def halves(table):
    high = table.astype(bf16)
    low = (table - high.astype(f32)).astype(bf16)
    return high, low


def turn_tables(turn_ref, far):
    ca = turn_ref[pl.ds(far, 1), :]
    sa = turn_ref[pl.ds(32 + far, 1), :]
    cb = turn_ref[64:320, :]
    sb = turn_ref[320:576, :]
    cosine = ca * cb - sa * sb
    sine = sa * cb + ca * sb
    return jnp.concatenate([cosine, cosine], axis=1), jnp.concatenate([sine, sine], axis=1)


def pick(ids, levels=256):
    columns = lax.broadcasted_iota(jnp.int32, (ids.shape[0], levels), 1)
    return (ids == columns).astype(f32).astype(bf16)


def turned_rows(hot, tab_ref, n, cosine, sine):
    return (dot(hot, tab_ref[n]) * cosine + dot(hot, tab_ref[n + 1]) * sine).astype(bf16)


def fine_tables_kernel(
    where_ref, gain_hbm, emb_hbm, wq_hbm, wk_hbm, wv_hbm, fo_hbm,
    tab_hbm, fo_half, tab_ref, gain_ref, emb_ref, w_ref, sems,
):
    pairs = [(emb_hbm, emb_ref), (gain_hbm, gain_ref)]
    for n, w in enumerate((wq_hbm, wk_hbm, wv_hbm)):
        for part in range(2):
            rows = pl.ds(part * 512, 512)
            pairs.append((w.at[rows], w_ref.at[n, rows]))
    half = pl.ds(pl.multiple_of(where_ref[2] * 128, 128), 128)
    pairs.append((fo_hbm.at[half], fo_half))
    copies = begin_copies(pairs, sems)
    finish_copies(copies[:2])
    fine_in = norm_rows(emb_ref[...].astype(f32), gain_ref[...])
    finish_copies(copies[2:8])
    tq = dot(fine_in, w_ref[0]) * q_scale
    tk = dot(fine_in, w_ref[1])
    tables = (tq, partner(tq), tk, partner(tk), dot(fine_in, w_ref[2]))
    for n, table in enumerate(tables):
        tab_ref[n] = table.astype(bf16)
    finish_copies(begin_copies([(tab_ref.at[n], tab_hbm.at[n]) for n in range(5)], sems))
    finish_copies(copies[8:])


def fine_kernel(
    where_ref, before_ref, prior_ref, own_ref, tab_hbm, turn_hbm,
    out_ref, q_ref, k_ref, v_ref, tab_ref, turn_ref, sems,
):
    step = pl.program_id(0)
    lowest = jnp.maximum(PAST - where_ref[0] * ROWS, 0)
    head_lane = lax.broadcasted_iota(jnp.int32, (1, SHARE), 1) // HEAD_DIM

    @pl.when(step == 0)
    def _():
        pairs = [(tab_hbm.at[n], tab_ref.at[n]) for n in range(5)] + [(turn_hbm, turn_ref)]
        finish_copies(begin_copies(pairs, sems))
        cosine, sine = turn_tables(turn_ref, 0)
        oldest = pick(before_ref[...])
        at = slice(BLOCK - HALO, BLOCK)
        k_ref[at, :] = turned_rows(oldest, tab_ref, 2, cosine[at], sine[at])
        v_ref[at, :] = dot(oldest, tab_ref[4]).astype(bf16)

        def build(block, ids, with_q):
            begin = pl.multiple_of(block * BLOCK, BLOCK)
            hot = pick(ids)
            cosine, sine = turn_tables(turn_ref, block)
            k_ref[pl.ds(begin, BLOCK), :] = turned_rows(hot, tab_ref, 2, cosine, sine)
            v_ref[pl.ds(begin, BLOCK), :] = dot(hot, tab_ref[4]).astype(bf16)
            if with_q:
                at = pl.multiple_of(begin - (PAST - BLOCK), BLOCK)
                q_ref[pl.ds(at, BLOCK), :] = turned_rows(hot, tab_ref, 0, cosine, sine)

        def build_from(ref, first, with_q):
            def body(n, _):
                ids = ref[pl.ds(pl.multiple_of(n * BLOCK, BLOCK), BLOCK), :]
                build(first + n, ids, with_q)
                return 0

            return body

        for n in range(3):
            build(1 + n, prior_ref[n * BLOCK : (n + 1) * BLOCK, :], False)
        build(4, prior_ref[3 * BLOCK :, :], True)
        for n in range(4):
            build(5 + n, own_ref[n * BLOCK : (n + 1) * BLOCK, :], True)
        halo_q = q_ref[BLOCK - HALO : BLOCK, :]
        stacked = jnp.concatenate(
            [jnp.where(head_lane == h, halo_q, jnp.zeros_like(halo_q)) for h in range(4)], axis=0
        )
        scores = dot_t(stacked, k_ref[BLOCK - HALO : PAST, :])
        row = lax.broadcasted_iota(jnp.int32, scores.shape, 0) % HALO + (PAST - HALO)
        col = lax.broadcasted_iota(jnp.int32, scores.shape, 1) + (BLOCK - HALO)
        allowed = (col <= row) & (col > row - WINDOW) & (col >= lowest)
        scores = jnp.where(allowed, scores, masked_low)
        top = jnp.max(scores, axis=1, keepdims=True)
        weights = jnp.exp2(scores - top)
        total = jnp.sum(weights, axis=1, keepdims=True)
        mixed = dot(weights.astype(bf16), v_ref[BLOCK - HALO : PAST, :]) / total
        result = jnp.zeros((HALO, SHARE), f32)
        for h in range(4):
            result = jnp.where(head_lane == h, mixed[h * HALO : (h + 1) * HALO], result)
        out_ref[0, 0:HALO, :] = result.astype(bf16)

    for late in range(2):
        place = 2 * step + late
        begin = pl.multiple_of((place + 1) * BLOCK, BLOCK)
        keys = k_ref[pl.ds(begin, PAST), :]
        values = v_ref[pl.ds(begin, PAST), :]
        query = q_ref[pl.ds(begin, BLOCK), :]
        row = lax.broadcasted_iota(jnp.int32, (BLOCK, BLOCK), 0)
        col = lax.broadcasted_iota(jnp.int32, (BLOCK, BLOCK), 1)
        biases = [
            jnp.where(begin + t * BLOCK >= lowest, 0.0, masked_low).astype(f32) for t in range(4)
        ]
        inside = col <= row
        ones = jnp.ones((PAST, 128), bf16)
        low_lanes = lax.broadcasted_iota(jnp.int32, (1, 128), 1) < 64
        results = []

        def score(h):
            return dot_t(jnp.where(head_lane == h, query, jnp.zeros_like(query)), keys)

        ahead = score(0)
        for h in range(4):
            scores = ahead
            if h < 3:
                ahead = score(h + 1)
            tiles = [scores[:, t * BLOCK : (t + 1) * BLOCK] for t in range(5)]
            edge = jnp.where(inside, tiles[4], tiles[0] + biases[0])
            middle = [tiles[t] + biases[t] for t in range(1, 4)]
            peak = edge
            for tile in middle:
                peak = jnp.maximum(peak, tile)
            top = jnp.max(peak, axis=1, keepdims=True)
            edge = jnp.exp2(edge - top).astype(bf16)
            none = jnp.zeros_like(edge)
            weights = [jnp.exp2(tile - top).astype(bf16) for tile in middle]
            weights = [jnp.where(inside, none, edge), *weights, jnp.where(inside, edge, none)]
            pair = (h // 2) * 128
            wide = jnp.concatenate([values[:, pair : pair + 128], ones], axis=1)
            mixed = dot(jnp.concatenate(weights, axis=1), wide)
            results.append(mixed[:, :128] / mixed[:, 128:])
        result = jnp.concatenate(
            [jnp.where(low_lanes, results[2 * n], results[2 * n + 1]) for n in range(2)], axis=1
        )
        result = result.astype(bf16)
        out_ref[place, HALO:, :] = result

        @pl.when(place < 3)
        def _():
            out_ref[place + 1, 0:HALO, :] = result[BLOCK - HALO :]


def vmem():
    return pl.BlockSpec(memory_space=pltpu.VMEM)


def smem():
    return pl.BlockSpec(memory_space=pltpu.SMEM)


def space(shape):
    plain = isinstance(shape, jax.ShapeDtypeStruct)
    return vmem() if plain else pl.BlockSpec(memory_space=pltpu.HBM)


def call(kernel, name, shapes, scalars, arrays, scratch=(), grid=None, limit=16, us=2, hbm=(), free=()):
    one = not isinstance(shapes, (list, tuple))
    extra = {} if grid is None else {"grid": grid}
    return pl.pallas_call(
        kernel,
        out_shape=shapes,
        in_specs=[smem()] * len(scalars)
        + [vmem()] * len(arrays)
        + [pl.BlockSpec(memory_space=pltpu.HBM)] * len(hbm)
        + [pl.BlockSpec(memory_space=pl.ANY)] * len(free),
        out_specs=space(shapes) if one else [space(shape) for shape in shapes],
        scratch_shapes=list(scratch),
        compiler_params=pltpu.CompilerParams(vmem_limit_bytes=limit << 20),
        cost_estimate=pl.CostEstimate(
            flops=us * 10**9, transcendentals=0, bytes_accessed=us * 2 * 10**6
        ),
        name=name,
        **extra,
    )(*scalars, *arrays, *(pltpu.with_memory_space_constraint(a, pltpu.HBM) for a in hbm), *free)


def begin_copies(pairs, sems):
    copies = [pltpu.make_async_copy(a, b, sems.at[n]) for n, (a, b) in enumerate(pairs)]
    for copy in copies:
        copy.start()
    return copies


def finish_copies(copies):
    for copy in copies:
        copy.wait()


def fine_rows_kernel(
    where_ref, ids_ref, emb_ref, got_ref, own_ref, m1, m2, t1, t2, w_hbm,
    out_ref, w_ref, sems,
):
    place, head, core = where_ref[0], where_ref[1], where_ref[2]
    copies = begin_copies([(w_hbm.at[n], w_ref.at[n]) for n in range(4)], sems)
    merged = dot(pick(ids_ref[...]), emb_ref[...]) + dot(got_ref[head], own_ref[...])
    near, far, apart = sources(head, core)
    merged += dot(got_ref[near], m1[...]) + dot(got_ref[far], t1[...])
    at = pl.ds(pl.multiple_of(core * 128, 128), 128)
    merged += dot(got_ref[apart, :, at], m2[...])
    at = pl.ds(pl.multiple_of(128 - core * 128, 128), 128)
    merged += dot(got_ref[apart, :, at], t2[...])
    rows = 256 + HALO
    token = (
        place * ROWS + head * 256 - HALO + lax.broadcasted_iota(jnp.int32, (rows, D), 0)
    )
    fine = jnp.where(token >= 0, merged, 0.0).astype(bf16)
    index = lax.broadcasted_iota(jnp.int32, (256, rows), 0)
    column = lax.broadcasted_iota(jnp.int32, (256, rows), 1)
    source = 4 * (index % 64) + index // 64 + (HALO - 3)
    choose = (source == column).astype(f32).astype(bf16)
    grouped = dot(choose, fine).astype(bf16)
    for d in range(4):
        out_ref[d, 0:256, :] = grouped[:, d * SHARE : (d + 1) * SHARE]
        out_ref[d, 256:rows, :] = fine[256:rows, d * SHARE : (d + 1) * SHARE]
    finish_copies(copies)


def short_part_kernel(group_ref, w_ref, out_ref):
    total = dot(group_ref[0:64, :], w_ref[0])
    for r in range(1, SHORTEN):
        total += dot(group_ref[r * 64 : (r + 1) * 64, :], w_ref[r])
    out_ref[...] = total.astype(bf16)


def coarse_pack_kernel(
    where_ref, s0, s1, s2, s3, gain_ref, wq_ref, wk_ref, wv_ref, turn_ref,
    out_ref, short_ref,
):
    place, head = where_ref[0], where_ref[1]
    for s, ref in enumerate((s0, s1, s2, s3)):
        begin = pl.multiple_of(lax.rem(head - s + 4, 4) * 64, 64)
        short_ref[pl.ds(begin, 64), :] = ref[...]
    x = norm_rows(short_ref[...].astype(f32), gain_ref[...])
    cosine, sine = turn_tables(turn_ref, place)

    def turned(values):
        return values * cosine + partner(values) * sine

    q = turned(dot(x, wq_ref[...])) * q_scale
    k = turned(dot(x, wk_ref[...]))
    v = dot(x, wv_ref[...])
    low_lanes = lax.broadcasted_iota(jnp.int32, (1, 128), 1) < 64
    half = COARSE_ROWS // 2
    for h in range(4):
        pair = (h // 2) * 128
        kp = k[:, pair : pair + 128]
        vp = v[:, pair : pair + 128]
        qp = q[:, pair : pair + 128]
        if h % 2 == 0:
            kv = jnp.where(low_lanes, kp, pltpu.roll(vp, 64, 1))
            qq = jnp.where(low_lanes, qp[:half], pltpu.roll(qp[half:], 64, 1))
        else:
            kv = jnp.where(low_lanes, pltpu.roll(kp, 64, 1), vp)
            qq = jnp.where(low_lanes, pltpu.roll(qp[:half], 64, 1), qp[half:])
        out_ref[h, 0:COARSE_ROWS, :] = kv.astype(bf16)
        out_ref[h, COARSE_ROWS : COARSE_ROWS + half, :] = qq.astype(bf16)


def with_ones(kv):
    return jnp.concatenate([kv, jnp.ones((kv.shape[0], 128), bf16)], axis=1)


def absorb(state, jobs):
    q_ref, top_ref, total_ref, acc_ref = state

    def score(job):
        query = q_ref[pl.ds(job[0], job[1]), :]
        return [dot_t(query, kv) for kv in job[2]]

    ahead = score(jobs[0])
    for n, (begin, rows, parts) in enumerate(jobs):
        scores = ahead
        if n + 1 < len(jobs):
            ahead = score(jobs[n + 1])
        at = pl.ds(begin, rows)
        peak = scores[0]
        for s in scores[1:]:
            peak = jnp.maximum(peak, s)
        old = top_ref[at, :]
        top = jnp.maximum(old, jnp.max(peak, axis=1, keepdims=True))
        factor = jnp.exp2(old - top)
        both = jnp.concatenate([top, top], axis=1)
        contrib = dot(jnp.exp2(scores[0] - both).astype(bf16), with_ones(parts[0]))
        for s, kv in zip(scores[1:], parts[1:]):
            contrib = contrib + dot(jnp.exp2(s - both).astype(bf16), with_ones(kv))
        top_ref[at, :] = top
        total_ref[at, :] = total_ref[at, :] * factor + contrib[:, 128:]
        acc_ref[at, :] = acc_ref[at, :] * factor + contrib[:, :128]


def coarse_first_kernel(flag_ref, turned_ref, far_ref, q_ref, top_ref, total_ref, acc_ref):
    half = COARSE_ROWS // 2
    low_lanes = lax.broadcasted_iota(jnp.int32, (1, 128), 1) < 64
    row = lax.broadcasted_iota(jnp.int32, (256, 256), 0)
    col = lax.broadcasted_iota(jnp.int32, (256, 256), 1)
    for z in range(4):
        packed = turned_ref[z, COARSE_ROWS:, :].astype(f32)
        zero = jnp.zeros_like(packed)
        q_ref[z * 256 : z * 256 + half, :] = jnp.where(low_lanes, packed, zero).astype(bf16)
        q_ref[z * 256 + half : (z + 1) * 256, :] = jnp.where(
            low_lanes, pltpu.roll(packed, 64, 1), zero
        ).astype(bf16)
        kv = turned_ref[z, :COARSE_ROWS, :]
        at = pl.ds(z * 256, 256)
        scores = jnp.where(col <= row, dot_t(q_ref[at, :], kv), masked_low)
        top = jnp.max(scores, axis=1, keepdims=True)
        contrib = dot(jnp.exp2(scores - top).astype(bf16), with_ones(kv))
        top_ref[at, :] = jnp.broadcast_to(top, (256, 128))
        total_ref[at, :] = contrib[:, 128:]
        acc_ref[at, :] = contrib[:, :128]
    state = (q_ref, top_ref, total_ref, acc_ref)
    absorb(
        state,
        [
            ((z + 1) * 256, (3 - z) * 256, [turned_ref[z, :COARSE_ROWS, :], far_ref[z]])
            for z in range(3)
        ],
    )

    @pl.when(flag_ref[0] > 0)
    def _():
        absorb(state, [(z * 256, 256, [far_ref[z]]) for z in range(4)])


def coarse_more_kernel(which, last, flag_ref, *refs):
    count = 2 * len(which)
    sems = refs[-1]
    refs = refs[:-1]
    chunks = refs[:count]
    q_ref, top_in, total_in, acc_in = refs[count : count + 4]
    refs = refs[count + 4 :]
    top_ref, total_ref, acc_ref = refs[-3:]
    if last:
        own, m1, m2, t1, t2, target, out_ref = refs[:-3]
        pairs = place_copies(flag_ref[4], flag_ref[5], own, (m1, m2), (t1, t2), target)
    else:
        pairs = []
        for a, b in zip(refs[:2], refs[2:4]):
            for part in range(4):
                at = pl.ds(part * 256, 256)
                pairs.append((a.at[at], b.at[at]))
    copies = begin_copies(pairs, sems)
    top_ref[...] = top_in[...]
    total_ref[...] = total_in[...]
    acc_ref[...] = acc_in[...]
    state = (q_ref, top_ref, total_ref, acc_ref)
    pairs_of = [(chunks[2 * n], chunks[2 * n + 1]) for n in range(len(which))]
    absorb(
        state,
        [
            ((z + 1) * 256, (3 - z) * 256, [near[z], far[z]])
            for near, far in pairs_of
            for z in range(3)
        ],
    )
    for s, (near, far) in zip(which, pairs_of):

        @pl.when(flag_ref[s] > 0)
        def _(near=near, far=far):
            absorb(state, [(z * 256, 256, [near[z], far[z]]) for z in range(4)])

    if last:
        mixed = acc_ref[...] / total_ref[...]
        low_lanes = lax.broadcasted_iota(jnp.int32, (1, 128), 1) < 64
        for z in range(4):
            upper = pltpu.roll(mixed[z * 256 : z * 256 + 128], 64, 1)
            lower = mixed[z * 256 + 128 : (z + 1) * 256]
            block = jnp.where(low_lanes, upper, lower).astype(bf16)
            for y in range(4):
                out_ref[z * 4 + y] = block
    finish_copies(copies)


def feed_kernel(
    where_ref, heads_ref, short_ref, gain_ref, co_ref, up_ref, down_ref,
    part_ref, first_ref, mixed_ref, all_ref,
):
    head = where_ref[1]
    low_lanes = lax.broadcasted_iota(jnp.int32, (1, 128), 1) < 64
    for y in range(4):
        for pair in range(2):
            even = heads_ref[2 * pair * 4 + y].astype(f32)
            odd = heads_ref[(2 * pair + 1) * 4 + y].astype(f32)
            at = slice(y * 256 + pair * 128, y * 256 + (pair + 1) * 128)
            mixed_ref[0:128, at] = jnp.where(low_lanes, even, pltpu.roll(odd, 64, 1)).astype(bf16)
            mixed_ref[128:256, at] = jnp.where(low_lanes, pltpu.roll(even, 64, 1), odd).astype(bf16)
    first = short_ref[...].astype(f32) + dot(mixed_ref[...], co_ref[...])
    all_ref[...] = first
    first_ref[...] = all_ref[pl.ds(pl.multiple_of(head * 64, 64), 64), :]
    feed = norm_rows(first, gain_ref[...])
    inner = jax.nn.gelu(dot(feed, up_ref[...])).astype(bf16)
    part_ref[...] = dot(inner, down_ref[...]).astype(bf16).reshape(4, 64, D)


def final_kernel(where_ref, s0, s1, s2, s3, b0, b1, b2, b3, up_ref, out_ref):
    head = where_ref[1]
    rows = 256 + HALO
    second = jnp.concatenate([ref[...] for ref in (s0, s1, s2, s3)], axis=0)
    lifted = dot(second, up_ref[...])
    index = lax.broadcasted_iota(jnp.int32, (256, rows), 0)
    column = lax.broadcasted_iota(jnp.int32, (256, rows), 1)
    r, m = index // 64, index % 64
    source = jnp.where(r == 0, 192 + m, jnp.where(m == 63, 268 + r, (r - 1) * 64 + m + 1))
    choose = (source == column).astype(f32).astype(bf16)
    index = lax.broadcasted_iota(jnp.int32, (256, 256), 0)
    column = lax.broadcasted_iota(jnp.int32, (256, 256), 1)
    weave = ((index % 4) * 64 + index // 4 == column).astype(f32).astype(bf16)
    for s, block in enumerate((b0, b1, b2, b3)):
        mine = lifted[s * 64 : (s + 1) * 64]
        raised = jnp.concatenate([mine[:, q * SHARE : (q + 1) * SHARE] for q in range(4)], axis=0)
        value = (dot(choose, block[...]) + raised).astype(bf16)
        begin = pl.multiple_of(lax.rem(head - s + 4, 4) * 256, 256)
        out_ref[pl.ds(begin, 256), :] = dot(weave, value).astype(bf16)


def fetch_rest(weight, half):
    pairs = []
    for c, step in ((0, 1), (1, 3)):
        pairs += [(4 * c + y, 4 * c + (y + step) % 4) for y in range(4)]
    whole = lax.ppermute(weight, ("core", "head"), pairs)
    return [whole, shift(half, "head", 2, 4)]


def swap_cores(parts):
    return [shift(part, "core", 1, 2) for part in parts]


def sources(head, core):
    mine = lax.rem(head + 3 - 2 * core, 4)
    other = lax.rem(head + 1 + 2 * core, 4)
    return mine, other, lax.rem(head + 2, 4)


def place_copies(head, core, own, mine, other, target):
    near, far, apart = sources(head, core)
    halves_at = apart * 256
    return [
        (own, target.at[pl.ds(pl.multiple_of(head * 256, 256), 256)]),
        (mine[0], target.at[pl.ds(pl.multiple_of(near * 256, 256), 256)]),
        (other[0], target.at[pl.ds(pl.multiple_of(far * 256, 256), 256)]),
        (mine[1], target.at[pl.ds(pl.multiple_of(halves_at + core * 128, 128), 128)]),
        (other[1], target.at[pl.ds(pl.multiple_of(halves_at + 128 - core * 128, 128), 128)]),
    ]


def after(value, gate):
    return lax.optimization_barrier((value, gate))


def local(
    token_ids, embedding, fine_norm, fine_query, fine_key, fine_value, fine_output,
    shorten_weight, coarse_norm, coarse_query, coarse_key, coarse_value, coarse_output,
    ffn_norm, ffn_up, ffn_down, upsample_weight,
):
    place = lax.axis_index(SEQ).astype(jnp.int32)
    head = lax.axis_index("head").astype(jnp.int32)
    x_place = lax.axis_index("x").astype(jnp.int32)
    core = lax.axis_index("core").astype(jnp.int32)
    tables = jnp.asarray(angle_tables())
    where = jnp.stack([place, head, core])

    prior = later(token_ids, SEQ, 1, 32)
    before = later(token_ids, SEQ, 2, 32)[ROWS - HALO :]
    tab, fo_half = call(
        fine_tables_kernel, "fine_tables",
        [pltpu.HBM((5, 256, SHARE), bf16), pltpu.HBM((128, D), bf16)], [where], [],
        [
            pltpu.VMEM((5, 256, SHARE), bf16),
            pltpu.VMEM((1, D), f32), pltpu.VMEM((256, D), bf16),
            pltpu.VMEM((3, D, SHARE), bf16), pltpu.SemaphoreType.DMA((9,)),
        ],
        us=3, hbm=[
            fine_norm[None], embedding, fine_query, fine_key, fine_value,
            fine_output,
        ],
    )
    own_ids_column = token_ids[:, None]
    fine_output_held, own_ids_column = after(fine_output, own_ids_column)
    out_mine = fetch_rest(fine_output_held, fo_half)
    rows = 256 + HALO
    mixed = call(
        fine_kernel, "fine_attention", jax.ShapeDtypeStruct((4, rows, SHARE), bf16),
        [where], [before[:, None], prior[:, None], own_ids_column],
        [
            pltpu.VMEM((BLOCK + ROWS, SHARE), bf16),
            pltpu.VMEM((KEYS, SHARE), bf16), pltpu.VMEM((KEYS, SHARE), bf16),
            pltpu.VMEM((5, 256, SHARE), bf16), pltpu.VMEM((576, 128), f32),
            pltpu.SemaphoreType.DMA((10,)),
        ],
        grid=(2,), us=12, limit=24, hbm=[tab, tables],
    )

    out_mine, mixed = after(out_mine, mixed)
    got = lax.all_to_all(mixed, "head", 0, 0)
    out_other = swap_cores(out_mine)
    own_ids = lax.dynamic_slice_in_dim(
        jnp.concatenate([prior[ROWS - HALO :], token_ids]), head * 256, rows, 0
    )
    sends, shorten_near = call(
        fine_rows_kernel, "fine_rows",
        [
            jax.ShapeDtypeStruct((4, rows, SHARE), bf16),
            jax.ShapeDtypeStruct((SHORTEN, SHARE, D), bf16),
        ],
        [where],
        [own_ids[:, None], embedding, got, fine_output, *out_mine, *out_other],
        [pltpu.SemaphoreType.DMA((4,))], hbm=[shorten_weight],
    )
    blocks = exchange(lambda d: lax.dynamic_index_in_dim(sends, d, 0, keepdims=False), "head", 4)

    terms = []
    for s, block in enumerate(blocks):
        part = call(
            short_part_kernel, "short_part", jax.ShapeDtypeStruct((64, D), bf16), [],
            [block, shorten_near],
        )
        terms.append(part if s == 0 else shift(part, "head", 4 - s, 4))
    short_own = sum(t.astype(f32) for t in terms).astype(bf16)
    shorts = [short_own] + [shift(short_own, "head", s, 4) for s in range(1, 4)]
    packed, short = call(
        coarse_pack_kernel, "coarse_pack",
        [
            jax.ShapeDtypeStruct((4, COARSE_ROWS * 3 // 2, 128), bf16),
            jax.ShapeDtypeStruct((COARSE_ROWS, D), bf16),
        ],
        [where],
        [*shorts, coarse_norm[None], coarse_query, coarse_key, coarse_value, tables],
    )

    coarse_output_held, packed = after(coarse_output, packed)
    co_half = lax.dynamic_slice_in_dim(coarse_output_held, core * 128, 128, 0)
    co_mine = fetch_rest(coarse_output_held, co_half)
    turned = lax.all_to_all(packed, "z", 0, 0)
    kv = turned[:, :COARSE_ROWS]
    far = [shift(kv, "core", 1, 2)]
    near = [shift(kv, "x", s, 4) for s in range(1, 4)]
    steps = jnp.arange(4, dtype=jnp.int32)
    flags = ((x_place - steps + 4) % 4 < x_place).astype(jnp.int32) + (steps == 0) * core
    flags = jnp.concatenate([flags, where[1:]])
    wide = jax.ShapeDtypeStruct((1024, 128), f32)
    q_all, *sums = call(
        coarse_first_kernel, "coarse_first",
        [jax.ShapeDtypeStruct((1024, 128), bf16), wide, wide, wide], [flags], [turned, far[0]],
        us=3, limit=24,
    )
    near_held, co_held, q_all = lax.optimization_barrier((near, co_mine, q_all))
    far += [shift(part, "core", 1, 2) for part in near_held]
    co_other = swap_cores(co_held)
    square = jax.ShapeDtypeStruct((D, D), bf16)
    up_near, down_near, *sums = call(
        functools.partial(coarse_more_kernel, (1, 3), False), "coarse_more",
        [square, square, wide, wide, wide],
        [flags], [near[0], far[1], near[2], far[3], q_all, *sums],
        [pltpu.SemaphoreType.DMA((8,))], us=6, limit=24, hbm=[ffn_up, ffn_down],
    )
    output_near, wide_sends = call(
        functools.partial(coarse_more_kernel, (2,), True), "coarse_last",
        [square, jax.ShapeDtypeStruct((16, 128, 128), bf16)],
        [flags], [near[1], far[2], q_all, *sums],
        [pltpu.VMEM((1024, 128), f32)] * 3 + [pltpu.SemaphoreType.DMA((5,))],
        us=3, limit=24, hbm=[coarse_output], free=[*co_mine, *co_other],
    )

    heads_in = lax.all_to_all(wide_sends, ("z", "head"), 0, 0)
    parts, first_own = call(
        feed_kernel, "feed",
        [jax.ShapeDtypeStruct((4, 64, D), bf16), jax.ShapeDtypeStruct((64, D), f32)],
        [where],
        [heads_in, short, ffn_norm[None], output_near, up_near, down_near],
        [
            pltpu.VMEM((COARSE_ROWS, D), bf16), pltpu.VMEM((COARSE_ROWS, D), f32),
        ],
        us=4,
    )
    sums = exchange(lambda d: lax.dynamic_index_in_dim(parts, d, 0, keepdims=False), "head", 4)
    second_own = (first_own + sum(t.astype(f32) for t in sums)).astype(bf16)
    seconds = [second_own] + [shift(second_own, "head", s, 4) for s in range(1, 4)]
    return call(
        final_kernel, "final", jax.ShapeDtypeStruct((ROWS, SHARE), bf16),
        [where], [*seconds, *blocks, upsample_weight.reshape(D, SHORTEN * SHARE)],
    )


def solution(mesh):
    split = Mesh(mesh.devices.reshape(4, 4, 2, 4), ("z", "x", "core", "head"))
    return jax.shard_map(
        local,
        mesh=split,
        in_specs=(
            P(SEQ), P(), P(), P(None, "head"), P(None, "head"), P(None, "head"), P("head", None),
            P(None, "head", None), P(), P(None, "head"), P(None, "head"), P(None, "head"),
            P("head", None), P(), P(None, "head"), P("head", None), P(None, None, "head"),
        ),
        out_specs=P(SEQ, "head"),
        check_vma=False,
    )
```

```python
import functools
import math

import jax
import jax.numpy as jnp
import numpy as np
from jax import lax
from jax.experimental import pallas as pl
from jax.experimental.pallas import tpu as pltpu
from jax.sharding import Mesh
from jax.sharding import PartitionSpec as P

D = 1024
HEAD_DIM = 64
SHORTEN = 4
WINDOW = 1024
BLOCK = 256
HALO = 16
ROWS = 1024
PAST = WINDOW + BLOCK
KEYS = PAST + ROWS
SHARE = 256
COARSE_ROWS = 256
SEQ = ("z", "x", "core")

epsilon = 1e-06
masked_low = -1e30
q_scale = HEAD_DIM ** (-0.5) * math.log2(math.e)
bf16 = jnp.bfloat16
f32 = jnp.float32


def angle_tables():
    lane = np.arange(128) % 32
    period = 2.0 ** (4 + lane * 14 // 32)
    coarse = (256.0 * np.arange(32)[:, None]) % period[None]
    near = np.arange(256)[:, None] % period[None]
    a = coarse * (2.0 * np.pi / period)[None]
    b = near * (2.0 * np.pi / period)[None]
    parts = [np.cos(a), np.sin(a), np.cos(b), np.sin(b)]
    return np.concatenate(parts, axis=0).astype(np.float32)


def shift(value, axis, steps, count):
    return lax.ppermute(value, axis, [(i, (i + steps) % count) for i in range(count)])


def later(value, axis, steps, count):
    return lax.ppermute(value, axis, [(i, i + steps) for i in range(count - steps)])


def exchange(block_for, axis, count):
    me = lax.axis_index(axis)
    got = [block_for(me)]
    for s in range(1, count):
        got.append(shift(block_for((me + s) % count), axis, s, count))
    return got


def dot(left, right):
    return jnp.dot(left, right, preferred_element_type=f32)


def dot_t(left, right):
    return lax.dot_general(left, right, (((1,), (1,)), ((), ())), preferred_element_type=f32)


def norm_rows(data, gain):
    power = jnp.mean(data * data, axis=-1, keepdims=True)
    return (data * lax.rsqrt(power + epsilon) * gain).astype(bf16)


def partner(values):
    width = values.shape[1]
    lane = lax.broadcasted_iota(jnp.int32, values.shape, 1)
    ahead = pltpu.roll(values, width - 32, 1)
    behind = pltpu.roll(values, 32, 1)
    return jnp.where(lane % 64 < 32, -ahead, behind)


def halves(table):
    high = table.astype(bf16)
    low = (table - high.astype(f32)).astype(bf16)
    return high, low


def turn_tables(turn_ref, far):
    ca = turn_ref[pl.ds(far, 1), :]
    sa = turn_ref[pl.ds(32 + far, 1), :]
    cb = turn_ref[64:320, :]
    sb = turn_ref[320:576, :]
    cosine = ca * cb - sa * sb
    sine = sa * cb + ca * sb
    return jnp.concatenate([cosine, cosine], axis=1), jnp.concatenate([sine, sine], axis=1)


def pick(ids, levels=256):
    columns = lax.broadcasted_iota(jnp.int32, (ids.shape[0], levels), 1)
    return (ids == columns).astype(f32).astype(bf16)


def turned_rows(hot, tab_ref, n, cosine, sine):
    return (dot(hot, tab_ref[n]) * cosine + dot(hot, tab_ref[n + 1]) * sine).astype(bf16)


def fine_tables_kernel(
    where_ref, gain_hbm, emb_hbm, wq_hbm, wk_hbm, wv_hbm, fo_hbm,
    tab_hbm, fo_half, tab_ref, gain_ref, emb_ref, w_ref, half_ref, sems,
):
    pairs = [(emb_hbm, emb_ref), (gain_hbm, gain_ref)]
    for n, w in enumerate((wq_hbm, wk_hbm, wv_hbm)):
        for part in range(2):
            rows = pl.ds(part * 512, 512)
            pairs.append((w.at[rows], w_ref.at[n, rows]))
    half = pl.ds(pl.multiple_of(where_ref[2] * 128, 128), 128)
    pairs.append((fo_hbm.at[half], half_ref))
    copies = begin_copies(pairs, sems)
    finish_copies(copies[:2])
    fine_in = norm_rows(emb_ref[...].astype(f32), gain_ref[...])
    finish_copies(copies[2:8])
    finish_copies(copies[8:])
    out = pltpu.make_async_copy(half_ref, fo_half, sems.at[9])
    out.start()
    tq = dot(fine_in, w_ref[0]) * q_scale
    tk = dot(fine_in, w_ref[1])
    tables = (tq, partner(tq), tk, partner(tk), dot(fine_in, w_ref[2]))
    for n, table in enumerate(tables):
        tab_ref[n] = table.astype(bf16)
    finish_copies(begin_copies([(tab_ref.at[n], tab_hbm.at[n]) for n in range(5)], sems))
    out.wait()


def fine_kernel(
    where_ref, before_ref, prior_ref, own_ref, tab_hbm, turn_hbm,
    out_ref, q_ref, k_ref, v_ref, tab_ref, turn_ref, sems,
):
    step = pl.program_id(0)
    lowest = jnp.maximum(PAST - where_ref[0] * ROWS, 0)
    head_lane = lax.broadcasted_iota(jnp.int32, (1, SHARE), 1) // HEAD_DIM

    @pl.when(step == 0)
    def _():
        pairs = [(tab_hbm.at[n], tab_ref.at[n]) for n in range(5)] + [(turn_hbm, turn_ref)]
        finish_copies(begin_copies(pairs, sems))
        cosine, sine = turn_tables(turn_ref, 0)
        oldest = pick(before_ref[...])
        at = slice(BLOCK - HALO, BLOCK)
        k_ref[at, :] = turned_rows(oldest, tab_ref, 2, cosine[at], sine[at])
        v_ref[at, :] = dot(oldest, tab_ref[4]).astype(bf16)

        def build(block, ids, with_q):
            begin = pl.multiple_of(block * BLOCK, BLOCK)
            hot = pick(ids)
            cosine, sine = turn_tables(turn_ref, block)
            k_ref[pl.ds(begin, BLOCK), :] = turned_rows(hot, tab_ref, 2, cosine, sine)
            v_ref[pl.ds(begin, BLOCK), :] = dot(hot, tab_ref[4]).astype(bf16)
            if with_q:
                at = pl.multiple_of(begin - (PAST - BLOCK), BLOCK)
                q_ref[pl.ds(at, BLOCK), :] = turned_rows(hot, tab_ref, 0, cosine, sine)

        def build_from(ref, first, with_q):
            def body(n, _):
                ids = ref[pl.ds(pl.multiple_of(n * BLOCK, BLOCK), BLOCK), :]
                build(first + n, ids, with_q)
                return 0

            return body

        for n in range(3):
            build(1 + n, prior_ref[n * BLOCK : (n + 1) * BLOCK, :], False)
        build(4, prior_ref[3 * BLOCK :, :], True)
        for n in range(4):
            build(5 + n, own_ref[n * BLOCK : (n + 1) * BLOCK, :], True)
        halo_q = q_ref[BLOCK - HALO : BLOCK, :]
        stacked = jnp.concatenate(
            [jnp.where(head_lane == h, halo_q, jnp.zeros_like(halo_q)) for h in range(4)], axis=0
        )
        scores = dot_t(stacked, k_ref[BLOCK - HALO : PAST, :])
        row = lax.broadcasted_iota(jnp.int32, scores.shape, 0) % HALO + (PAST - HALO)
        col = lax.broadcasted_iota(jnp.int32, scores.shape, 1) + (BLOCK - HALO)
        allowed = (col <= row) & (col > row - WINDOW) & (col >= lowest)
        scores = jnp.where(allowed, scores, masked_low)
        top = jnp.max(scores, axis=1, keepdims=True)
        weights = jnp.exp2(scores - top)
        total = jnp.sum(weights, axis=1, keepdims=True)
        mixed = dot(weights.astype(bf16), v_ref[BLOCK - HALO : PAST, :]) / total
        result = jnp.zeros((HALO, SHARE), f32)
        for h in range(4):
            result = jnp.where(head_lane == h, mixed[h * HALO : (h + 1) * HALO], result)
        out_ref[0, 0:HALO, :] = result.astype(bf16)

    for late in range(2):
        place = 2 * step + late
        begin = pl.multiple_of((place + 1) * BLOCK, BLOCK)
        keys = k_ref[pl.ds(begin, PAST), :]
        values = v_ref[pl.ds(begin, PAST), :]
        query = q_ref[pl.ds(begin, BLOCK), :]
        row = lax.broadcasted_iota(jnp.int32, (BLOCK, BLOCK), 0)
        col = lax.broadcasted_iota(jnp.int32, (BLOCK, BLOCK), 1)
        biases = [
            jnp.where(begin + t * BLOCK >= lowest, 0.0, masked_low).astype(f32) for t in range(4)
        ]
        inside = col <= row
        ones = jnp.ones((PAST, 128), bf16)
        low_lanes = lax.broadcasted_iota(jnp.int32, (1, 128), 1) < 64
        results = []

        def score(h):
            return dot_t(jnp.where(head_lane == h, query, jnp.zeros_like(query)), keys)

        ahead = score(0)
        for h in range(4):
            scores = ahead
            if h < 3:
                ahead = score(h + 1)
            tiles = [scores[:, t * BLOCK : (t + 1) * BLOCK] for t in range(5)]
            edge = jnp.where(inside, tiles[4], tiles[0] + biases[0])
            middle = [tiles[t] + biases[t] for t in range(1, 4)]
            peak = edge
            for tile in middle:
                peak = jnp.maximum(peak, tile)
            top = jnp.max(peak, axis=1, keepdims=True)
            edge = jnp.exp2(edge - top).astype(bf16)
            none = jnp.zeros_like(edge)
            weights = [jnp.exp2(tile - top).astype(bf16) for tile in middle]
            weights = [jnp.where(inside, none, edge), *weights, jnp.where(inside, edge, none)]
            pair = (h // 2) * 128
            wide = jnp.concatenate([values[:, pair : pair + 128], ones], axis=1)
            mixed = dot(jnp.concatenate(weights, axis=1), wide)
            results.append(mixed[:, :128] / mixed[:, 128:])
        result = jnp.concatenate(
            [jnp.where(low_lanes, results[2 * n], results[2 * n + 1]) for n in range(2)], axis=1
        )
        result = result.astype(bf16)
        out_ref[place, HALO:, :] = result

        @pl.when(place < 3)
        def _():
            out_ref[place + 1, 0:HALO, :] = result[BLOCK - HALO :]


def vmem():
    return pl.BlockSpec(memory_space=pltpu.VMEM)


def smem():
    return pl.BlockSpec(memory_space=pltpu.SMEM)


def space(shape):
    plain = isinstance(shape, jax.ShapeDtypeStruct)
    return vmem() if plain else pl.BlockSpec(memory_space=pltpu.HBM)


def call(kernel, name, shapes, scalars, arrays, scratch=(), grid=None, limit=16, us=2, hbm=(), free=()):
    one = not isinstance(shapes, (list, tuple))
    extra = {} if grid is None else {"grid": grid}
    return pl.pallas_call(
        kernel,
        out_shape=shapes,
        in_specs=[smem()] * len(scalars)
        + [vmem()] * len(arrays)
        + [pl.BlockSpec(memory_space=pltpu.HBM)] * len(hbm)
        + [pl.BlockSpec(memory_space=pl.ANY)] * len(free),
        out_specs=space(shapes) if one else [space(shape) for shape in shapes],
        scratch_shapes=list(scratch),
        compiler_params=pltpu.CompilerParams(vmem_limit_bytes=limit << 20),
        cost_estimate=pl.CostEstimate(
            flops=us * 10**9, transcendentals=0, bytes_accessed=us * 2 * 10**6
        ),
        name=name,
        **extra,
    )(*scalars, *arrays, *(pltpu.with_memory_space_constraint(a, pltpu.HBM) for a in hbm), *free)


def begin_copies(pairs, sems):
    copies = [pltpu.make_async_copy(a, b, sems.at[n]) for n, (a, b) in enumerate(pairs)]
    for copy in copies:
        copy.start()
    return copies


def finish_copies(copies):
    for copy in copies:
        copy.wait()


def fine_rows_kernel(
    where_ref, ids_ref, emb_ref, got_ref, own_ref, m1, m2, t1, t2, w_hbm,
    out_ref, w_ref, sems,
):
    place, head, core = where_ref[0], where_ref[1], where_ref[2]
    copies = begin_copies([(w_hbm.at[n], w_ref.at[n]) for n in range(4)], sems)
    merged = dot(pick(ids_ref[...]), emb_ref[...]) + dot(got_ref[head], own_ref[...])
    near, far, apart = sources(head, core)
    merged += dot(got_ref[near], m1[...]) + dot(got_ref[far], t1[...])
    at = pl.ds(pl.multiple_of(core * 128, 128), 128)
    merged += dot(got_ref[apart, :, at], m2[...])
    at = pl.ds(pl.multiple_of(128 - core * 128, 128), 128)
    merged += dot(got_ref[apart, :, at], t2[...])
    rows = 256 + HALO
    token = (
        place * ROWS + head * 256 - HALO + lax.broadcasted_iota(jnp.int32, (rows, D), 0)
    )
    fine = jnp.where(token >= 0, merged, 0.0).astype(bf16)
    index = lax.broadcasted_iota(jnp.int32, (256, rows), 0)
    column = lax.broadcasted_iota(jnp.int32, (256, rows), 1)
    source = 4 * (index % 64) + index // 64 + (HALO - 3)
    choose = (source == column).astype(f32).astype(bf16)
    grouped = dot(choose, fine).astype(bf16)
    for d in range(4):
        out_ref[d, 0:256, :] = grouped[:, d * SHARE : (d + 1) * SHARE]
        out_ref[d, 256:rows, :] = fine[256:rows, d * SHARE : (d + 1) * SHARE]
    finish_copies(copies)


def short_part_kernel(group_ref, w_ref, out_ref):
    total = dot(group_ref[0:64, :], w_ref[0])
    for r in range(1, SHORTEN):
        total += dot(group_ref[r * 64 : (r + 1) * 64, :], w_ref[r])
    out_ref[...] = total.astype(bf16)


def coarse_pack_kernel(
    where_ref, s0, s1, s2, s3, gain_ref, wq_ref, wk_ref, wv_ref, turn_ref,
    out_ref, short_ref,
):
    place, head = where_ref[0], where_ref[1]
    for s, ref in enumerate((s0, s1, s2, s3)):
        begin = pl.multiple_of(lax.rem(head - s + 4, 4) * 64, 64)
        short_ref[pl.ds(begin, 64), :] = ref[...]
    x = norm_rows(short_ref[...].astype(f32), gain_ref[...])
    cosine, sine = turn_tables(turn_ref, place)

    def turned(values):
        return values * cosine + partner(values) * sine

    q = turned(dot(x, wq_ref[...])) * q_scale
    k = turned(dot(x, wk_ref[...]))
    v = dot(x, wv_ref[...])
    low_lanes = lax.broadcasted_iota(jnp.int32, (1, 128), 1) < 64
    half = COARSE_ROWS // 2
    for h in range(4):
        pair = (h // 2) * 128
        kp = k[:, pair : pair + 128]
        vp = v[:, pair : pair + 128]
        qp = q[:, pair : pair + 128]
        if h % 2 == 0:
            kv = jnp.where(low_lanes, kp, pltpu.roll(vp, 64, 1))
            qq = jnp.where(low_lanes, qp[:half], pltpu.roll(qp[half:], 64, 1))
        else:
            kv = jnp.where(low_lanes, pltpu.roll(kp, 64, 1), vp)
            qq = jnp.where(low_lanes, pltpu.roll(qp[:half], 64, 1), qp[half:])
        out_ref[h, 0:COARSE_ROWS, :] = kv.astype(bf16)
        out_ref[h, COARSE_ROWS : COARSE_ROWS + half, :] = qq.astype(bf16)


def with_ones(kv):
    return jnp.concatenate([kv, jnp.ones((kv.shape[0], 128), bf16)], axis=1)


def absorb(state, jobs):
    q_ref, top_ref, total_ref, acc_ref = state

    def score(job):
        query = q_ref[pl.ds(job[0], job[1]), :]
        return [dot_t(query, kv) for kv in job[2]]

    ahead = score(jobs[0])
    for n, (begin, rows, parts) in enumerate(jobs):
        scores = ahead
        if n + 1 < len(jobs):
            ahead = score(jobs[n + 1])
        at = pl.ds(begin, rows)
        peak = scores[0]
        for s in scores[1:]:
            peak = jnp.maximum(peak, s)
        old = top_ref[at, :]
        top = jnp.maximum(old, jnp.max(peak, axis=1, keepdims=True))
        factor = jnp.exp2(old - top)
        both = jnp.concatenate([top, top], axis=1)
        contrib = dot(jnp.exp2(scores[0] - both).astype(bf16), with_ones(parts[0]))
        for s, kv in zip(scores[1:], parts[1:]):
            contrib = contrib + dot(jnp.exp2(s - both).astype(bf16), with_ones(kv))
        top_ref[at, :] = top
        total_ref[at, :] = total_ref[at, :] * factor + contrib[:, 128:]
        acc_ref[at, :] = acc_ref[at, :] * factor + contrib[:, :128]


def coarse_first_kernel(flag_ref, turned_ref, far_ref, q_ref, top_ref, total_ref, acc_ref):
    half = COARSE_ROWS // 2
    low_lanes = lax.broadcasted_iota(jnp.int32, (1, 128), 1) < 64
    row = lax.broadcasted_iota(jnp.int32, (256, 256), 0)
    col = lax.broadcasted_iota(jnp.int32, (256, 256), 1)
    for z in range(4):
        packed = turned_ref[z, COARSE_ROWS:, :].astype(f32)
        zero = jnp.zeros_like(packed)
        q_ref[z * 256 : z * 256 + half, :] = jnp.where(low_lanes, packed, zero).astype(bf16)
        q_ref[z * 256 + half : (z + 1) * 256, :] = jnp.where(
            low_lanes, pltpu.roll(packed, 64, 1), zero
        ).astype(bf16)
        kv = turned_ref[z, :COARSE_ROWS, :]
        at = pl.ds(z * 256, 256)
        scores = jnp.where(col <= row, dot_t(q_ref[at, :], kv), masked_low)
        top = jnp.max(scores, axis=1, keepdims=True)
        contrib = dot(jnp.exp2(scores - top).astype(bf16), with_ones(kv))
        top_ref[at, :] = jnp.broadcast_to(top, (256, 128))
        total_ref[at, :] = contrib[:, 128:]
        acc_ref[at, :] = contrib[:, :128]
    state = (q_ref, top_ref, total_ref, acc_ref)
    absorb(
        state,
        [
            ((z + 1) * 256, (3 - z) * 256, [turned_ref[z, :COARSE_ROWS, :], far_ref[z]])
            for z in range(3)
        ],
    )

    @pl.when(flag_ref[0] > 0)
    def _():
        absorb(state, [(z * 256, 256, [far_ref[z]]) for z in range(4)])


def coarse_more_kernel(which, last, flag_ref, *refs):
    count = 2 * len(which)
    sems = refs[-1]
    refs = refs[:-1]
    chunks = refs[:count]
    q_ref, top_in, total_in, acc_in = refs[count : count + 4]
    refs = refs[count + 4 :]
    top_ref, total_ref, acc_ref = refs[-3:]
    if last:
        own, m1, m2, t1, t2, target, out_ref = refs[:-3]
        pairs = place_copies(flag_ref[4], flag_ref[5], own, (m1, m2), (t1, t2), target)
    else:
        pairs = []
        for a, b in zip(refs[:2], refs[2:4]):
            for part in range(4):
                at = pl.ds(part * 256, 256)
                pairs.append((a.at[at], b.at[at]))
    copies = begin_copies(pairs, sems)
    top_ref[...] = top_in[...]
    total_ref[...] = total_in[...]
    acc_ref[...] = acc_in[...]
    state = (q_ref, top_ref, total_ref, acc_ref)
    pairs_of = [(chunks[2 * n], chunks[2 * n + 1]) for n in range(len(which))]
    absorb(
        state,
        [
            ((z + 1) * 256, (3 - z) * 256, [near[z], far[z]])
            for near, far in pairs_of
            for z in range(3)
        ],
    )
    for s, (near, far) in zip(which, pairs_of):

        @pl.when(flag_ref[s] > 0)
        def _(near=near, far=far):
            absorb(state, [(z * 256, 256, [near[z], far[z]]) for z in range(4)])

    if last:
        mixed = acc_ref[...] / total_ref[...]
        low_lanes = lax.broadcasted_iota(jnp.int32, (1, 128), 1) < 64
        for z in range(4):
            upper = pltpu.roll(mixed[z * 256 : z * 256 + 128], 64, 1)
            lower = mixed[z * 256 + 128 : (z + 1) * 256]
            block = jnp.where(low_lanes, upper, lower).astype(bf16)
            for y in range(4):
                out_ref[z * 4 + y] = block
    finish_copies(copies)


def feed_kernel(
    where_ref, heads_ref, short_ref, gain_ref, co_ref, up_ref, down_ref,
    part_ref, first_ref, mixed_ref, all_ref,
):
    head = where_ref[1]
    low_lanes = lax.broadcasted_iota(jnp.int32, (1, 128), 1) < 64
    for y in range(4):
        for pair in range(2):
            even = heads_ref[2 * pair * 4 + y].astype(f32)
            odd = heads_ref[(2 * pair + 1) * 4 + y].astype(f32)
            at = slice(y * 256 + pair * 128, y * 256 + (pair + 1) * 128)
            mixed_ref[0:128, at] = jnp.where(low_lanes, even, pltpu.roll(odd, 64, 1)).astype(bf16)
            mixed_ref[128:256, at] = jnp.where(low_lanes, pltpu.roll(even, 64, 1), odd).astype(bf16)
    first = short_ref[...].astype(f32) + dot(mixed_ref[...], co_ref[...])
    all_ref[...] = first
    first_ref[...] = all_ref[pl.ds(pl.multiple_of(head * 64, 64), 64), :]
    feed = norm_rows(first, gain_ref[...])
    inner = jax.nn.gelu(dot(feed, up_ref[...])).astype(bf16)
    part_ref[...] = dot(inner, down_ref[...]).astype(bf16).reshape(4, 64, D)


def final_kernel(where_ref, s0, s1, s2, s3, b0, b1, b2, b3, up_ref, out_ref):
    head = where_ref[1]
    rows = 256 + HALO
    second = jnp.concatenate([ref[...] for ref in (s0, s1, s2, s3)], axis=0)
    lifted = dot(second, up_ref[...])
    index = lax.broadcasted_iota(jnp.int32, (256, rows), 0)
    column = lax.broadcasted_iota(jnp.int32, (256, rows), 1)
    r, m = index // 64, index % 64
    source = jnp.where(r == 0, 192 + m, jnp.where(m == 63, 268 + r, (r - 1) * 64 + m + 1))
    choose = (source == column).astype(f32).astype(bf16)
    index = lax.broadcasted_iota(jnp.int32, (256, 256), 0)
    column = lax.broadcasted_iota(jnp.int32, (256, 256), 1)
    weave = ((index % 4) * 64 + index // 4 == column).astype(f32).astype(bf16)
    for s, block in enumerate((b0, b1, b2, b3)):
        mine = lifted[s * 64 : (s + 1) * 64]
        raised = jnp.concatenate([mine[:, q * SHARE : (q + 1) * SHARE] for q in range(4)], axis=0)
        value = (dot(choose, block[...]) + raised).astype(bf16)
        begin = pl.multiple_of(lax.rem(head - s + 4, 4) * 256, 256)
        out_ref[pl.ds(begin, 256), :] = dot(weave, value).astype(bf16)


def fetch_rest(weight, half):
    pairs = []
    for c, step in ((0, 1), (1, 3)):
        pairs += [(4 * c + y, 4 * c + (y + step) % 4) for y in range(4)]
    whole = lax.ppermute(weight, ("core", "head"), pairs)
    return [whole, shift(half, "head", 2, 4)]


def swap_cores(parts):
    return [shift(part, "core", 1, 2) for part in parts]


def sources(head, core):
    mine = lax.rem(head + 3 - 2 * core, 4)
    other = lax.rem(head + 1 + 2 * core, 4)
    return mine, other, lax.rem(head + 2, 4)


def place_copies(head, core, own, mine, other, target):
    near, far, apart = sources(head, core)
    halves_at = apart * 256
    return [
        (own, target.at[pl.ds(pl.multiple_of(head * 256, 256), 256)]),
        (mine[0], target.at[pl.ds(pl.multiple_of(near * 256, 256), 256)]),
        (other[0], target.at[pl.ds(pl.multiple_of(far * 256, 256), 256)]),
        (mine[1], target.at[pl.ds(pl.multiple_of(halves_at + core * 128, 128), 128)]),
        (other[1], target.at[pl.ds(pl.multiple_of(halves_at + 128 - core * 128, 128), 128)]),
    ]


def after(value, gate):
    return lax.optimization_barrier((value, gate))


def local(
    token_ids, embedding, fine_norm, fine_query, fine_key, fine_value, fine_output,
    shorten_weight, coarse_norm, coarse_query, coarse_key, coarse_value, coarse_output,
    ffn_norm, ffn_up, ffn_down, upsample_weight,
):
    place = lax.axis_index(SEQ).astype(jnp.int32)
    head = lax.axis_index("head").astype(jnp.int32)
    x_place = lax.axis_index("x").astype(jnp.int32)
    core = lax.axis_index("core").astype(jnp.int32)
    tables = jnp.asarray(angle_tables())
    where = jnp.stack([place, head, core])

    prior = later(token_ids, SEQ, 1, 32)
    before = later(token_ids, SEQ, 2, 32)[ROWS - HALO :]
    tab, fo_half = call(
        fine_tables_kernel, "fine_tables",
        [pltpu.HBM((5, 256, SHARE), bf16), pltpu.HBM((128, D), bf16)], [where], [],
        [
            pltpu.VMEM((5, 256, SHARE), bf16),
            pltpu.VMEM((1, D), f32), pltpu.VMEM((256, D), bf16),
            pltpu.VMEM((3, D, SHARE), bf16), pltpu.VMEM((128, D), bf16),
            pltpu.SemaphoreType.DMA((10,)),
        ],
        us=3, hbm=[
            fine_norm[None], embedding, fine_query, fine_key, fine_value,
            fine_output,
        ],
    )
    own_ids_column = token_ids[:, None]
    fine_output_held, own_ids_column = after(fine_output, own_ids_column)
    out_mine = fetch_rest(fine_output_held, fo_half)
    rows = 256 + HALO
    mixed = call(
        fine_kernel, "fine_attention", jax.ShapeDtypeStruct((4, rows, SHARE), bf16),
        [where], [before[:, None], prior[:, None], own_ids_column],
        [
            pltpu.VMEM((BLOCK + ROWS, SHARE), bf16),
            pltpu.VMEM((KEYS, SHARE), bf16), pltpu.VMEM((KEYS, SHARE), bf16),
            pltpu.VMEM((5, 256, SHARE), bf16), pltpu.VMEM((576, 128), f32),
            pltpu.SemaphoreType.DMA((10,)),
        ],
        grid=(2,), us=12, limit=24, hbm=[tab, tables],
    )

    out_mine, mixed = after(out_mine, mixed)
    got = lax.all_to_all(mixed, "head", 0, 0)
    out_other = swap_cores(out_mine)
    own_ids = lax.dynamic_slice_in_dim(
        jnp.concatenate([prior[ROWS - HALO :], token_ids]), head * 256, rows, 0
    )
    sends, shorten_near = call(
        fine_rows_kernel, "fine_rows",
        [
            jax.ShapeDtypeStruct((4, rows, SHARE), bf16),
            jax.ShapeDtypeStruct((SHORTEN, SHARE, D), bf16),
        ],
        [where],
        [own_ids[:, None], embedding, got, fine_output, *out_mine, *out_other],
        [pltpu.SemaphoreType.DMA((4,))], hbm=[shorten_weight],
    )
    blocks = exchange(lambda d: lax.dynamic_index_in_dim(sends, d, 0, keepdims=False), "head", 4)

    terms = []
    for s, block in enumerate(blocks):
        part = call(
            short_part_kernel, "short_part", jax.ShapeDtypeStruct((64, D), bf16), [],
            [block, shorten_near],
        )
        terms.append(part if s == 0 else shift(part, "head", 4 - s, 4))
    short_own = sum(t.astype(f32) for t in terms).astype(bf16)
    shorts = [short_own] + [shift(short_own, "head", s, 4) for s in range(1, 4)]
    packed, short = call(
        coarse_pack_kernel, "coarse_pack",
        [
            jax.ShapeDtypeStruct((4, COARSE_ROWS * 3 // 2, 128), bf16),
            jax.ShapeDtypeStruct((COARSE_ROWS, D), bf16),
        ],
        [where],
        [*shorts, coarse_norm[None], coarse_query, coarse_key, coarse_value, tables],
    )

    coarse_output_held, packed = after(coarse_output, packed)
    co_half = lax.dynamic_slice_in_dim(coarse_output_held, core * 128, 128, 0)
    co_mine = fetch_rest(coarse_output_held, co_half)
    turned = lax.all_to_all(packed, "z", 0, 0)
    kv = turned[:, :COARSE_ROWS]
    far = [shift(kv, "core", 1, 2)]
    near = [shift(kv, "x", s, 4) for s in range(1, 4)]
    steps = jnp.arange(4, dtype=jnp.int32)
    flags = ((x_place - steps + 4) % 4 < x_place).astype(jnp.int32) + (steps == 0) * core
    flags = jnp.concatenate([flags, where[1:]])
    wide = jax.ShapeDtypeStruct((1024, 128), f32)
    q_all, *sums = call(
        coarse_first_kernel, "coarse_first",
        [jax.ShapeDtypeStruct((1024, 128), bf16), wide, wide, wide], [flags], [turned, far[0]],
        us=3, limit=24,
    )
    near_held, co_held, q_all = lax.optimization_barrier((near, co_mine, q_all))
    far += [shift(part, "core", 1, 2) for part in near_held]
    co_other = swap_cores(co_held)
    square = jax.ShapeDtypeStruct((D, D), bf16)
    up_near, down_near, *sums = call(
        functools.partial(coarse_more_kernel, (1, 3), False), "coarse_more",
        [square, square, wide, wide, wide],
        [flags], [near[0], far[1], near[2], far[3], q_all, *sums],
        [pltpu.SemaphoreType.DMA((8,))], us=6, limit=24, hbm=[ffn_up, ffn_down],
    )
    output_near, wide_sends = call(
        functools.partial(coarse_more_kernel, (2,), True), "coarse_last",
        [square, jax.ShapeDtypeStruct((16, 128, 128), bf16)],
        [flags], [near[1], far[2], q_all, *sums],
        [pltpu.VMEM((1024, 128), f32)] * 3 + [pltpu.SemaphoreType.DMA((5,))],
        us=3, limit=24, hbm=[coarse_output], free=[*co_mine, *co_other],
    )

    heads_in = lax.all_to_all(wide_sends, ("z", "head"), 0, 0)
    parts, first_own = call(
        feed_kernel, "feed",
        [jax.ShapeDtypeStruct((4, 64, D), bf16), jax.ShapeDtypeStruct((64, D), f32)],
        [where],
        [heads_in, short, ffn_norm[None], output_near, up_near, down_near],
        [
            pltpu.VMEM((COARSE_ROWS, D), bf16), pltpu.VMEM((COARSE_ROWS, D), f32),
        ],
        us=4,
    )
    sums = exchange(lambda d: lax.dynamic_index_in_dim(parts, d, 0, keepdims=False), "head", 4)
    second_own = (first_own + sum(t.astype(f32) for t in sums)).astype(bf16)
    seconds = [second_own] + [shift(second_own, "head", s, 4) for s in range(1, 4)]
    return call(
        final_kernel, "final", jax.ShapeDtypeStruct((ROWS, SHARE), bf16),
        [where], [*seconds, *blocks, upsample_weight.reshape(D, SHORTEN * SHARE)],
    )


def solution(mesh):
    split = Mesh(mesh.devices.reshape(4, 4, 2, 4), ("z", "x", "core", "head"))
    return jax.shard_map(
        local,
        mesh=split,
        in_specs=(
            P(SEQ), P(), P(), P(None, "head"), P(None, "head"), P(None, "head"), P("head", None),
            P(None, "head", None), P(), P(None, "head"), P(None, "head"), P(None, "head"),
            P("head", None), P(), P(None, "head"), P("head", None), P(None, None, "head"),
        ),
        out_specs=P(SEQ, "head"),
        check_vma=False,
    )
```

```python
import functools
import math

import jax
import jax.numpy as jnp
import numpy as np
from jax import lax
from jax.experimental import pallas as pl
from jax.experimental.pallas import tpu as pltpu
from jax.sharding import Mesh
from jax.sharding import PartitionSpec as P

D = 1024
HEAD_DIM = 64
SHORTEN = 4
WINDOW = 1024
BLOCK = 256
HALO = 16
ROWS = 1024
PAST = WINDOW + BLOCK
KEYS = PAST + ROWS
SHARE = 256
COARSE_ROWS = 256
SEQ = ("z", "x", "core")

epsilon = 1e-06
masked_low = -1e30
q_scale = HEAD_DIM ** (-0.5) * math.log2(math.e)
bf16 = jnp.bfloat16
f32 = jnp.float32


def angle_tables():
    lane = np.arange(128) % 32
    period = 2.0 ** (4 + lane * 14 // 32)
    coarse = (256.0 * np.arange(32)[:, None]) % period[None]
    near = np.arange(256)[:, None] % period[None]
    a = coarse * (2.0 * np.pi / period)[None]
    b = near * (2.0 * np.pi / period)[None]
    parts = [np.cos(a), np.sin(a), np.cos(b), np.sin(b)]
    return np.concatenate(parts, axis=0).astype(np.float32)


def shift(value, axis, steps, count):
    return lax.ppermute(value, axis, [(i, (i + steps) % count) for i in range(count)])


def later(value, axis, steps, count):
    return lax.ppermute(value, axis, [(i, i + steps) for i in range(count - steps)])


def exchange(block_for, axis, count):
    me = lax.axis_index(axis)
    got = [block_for(me)]
    for s in range(1, count):
        got.append(shift(block_for((me + s) % count), axis, s, count))
    return got


def dot(left, right):
    return jnp.dot(left, right, preferred_element_type=f32)


def dot_t(left, right):
    return lax.dot_general(left, right, (((1,), (1,)), ((), ())), preferred_element_type=f32)


def norm_rows(data, gain):
    power = jnp.mean(data * data, axis=-1, keepdims=True)
    return (data * lax.rsqrt(power + epsilon) * gain).astype(bf16)


def partner(values):
    width = values.shape[1]
    lane = lax.broadcasted_iota(jnp.int32, values.shape, 1)
    ahead = pltpu.roll(values, width - 32, 1)
    behind = pltpu.roll(values, 32, 1)
    return jnp.where(lane % 64 < 32, -ahead, behind)


def halves(table):
    high = table.astype(bf16)
    low = (table - high.astype(f32)).astype(bf16)
    return high, low


def turn_tables(turn_ref, far):
    ca = turn_ref[pl.ds(far, 1), :]
    sa = turn_ref[pl.ds(32 + far, 1), :]
    cb = turn_ref[64:320, :]
    sb = turn_ref[320:576, :]
    cosine = ca * cb - sa * sb
    sine = sa * cb + ca * sb
    return jnp.concatenate([cosine, cosine], axis=1), jnp.concatenate([sine, sine], axis=1)


def pick(ids, levels=256):
    columns = lax.broadcasted_iota(jnp.int32, (ids.shape[0], levels), 1)
    return (ids == columns).astype(f32).astype(bf16)


def turned_rows(hot, tab_ref, n, cosine, sine):
    return (dot(hot, tab_ref[n]) * cosine + dot(hot, tab_ref[n + 1]) * sine).astype(bf16)


def fine_tables_kernel(gain_hbm, emb_hbm, wq_hbm, wk_hbm, wv_hbm, tab_hbm, tab_ref, gain_ref, emb_ref, w_ref, sems):
    pairs = [(emb_hbm, emb_ref), (gain_hbm, gain_ref)]
    for n, w in enumerate((wq_hbm, wk_hbm, wv_hbm)):
        for part in range(2):
            rows = pl.ds(part * 512, 512)
            pairs.append((w.at[rows], w_ref.at[n, rows]))
    copies = begin_copies(pairs, sems)
    finish_copies(copies[:2])
    fine_in = norm_rows(emb_ref[...].astype(f32), gain_ref[...])
    finish_copies(copies[2:])
    tq = dot(fine_in, w_ref[0]) * q_scale
    tk = dot(fine_in, w_ref[1])
    tables = (tq, partner(tq), tk, partner(tk), dot(fine_in, w_ref[2]))
    for n, table in enumerate(tables):
        tab_ref[n] = table.astype(bf16)
    finish_copies(begin_copies([(tab_ref.at[n], tab_hbm.at[n]) for n in range(5)], sems))


def fine_kernel(
    where_ref, before_ref, prior_ref, own_ref, tab_hbm, turn_hbm,
    own_hbm, o1, o2, o3, q_ref, k_ref, v_ref, tab_ref, turn_ref, block_ref, sems,
):
    step = pl.program_id(0)
    head = where_ref[1]
    outs = (block_ref, o1, o2, o3)
    turns = ((3, 0), (1, 2))
    lowest = jnp.maximum(PAST - where_ref[0] * ROWS, 0)
    head_lane = lax.broadcasted_iota(jnp.int32, (1, SHARE), 1) // HEAD_DIM

    @pl.when(step == 0)
    def _():
        pairs = [(tab_hbm.at[n], tab_ref.at[n]) for n in range(5)] + [(turn_hbm, turn_ref)]
        finish_copies(begin_copies(pairs, sems))
        cosine, sine = turn_tables(turn_ref, 0)
        oldest = pick(before_ref[...])
        at = slice(BLOCK - HALO, BLOCK)
        k_ref[at, :] = turned_rows(oldest, tab_ref, 2, cosine[at], sine[at])
        v_ref[at, :] = dot(oldest, tab_ref[4]).astype(bf16)

        def build(block, ids, with_q):
            begin = pl.multiple_of(block * BLOCK, BLOCK)
            hot = pick(ids)
            cosine, sine = turn_tables(turn_ref, block)
            k_ref[pl.ds(begin, BLOCK), :] = turned_rows(hot, tab_ref, 2, cosine, sine)
            v_ref[pl.ds(begin, BLOCK), :] = dot(hot, tab_ref[4]).astype(bf16)
            if with_q:
                at = pl.multiple_of(begin - (PAST - BLOCK), BLOCK)
                q_ref[pl.ds(at, BLOCK), :] = turned_rows(hot, tab_ref, 0, cosine, sine)

        def build_from(ref, first, with_q):
            def body(n, _):
                ids = ref[pl.ds(pl.multiple_of(n * BLOCK, BLOCK), BLOCK), :]
                build(first + n, ids, with_q)
                return 0

            return body

        for n in range(3):
            build(1 + n, prior_ref[n * BLOCK : (n + 1) * BLOCK, :], False)
        build(4, prior_ref[3 * BLOCK :, :], True)
        for n in range(4):
            build(5 + n, own_ref[n * BLOCK : (n + 1) * BLOCK, :], True)
        halo_q = q_ref[BLOCK - HALO : BLOCK, :]
        stacked = jnp.concatenate(
            [jnp.where(head_lane == h, halo_q, jnp.zeros_like(halo_q)) for h in range(4)], axis=0
        )
        scores = dot_t(stacked, k_ref[BLOCK - HALO : PAST, :])
        row = lax.broadcasted_iota(jnp.int32, scores.shape, 0) % HALO + (PAST - HALO)
        col = lax.broadcasted_iota(jnp.int32, scores.shape, 1) + (BLOCK - HALO)
        allowed = (col <= row) & (col > row - WINDOW) & (col >= lowest)
        scores = jnp.where(allowed, scores, masked_low)
        top = jnp.max(scores, axis=1, keepdims=True)
        weights = jnp.exp2(scores - top)
        total = jnp.sum(weights, axis=1, keepdims=True)
        mixed = dot(weights.astype(bf16), v_ref[BLOCK - HALO : PAST, :]) / total
        result = jnp.zeros((HALO, SHARE), f32)
        for h in range(4):
            result = jnp.where(head_lane == h, mixed[h * HALO : (h + 1) * HALO], result)
        for s, out_ref in enumerate(outs):

            @pl.when(lax.rem(head + s, 4) == 0)
            def _(out_ref=out_ref):
                out_ref[0:HALO, :] = result.astype(bf16)

    for late in range(2):
        turn = jnp.where(step == 0, turns[0][late], turns[1][late])
        place = lax.rem(head + turn, 4)
        begin = pl.multiple_of((place + 1) * BLOCK, BLOCK)
        keys = k_ref[pl.ds(begin, PAST), :]
        values = v_ref[pl.ds(begin, PAST), :]
        query = q_ref[pl.ds(begin, BLOCK), :]
        row = lax.broadcasted_iota(jnp.int32, (BLOCK, BLOCK), 0)
        col = lax.broadcasted_iota(jnp.int32, (BLOCK, BLOCK), 1)
        biases = [
            jnp.where(begin + t * BLOCK >= lowest, 0.0, masked_low).astype(f32) for t in range(4)
        ]
        inside = col <= row
        ones = jnp.ones((PAST, 128), bf16)
        low_lanes = lax.broadcasted_iota(jnp.int32, (1, 128), 1) < 64
        results = []

        def score(h):
            return dot_t(jnp.where(head_lane == h, query, jnp.zeros_like(query)), keys)

        ahead = score(0)
        for h in range(4):
            scores = ahead
            if h < 3:
                ahead = score(h + 1)
            tiles = [scores[:, t * BLOCK : (t + 1) * BLOCK] for t in range(5)]
            edge = jnp.where(inside, tiles[4], tiles[0] + biases[0])
            middle = [tiles[t] + biases[t] for t in range(1, 4)]
            peak = edge
            for tile in middle:
                peak = jnp.maximum(peak, tile)
            top = jnp.max(peak, axis=1, keepdims=True)
            edge = jnp.exp2(edge - top).astype(bf16)
            none = jnp.zeros_like(edge)
            weights = [jnp.exp2(tile - top).astype(bf16) for tile in middle]
            weights = [jnp.where(inside, none, edge), *weights, jnp.where(inside, edge, none)]
            pair = (h // 2) * 128
            wide = jnp.concatenate([values[:, pair : pair + 128], ones], axis=1)
            mixed = dot(jnp.concatenate(weights, axis=1), wide)
            results.append(mixed[:, :128] / mixed[:, 128:])
        result = jnp.concatenate(
            [jnp.where(low_lanes, results[2 * n], results[2 * n + 1]) for n in range(2)], axis=1
        )
        result = result.astype(bf16)
        for n in range(2):

            @pl.when(step == n)
            def _(n=n, late=late, result=result, place=place):
                turn = turns[n][late]
                outs[turn][HALO:, :] = result

                @pl.when(place < 3)
                def _():
                    outs[(turn + 1) % 4][0:HALO, :] = result[BLOCK - HALO :]

    @pl.when(step == 0)
    def _():
        pltpu.make_async_copy(block_ref, own_hbm, sems.at[9]).start()

    @pl.when(step == 1)
    def _():
        pltpu.make_async_copy(block_ref, own_hbm, sems.at[9]).wait()


def vmem():
    return pl.BlockSpec(memory_space=pltpu.VMEM)


def smem():
    return pl.BlockSpec(memory_space=pltpu.SMEM)


def space(shape):
    plain = isinstance(shape, jax.ShapeDtypeStruct)
    return vmem() if plain else pl.BlockSpec(memory_space=pltpu.HBM)


def call(kernel, name, shapes, scalars, arrays, scratch=(), grid=None, limit=16, us=2, hbm=(), free=()):
    one = not isinstance(shapes, (list, tuple))
    extra = {} if grid is None else {"grid": grid}
    return pl.pallas_call(
        kernel,
        out_shape=shapes,
        in_specs=[smem()] * len(scalars)
        + [vmem()] * len(arrays)
        + [pl.BlockSpec(memory_space=pltpu.HBM)] * len(hbm)
        + [pl.BlockSpec(memory_space=pl.ANY)] * len(free),
        out_specs=space(shapes) if one else [space(shape) for shape in shapes],
        scratch_shapes=list(scratch),
        compiler_params=pltpu.CompilerParams(vmem_limit_bytes=limit << 20),
        cost_estimate=pl.CostEstimate(
            flops=us * 10**9, transcendentals=0, bytes_accessed=us * 2 * 10**6
        ),
        name=name,
        **extra,
    )(*scalars, *arrays, *(pltpu.with_memory_space_constraint(a, pltpu.HBM) for a in hbm), *free)


def begin_copies(pairs, sems):
    copies = [pltpu.make_async_copy(a, b, sems.at[n]) for n, (a, b) in enumerate(pairs)]
    for copy in copies:
        copy.start()
    return copies


def finish_copies(copies):
    for copy in copies:
        copy.wait()


def fine_rows_kernel(
    where_ref, ids_ref, emb_ref, g1, g2, g3, own_ref, m1, m2, t1, t2, w_hbm, block_hbm,
    out_ref, w_ref, block_ref, sems,
):
    place, head, core = where_ref[0], where_ref[1], where_ref[2]
    copies = begin_copies(
        [(block_hbm, block_ref)] + [(w_hbm.at[n], w_ref.at[n]) for n in range(4)], sems
    )
    merged = dot(pick(ids_ref[...]), emb_ref[...])
    near = jnp.where(core == 0, g1[...], g3[...])
    far = jnp.where(core == 0, g3[...], g1[...])
    merged += dot(near, m1[...]) + dot(far, t1[...])
    at = pl.ds(pl.multiple_of(core * 128, 128), 128)
    merged += dot(g2[:, at], m2[...])
    at = pl.ds(pl.multiple_of(128 - core * 128, 128), 128)
    merged += dot(g2[:, at], t2[...])
    finish_copies(copies[:1])
    merged += dot(block_ref[...], own_ref[...])
    rows = 256 + HALO
    token = (
        place * ROWS + head * 256 - HALO + lax.broadcasted_iota(jnp.int32, (rows, D), 0)
    )
    fine = jnp.where(token >= 0, merged, 0.0).astype(bf16)
    index = lax.broadcasted_iota(jnp.int32, (256, rows), 0)
    column = lax.broadcasted_iota(jnp.int32, (256, rows), 1)
    source = 4 * (index % 64) + index // 64 + (HALO - 3)
    choose = (source == column).astype(f32).astype(bf16)
    grouped = dot(choose, fine).astype(bf16)
    for d in range(4):
        out_ref[d, 0:256, :] = grouped[:, d * SHARE : (d + 1) * SHARE]
        out_ref[d, 256:rows, :] = fine[256:rows, d * SHARE : (d + 1) * SHARE]
    finish_copies(copies[1:])


def short_part_kernel(group_ref, w_ref, out_ref):
    total = dot(group_ref[0:64, :], w_ref[0])
    for r in range(1, SHORTEN):
        total += dot(group_ref[r * 64 : (r + 1) * 64, :], w_ref[r])
    out_ref[...] = total.astype(bf16)


def coarse_pack_kernel(
    where_ref, s0, s1, s2, s3, gain_ref, wq_ref, wk_ref, wv_ref, turn_ref,
    out_ref, short_ref,
):
    place, head = where_ref[0], where_ref[1]
    for s, ref in enumerate((s0, s1, s2, s3)):
        begin = pl.multiple_of(lax.rem(head - s + 4, 4) * 64, 64)
        short_ref[pl.ds(begin, 64), :] = ref[...]
    x = norm_rows(short_ref[...].astype(f32), gain_ref[...])
    cosine, sine = turn_tables(turn_ref, place)

    def turned(values):
        return values * cosine + partner(values) * sine

    q = turned(dot(x, wq_ref[...])) * q_scale
    k = turned(dot(x, wk_ref[...]))
    v = dot(x, wv_ref[...])
    low_lanes = lax.broadcasted_iota(jnp.int32, (1, 128), 1) < 64
    half = COARSE_ROWS // 2
    for h in range(4):
        pair = (h // 2) * 128
        kp = k[:, pair : pair + 128]
        vp = v[:, pair : pair + 128]
        qp = q[:, pair : pair + 128]
        if h % 2 == 0:
            kv = jnp.where(low_lanes, kp, pltpu.roll(vp, 64, 1))
            qq = jnp.where(low_lanes, qp[:half], pltpu.roll(qp[half:], 64, 1))
        else:
            kv = jnp.where(low_lanes, pltpu.roll(kp, 64, 1), vp)
            qq = jnp.where(low_lanes, pltpu.roll(qp[:half], 64, 1), qp[half:])
        out_ref[h, 0:COARSE_ROWS, :] = kv.astype(bf16)
        out_ref[h, COARSE_ROWS : COARSE_ROWS + half, :] = qq.astype(bf16)


def with_ones(kv):
    return jnp.concatenate([kv, jnp.ones((kv.shape[0], 128), bf16)], axis=1)


def absorb(state, jobs):
    q_ref, top_ref, total_ref, acc_ref = state

    def score(job):
        query = q_ref[pl.ds(job[0], job[1]), :]
        return [dot_t(query, kv) for kv in job[2]]

    ahead = score(jobs[0])
    for n, (begin, rows, parts) in enumerate(jobs):
        scores = ahead
        if n + 1 < len(jobs):
            ahead = score(jobs[n + 1])
        at = pl.ds(begin, rows)
        peak = scores[0]
        for s in scores[1:]:
            peak = jnp.maximum(peak, s)
        old = top_ref[at, :]
        top = jnp.maximum(old, jnp.max(peak, axis=1, keepdims=True))
        factor = jnp.exp2(old - top)
        both = jnp.concatenate([top, top], axis=1)
        contrib = dot(jnp.exp2(scores[0] - both).astype(bf16), with_ones(parts[0]))
        for s, kv in zip(scores[1:], parts[1:]):
            contrib = contrib + dot(jnp.exp2(s - both).astype(bf16), with_ones(kv))
        top_ref[at, :] = top
        total_ref[at, :] = total_ref[at, :] * factor + contrib[:, 128:]
        acc_ref[at, :] = acc_ref[at, :] * factor + contrib[:, :128]


def coarse_first_kernel(flag_ref, turned_ref, far_ref, q_ref, top_ref, total_ref, acc_ref):
    half = COARSE_ROWS // 2
    low_lanes = lax.broadcasted_iota(jnp.int32, (1, 128), 1) < 64
    row = lax.broadcasted_iota(jnp.int32, (256, 256), 0)
    col = lax.broadcasted_iota(jnp.int32, (256, 256), 1)
    for z in range(4):
        packed = turned_ref[z, COARSE_ROWS:, :].astype(f32)
        zero = jnp.zeros_like(packed)
        q_ref[z * 256 : z * 256 + half, :] = jnp.where(low_lanes, packed, zero).astype(bf16)
        q_ref[z * 256 + half : (z + 1) * 256, :] = jnp.where(
            low_lanes, pltpu.roll(packed, 64, 1), zero
        ).astype(bf16)
        kv = turned_ref[z, :COARSE_ROWS, :]
        at = pl.ds(z * 256, 256)
        scores = jnp.where(col <= row, dot_t(q_ref[at, :], kv), masked_low)
        top = jnp.max(scores, axis=1, keepdims=True)
        contrib = dot(jnp.exp2(scores - top).astype(bf16), with_ones(kv))
        top_ref[at, :] = jnp.broadcast_to(top, (256, 128))
        total_ref[at, :] = contrib[:, 128:]
        acc_ref[at, :] = contrib[:, :128]
    state = (q_ref, top_ref, total_ref, acc_ref)
    absorb(
        state,
        [
            ((z + 1) * 256, (3 - z) * 256, [turned_ref[z, :COARSE_ROWS, :], far_ref[z]])
            for z in range(3)
        ],
    )

    @pl.when(flag_ref[0] > 0)
    def _():
        absorb(state, [(z * 256, 256, [far_ref[z]]) for z in range(4)])


def coarse_more_kernel(which, last, flag_ref, *refs):
    count = 2 * len(which)
    sems = refs[-1]
    refs = refs[:-1]
    chunks = refs[:count]
    q_ref, top_in, total_in, acc_in = refs[count : count + 4]
    refs = refs[count + 4 :]
    top_ref, total_ref, acc_ref = refs[-3:]
    if last:
        own, m1, m2, t1, t2, target, out_ref = refs[:-3]
        pairs = place_copies(flag_ref[4], flag_ref[5], own, (m1, m2), (t1, t2), target)
    else:
        pairs = []
        for a, b in zip(refs[:2], refs[2:4]):
            for part in range(4):
                at = pl.ds(part * 256, 256)
                pairs.append((a.at[at], b.at[at]))
    copies = begin_copies(pairs, sems)
    top_ref[...] = top_in[...]
    total_ref[...] = total_in[...]
    acc_ref[...] = acc_in[...]
    state = (q_ref, top_ref, total_ref, acc_ref)
    pairs_of = [(chunks[2 * n], chunks[2 * n + 1]) for n in range(len(which))]
    absorb(
        state,
        [
            ((z + 1) * 256, (3 - z) * 256, [near[z], far[z]])
            for near, far in pairs_of
            for z in range(3)
        ],
    )
    for s, (near, far) in zip(which, pairs_of):

        @pl.when(flag_ref[s] > 0)
        def _(near=near, far=far):
            absorb(state, [(z * 256, 256, [near[z], far[z]]) for z in range(4)])

    if last:
        mixed = acc_ref[...] / total_ref[...]
        low_lanes = lax.broadcasted_iota(jnp.int32, (1, 128), 1) < 64
        for z in range(4):
            upper = pltpu.roll(mixed[z * 256 : z * 256 + 128], 64, 1)
            lower = mixed[z * 256 + 128 : (z + 1) * 256]
            block = jnp.where(low_lanes, upper, lower).astype(bf16)
            for y in range(4):
                out_ref[z * 4 + y] = block
    finish_copies(copies)


def feed_kernel(
    where_ref, heads_ref, short_ref, gain_ref, co_ref, up_ref, down_ref,
    part_ref, first_ref, mixed_ref, all_ref,
):
    head = where_ref[1]
    low_lanes = lax.broadcasted_iota(jnp.int32, (1, 128), 1) < 64
    for y in range(4):
        for pair in range(2):
            even = heads_ref[2 * pair * 4 + y].astype(f32)
            odd = heads_ref[(2 * pair + 1) * 4 + y].astype(f32)
            at = slice(y * 256 + pair * 128, y * 256 + (pair + 1) * 128)
            mixed_ref[0:128, at] = jnp.where(low_lanes, even, pltpu.roll(odd, 64, 1)).astype(bf16)
            mixed_ref[128:256, at] = jnp.where(low_lanes, pltpu.roll(even, 64, 1), odd).astype(bf16)
    first = short_ref[...].astype(f32) + dot(mixed_ref[...], co_ref[...])
    all_ref[...] = first
    first_ref[...] = all_ref[pl.ds(pl.multiple_of(head * 64, 64), 64), :]
    feed = norm_rows(first, gain_ref[...])
    inner = jax.nn.gelu(dot(feed, up_ref[...])).astype(bf16)
    part_ref[...] = dot(inner, down_ref[...]).astype(bf16).reshape(4, 64, D)


def final_kernel(where_ref, s0, s1, s2, s3, b0, b1, b2, b3, up_ref, out_ref):
    head = where_ref[1]
    rows = 256 + HALO
    second = jnp.concatenate([ref[...] for ref in (s0, s1, s2, s3)], axis=0)
    lifted = dot(second, up_ref[...])
    index = lax.broadcasted_iota(jnp.int32, (256, rows), 0)
    column = lax.broadcasted_iota(jnp.int32, (256, rows), 1)
    r, m = index // 64, index % 64
    source = jnp.where(r == 0, 192 + m, jnp.where(m == 63, 268 + r, (r - 1) * 64 + m + 1))
    choose = (source == column).astype(f32).astype(bf16)
    index = lax.broadcasted_iota(jnp.int32, (256, 256), 0)
    column = lax.broadcasted_iota(jnp.int32, (256, 256), 1)
    weave = ((index % 4) * 64 + index // 4 == column).astype(f32).astype(bf16)
    for s, block in enumerate((b0, b1, b2, b3)):
        mine = lifted[s * 64 : (s + 1) * 64]
        raised = jnp.concatenate([mine[:, q * SHARE : (q + 1) * SHARE] for q in range(4)], axis=0)
        value = (dot(choose, block[...]) + raised).astype(bf16)
        begin = pl.multiple_of(lax.rem(head - s + 4, 4) * 256, 256)
        out_ref[pl.ds(begin, 256), :] = dot(weave, value).astype(bf16)


def fetch_rest(weight, core):
    pairs = []
    for c, step in ((0, 1), (1, 3)):
        pairs += [(4 * c + y, 4 * c + (y + step) % 4) for y in range(4)]
    whole = lax.ppermute(weight, ("core", "head"), pairs)
    half = shift(lax.dynamic_slice_in_dim(weight, core * 128, 128, 0), "head", 2, 4)
    return [whole, half]


def swap_cores(parts):
    return [shift(part, "core", 1, 2) for part in parts]


def sources(head, core):
    mine = lax.rem(head + 3 - 2 * core, 4)
    other = lax.rem(head + 1 + 2 * core, 4)
    return mine, other, lax.rem(head + 2, 4)


def place_copies(head, core, own, mine, other, target):
    near, far, apart = sources(head, core)
    halves_at = apart * 256
    return [
        (own, target.at[pl.ds(pl.multiple_of(head * 256, 256), 256)]),
        (mine[0], target.at[pl.ds(pl.multiple_of(near * 256, 256), 256)]),
        (other[0], target.at[pl.ds(pl.multiple_of(far * 256, 256), 256)]),
        (mine[1], target.at[pl.ds(pl.multiple_of(halves_at + core * 128, 128), 128)]),
        (other[1], target.at[pl.ds(pl.multiple_of(halves_at + 128 - core * 128, 128), 128)]),
    ]


def after(value, gate):
    return lax.optimization_barrier((value, gate))


def local(
    token_ids, embedding, fine_norm, fine_query, fine_key, fine_value, fine_output,
    shorten_weight, coarse_norm, coarse_query, coarse_key, coarse_value, coarse_output,
    ffn_norm, ffn_up, ffn_down, upsample_weight,
):
    place = lax.axis_index(SEQ).astype(jnp.int32)
    head = lax.axis_index("head").astype(jnp.int32)
    x_place = lax.axis_index("x").astype(jnp.int32)
    core = lax.axis_index("core").astype(jnp.int32)
    tables = jnp.asarray(angle_tables())
    where = jnp.stack([place, head, core])

    prior = later(token_ids, SEQ, 1, 32)
    before = later(token_ids, SEQ, 2, 32)[ROWS - HALO :]
    tab = call(
        fine_tables_kernel, "fine_tables", pltpu.HBM((5, 256, SHARE), bf16), [], [],
        [
            pltpu.VMEM((5, 256, SHARE), bf16),
            pltpu.VMEM((1, D), f32), pltpu.VMEM((256, D), bf16),
            pltpu.VMEM((3, D, SHARE), bf16), pltpu.SemaphoreType.DMA((9,)),
        ],
        us=3, hbm=[fine_norm[None], embedding, fine_query, fine_key, fine_value],
    )
    own_ids_column = token_ids[:, None]
    fine_output_held, own_ids_column = after(fine_output, own_ids_column)
    out_mine = fetch_rest(fine_output_held, core)
    rows = 256 + HALO
    mixed = call(
        fine_kernel, "fine_attention",
        [pltpu.HBM((rows, SHARE), bf16)] + [jax.ShapeDtypeStruct((rows, SHARE), bf16)] * 3,
        [where], [before[:, None], prior[:, None], own_ids_column],
        [
            pltpu.VMEM((BLOCK + ROWS, SHARE), bf16),
            pltpu.VMEM((KEYS, SHARE), bf16), pltpu.VMEM((KEYS, SHARE), bf16),
            pltpu.VMEM((5, 256, SHARE), bf16), pltpu.VMEM((576, 128), f32),
            pltpu.VMEM((rows, SHARE), bf16), pltpu.SemaphoreType.DMA((10,)),
        ],
        grid=(2,), us=12, limit=24, hbm=[tab, tables],
    )

    out_mine, mixed = after(out_mine, mixed)
    got = [shift(mixed[s], "head", s, 4) for s in range(1, 4)]
    out_other = swap_cores(out_mine)
    own_ids = lax.dynamic_slice_in_dim(
        jnp.concatenate([prior[ROWS - HALO :], token_ids]), head * 256, rows, 0
    )
    sends, shorten_near = call(
        fine_rows_kernel, "fine_rows",
        [
            jax.ShapeDtypeStruct((4, rows, SHARE), bf16),
            jax.ShapeDtypeStruct((SHORTEN, SHARE, D), bf16),
        ],
        [where],
        [own_ids[:, None], embedding, *got, fine_output, *out_mine, *out_other],
        [pltpu.VMEM((rows, SHARE), bf16), pltpu.SemaphoreType.DMA((5,))],
        hbm=[shorten_weight, mixed[0]],
    )
    blocks = exchange(lambda d: lax.dynamic_index_in_dim(sends, d, 0, keepdims=False), "head", 4)

    terms = []
    for s, block in enumerate(blocks):
        part = call(
            short_part_kernel, "short_part", jax.ShapeDtypeStruct((64, D), bf16), [],
            [block, shorten_near],
        )
        terms.append(part if s == 0 else shift(part, "head", 4 - s, 4))
    short_own = sum(t.astype(f32) for t in terms).astype(bf16)
    shorts = [short_own] + [shift(short_own, "head", s, 4) for s in range(1, 4)]
    packed, short = call(
        coarse_pack_kernel, "coarse_pack",
        [
            jax.ShapeDtypeStruct((4, COARSE_ROWS * 3 // 2, 128), bf16),
            jax.ShapeDtypeStruct((COARSE_ROWS, D), bf16),
        ],
        [where],
        [*shorts, coarse_norm[None], coarse_query, coarse_key, coarse_value, tables],
    )

    coarse_output_held, packed = after(coarse_output, packed)
    co_mine = fetch_rest(coarse_output_held, core)
    turned = lax.all_to_all(packed, "z", 0, 0)
    kv = turned[:, :COARSE_ROWS]
    far = [shift(kv, "core", 1, 2)]
    near = [shift(kv, "x", s, 4) for s in range(1, 4)]
    steps = jnp.arange(4, dtype=jnp.int32)
    flags = ((x_place - steps + 4) % 4 < x_place).astype(jnp.int32) + (steps == 0) * core
    flags = jnp.concatenate([flags, where[1:]])
    wide = jax.ShapeDtypeStruct((1024, 128), f32)
    q_all, *sums = call(
        coarse_first_kernel, "coarse_first",
        [jax.ShapeDtypeStruct((1024, 128), bf16), wide, wide, wide], [flags], [turned, far[0]],
        us=3, limit=24,
    )
    near_held, co_held, q_all = lax.optimization_barrier((near, co_mine, q_all))
    far += [shift(part, "core", 1, 2) for part in near_held]
    co_other = swap_cores(co_held)
    square = jax.ShapeDtypeStruct((D, D), bf16)
    up_near, down_near, *sums = call(
        functools.partial(coarse_more_kernel, (1, 3), False), "coarse_more",
        [square, square, wide, wide, wide],
        [flags], [near[0], far[1], near[2], far[3], q_all, *sums],
        [pltpu.SemaphoreType.DMA((8,))], us=6, limit=24, hbm=[ffn_up, ffn_down],
    )
    output_near, wide_sends = call(
        functools.partial(coarse_more_kernel, (2,), True), "coarse_last",
        [square, jax.ShapeDtypeStruct((16, 128, 128), bf16)],
        [flags], [near[1], far[2], q_all, *sums],
        [pltpu.VMEM((1024, 128), f32)] * 3 + [pltpu.SemaphoreType.DMA((5,))],
        us=3, limit=24, hbm=[coarse_output], free=[*co_mine, *co_other],
    )

    heads_in = lax.all_to_all(wide_sends, ("z", "head"), 0, 0)
    parts, first_own = call(
        feed_kernel, "feed",
        [jax.ShapeDtypeStruct((4, 64, D), bf16), jax.ShapeDtypeStruct((64, D), f32)],
        [where],
        [heads_in, short, ffn_norm[None], output_near, up_near, down_near],
        [
            pltpu.VMEM((COARSE_ROWS, D), bf16), pltpu.VMEM((COARSE_ROWS, D), f32),
        ],
        us=4,
    )
    sums = exchange(lambda d: lax.dynamic_index_in_dim(parts, d, 0, keepdims=False), "head", 4)
    second_own = (first_own + sum(t.astype(f32) for t in sums)).astype(bf16)
    seconds = [second_own] + [shift(second_own, "head", s, 4) for s in range(1, 4)]
    return call(
        final_kernel, "final", jax.ShapeDtypeStruct((ROWS, SHARE), bf16),
        [where], [*seconds, *blocks, upsample_weight.reshape(D, SHORTEN * SHARE)],
    )


def solution(mesh):
    split = Mesh(mesh.devices.reshape(4, 4, 2, 4), ("z", "x", "core", "head"))
    return jax.shard_map(
        local,
        mesh=split,
        in_specs=(
            P(SEQ), P(), P(), P(None, "head"), P(None, "head"), P(None, "head"), P("head", None),
            P(None, "head", None), P(), P(None, "head"), P(None, "head"), P(None, "head"),
            P("head", None), P(), P(None, "head"), P("head", None), P(None, None, "head"),
        ),
        out_specs=P(SEQ, "head"),
        check_vma=False,
    )
```

```python
import functools
import math

import jax
import jax.numpy as jnp
import numpy as np
from jax import lax
from jax.experimental import pallas as pl
from jax.experimental.pallas import tpu as pltpu
from jax.sharding import Mesh
from jax.sharding import PartitionSpec as P

D = 1024
HEAD_DIM = 64
SHORTEN = 4
WINDOW = 1024
BLOCK = 256
HALO = 16
ROWS = 1024
PAST = WINDOW + BLOCK
KEYS = PAST + ROWS
SHARE = 256
COARSE_ROWS = 256
SEQ = ("z", "x", "core")

epsilon = 1e-06
masked_low = -1e30
q_scale = HEAD_DIM ** (-0.5) * math.log2(math.e)
bf16 = jnp.bfloat16
f32 = jnp.float32


def angle_tables():
    lane = np.arange(128) % 32
    period = 2.0 ** (4 + lane * 14 // 32)
    coarse = (256.0 * np.arange(32)[:, None]) % period[None]
    near = np.arange(256)[:, None] % period[None]
    a = coarse * (2.0 * np.pi / period)[None]
    b = near * (2.0 * np.pi / period)[None]
    parts = [np.cos(a), np.sin(a), np.cos(b), np.sin(b)]
    return np.concatenate(parts, axis=0).astype(np.float32)


def shift(value, axis, steps, count):
    return lax.ppermute(value, axis, [(i, (i + steps) % count) for i in range(count)])


def later(value, axis, steps, count):
    return lax.ppermute(value, axis, [(i, i + steps) for i in range(count - steps)])


def exchange(block_for, axis, count):
    me = lax.axis_index(axis)
    got = [block_for(me)]
    for s in range(1, count):
        got.append(shift(block_for((me + s) % count), axis, s, count))
    return got


def dot(left, right):
    return jnp.dot(left, right, preferred_element_type=f32)


def dot_t(left, right):
    return lax.dot_general(left, right, (((1,), (1,)), ((), ())), preferred_element_type=f32)


def norm_rows(data, gain):
    power = jnp.mean(data * data, axis=-1, keepdims=True)
    return (data * lax.rsqrt(power + epsilon) * gain).astype(bf16)


def partner(values):
    width = values.shape[1]
    lane = lax.broadcasted_iota(jnp.int32, values.shape, 1)
    ahead = pltpu.roll(values, width - 32, 1)
    behind = pltpu.roll(values, 32, 1)
    return jnp.where(lane % 64 < 32, -ahead, behind)


def halves(table):
    high = table.astype(bf16)
    low = (table - high.astype(f32)).astype(bf16)
    return high, low


def turn_tables(turn_ref, far):
    ca = turn_ref[pl.ds(far, 1), :]
    sa = turn_ref[pl.ds(32 + far, 1), :]
    cb = turn_ref[64:320, :]
    sb = turn_ref[320:576, :]
    cosine = ca * cb - sa * sb
    sine = sa * cb + ca * sb
    return jnp.concatenate([cosine, cosine], axis=1), jnp.concatenate([sine, sine], axis=1)


def pick(ids, levels=256):
    columns = lax.broadcasted_iota(jnp.int32, (ids.shape[0], levels), 1)
    return (ids == columns).astype(f32).astype(bf16)


def turned_rows(hot, tab_ref, n, cosine, sine):
    return (dot(hot, tab_ref[n]) * cosine + dot(hot, tab_ref[n + 1]) * sine).astype(bf16)


def fine_tables_kernel(gain_hbm, emb_hbm, wq_hbm, wk_hbm, wv_hbm, tab_hbm, tab_ref, gain_ref, emb_ref, w_ref, sems):
    pairs = [(emb_hbm, emb_ref), (gain_hbm, gain_ref)]
    for n, w in enumerate((wq_hbm, wk_hbm, wv_hbm)):
        for part in range(2):
            rows = pl.ds(part * 512, 512)
            pairs.append((w.at[rows], w_ref.at[n, rows]))
    copies = begin_copies(pairs, sems)
    finish_copies(copies[:2])
    fine_in = norm_rows(emb_ref[...].astype(f32), gain_ref[...])
    finish_copies(copies[2:])
    tq = dot(fine_in, w_ref[0]) * q_scale
    tk = dot(fine_in, w_ref[1])
    tables = (tq, partner(tq), tk, partner(tk), dot(fine_in, w_ref[2]))
    for n, table in enumerate(tables):
        tab_ref[n] = table.astype(bf16)
    finish_copies(begin_copies([(tab_ref.at[n], tab_hbm.at[n]) for n in range(5)], sems))


def fine_kernel(
    where_ref, before_ref, prior_ref, own_ref, tab_hbm, turn_hbm,
    own_hbm, o1, o2, o3, q_ref, k_ref, v_ref, tab_ref, turn_ref, block_ref, sems,
):
    step = pl.program_id(0)
    head = where_ref[1]
    outs = (block_ref, o1, o2, o3)
    turns = ((3, 0), (1, 2))
    lowest = jnp.maximum(PAST - where_ref[0] * ROWS, 0)
    head_lane = lax.broadcasted_iota(jnp.int32, (1, SHARE), 1) // HEAD_DIM

    @pl.when(step == 0)
    def _():
        pairs = [(tab_hbm.at[n], tab_ref.at[n]) for n in range(5)] + [(turn_hbm, turn_ref)]
        finish_copies(begin_copies(pairs, sems))
        cosine, sine = turn_tables(turn_ref, 0)
        oldest = pick(before_ref[...])
        at = slice(BLOCK - HALO, BLOCK)
        k_ref[at, :] = turned_rows(oldest, tab_ref, 2, cosine[at], sine[at])
        v_ref[at, :] = dot(oldest, tab_ref[4]).astype(bf16)

        def build(block, ids, with_q):
            begin = pl.multiple_of(block * BLOCK, BLOCK)
            hot = pick(ids)
            cosine, sine = turn_tables(turn_ref, block)
            k_ref[pl.ds(begin, BLOCK), :] = turned_rows(hot, tab_ref, 2, cosine, sine)
            v_ref[pl.ds(begin, BLOCK), :] = dot(hot, tab_ref[4]).astype(bf16)
            if with_q:
                at = pl.multiple_of(begin - (PAST - BLOCK), BLOCK)
                q_ref[pl.ds(at, BLOCK), :] = turned_rows(hot, tab_ref, 0, cosine, sine)

        def build_from(ref, first, with_q):
            def body(n, _):
                ids = ref[pl.ds(pl.multiple_of(n * BLOCK, BLOCK), BLOCK), :]
                build(first + n, ids, with_q)
                return 0

            return body

        for n in range(3):
            build(1 + n, prior_ref[n * BLOCK : (n + 1) * BLOCK, :], False)
        build(4, prior_ref[3 * BLOCK :, :], True)
        for n in range(4):
            build(5 + n, own_ref[n * BLOCK : (n + 1) * BLOCK, :], True)
        halo_q = q_ref[BLOCK - HALO : BLOCK, :]
        stacked = jnp.concatenate(
            [jnp.where(head_lane == h, halo_q, jnp.zeros_like(halo_q)) for h in range(4)], axis=0
        )
        scores = dot_t(stacked, k_ref[BLOCK - HALO : PAST, :])
        row = lax.broadcasted_iota(jnp.int32, scores.shape, 0) % HALO + (PAST - HALO)
        col = lax.broadcasted_iota(jnp.int32, scores.shape, 1) + (BLOCK - HALO)
        allowed = (col <= row) & (col > row - WINDOW) & (col >= lowest)
        scores = jnp.where(allowed, scores, masked_low)
        top = jnp.max(scores, axis=1, keepdims=True)
        weights = jnp.exp2(scores - top)
        total = jnp.sum(weights, axis=1, keepdims=True)
        mixed = dot(weights.astype(bf16), v_ref[BLOCK - HALO : PAST, :]) / total
        result = jnp.zeros((HALO, SHARE), f32)
        for h in range(4):
            result = jnp.where(head_lane == h, mixed[h * HALO : (h + 1) * HALO], result)
        for s, out_ref in enumerate(outs):

            @pl.when(lax.rem(head + s, 4) == 0)
            def _(out_ref=out_ref):
                out_ref[0:HALO, :] = result.astype(bf16)

    for late in range(2):
        turn = jnp.where(step == 0, turns[0][late], turns[1][late])
        place = lax.rem(head + turn, 4)
        begin = pl.multiple_of((place + 1) * BLOCK, BLOCK)
        keys = k_ref[pl.ds(begin, PAST), :]
        values = v_ref[pl.ds(begin, PAST), :]
        query = q_ref[pl.ds(begin, BLOCK), :]
        row = lax.broadcasted_iota(jnp.int32, (BLOCK, BLOCK), 0)
        col = lax.broadcasted_iota(jnp.int32, (BLOCK, BLOCK), 1)
        biases = [
            jnp.where(begin + t * BLOCK >= lowest, 0.0, masked_low).astype(f32) for t in range(4)
        ]
        inside = col <= row
        ones = jnp.ones((PAST, 128), bf16)
        low_lanes = lax.broadcasted_iota(jnp.int32, (1, 128), 1) < 64
        results = []

        def score(h):
            return dot_t(jnp.where(head_lane == h, query, jnp.zeros_like(query)), keys)

        ahead = score(0)
        for h in range(4):
            scores = ahead
            if h < 3:
                ahead = score(h + 1)
            tiles = [scores[:, t * BLOCK : (t + 1) * BLOCK] for t in range(5)]
            edge = jnp.where(inside, tiles[4], tiles[0] + biases[0])
            middle = [tiles[t] + biases[t] for t in range(1, 4)]
            peak = edge
            for tile in middle:
                peak = jnp.maximum(peak, tile)
            top = jnp.max(peak, axis=1, keepdims=True)
            edge = jnp.exp2(edge - top).astype(bf16)
            none = jnp.zeros_like(edge)
            weights = [jnp.exp2(tile - top).astype(bf16) for tile in middle]
            weights = [jnp.where(inside, none, edge), *weights, jnp.where(inside, edge, none)]
            pair = (h // 2) * 128
            wide = jnp.concatenate([values[:, pair : pair + 128], ones], axis=1)
            mixed = dot(jnp.concatenate(weights, axis=1), wide)
            results.append(mixed[:, :128] / mixed[:, 128:])
        result = jnp.concatenate(
            [jnp.where(low_lanes, results[2 * n], results[2 * n + 1]) for n in range(2)], axis=1
        )
        result = result.astype(bf16)
        for n in range(2):

            @pl.when(step == n)
            def _(n=n, late=late, result=result, place=place):
                turn = turns[n][late]
                outs[turn][HALO:, :] = result

                @pl.when(place < 3)
                def _():
                    outs[(turn + 1) % 4][0:HALO, :] = result[BLOCK - HALO :]

    @pl.when(step == 0)
    def _():
        pltpu.make_async_copy(block_ref, own_hbm, sems.at[9]).start()

    @pl.when(step == 1)
    def _():
        pltpu.make_async_copy(block_ref, own_hbm, sems.at[9]).wait()


def vmem():
    return pl.BlockSpec(memory_space=pltpu.VMEM)


def smem():
    return pl.BlockSpec(memory_space=pltpu.SMEM)


def space(shape):
    plain = isinstance(shape, jax.ShapeDtypeStruct)
    return vmem() if plain else pl.BlockSpec(memory_space=pltpu.HBM)


def call(kernel, name, shapes, scalars, arrays, scratch=(), grid=None, limit=16, us=2, hbm=(), free=()):
    one = not isinstance(shapes, (list, tuple))
    extra = {} if grid is None else {"grid": grid}
    return pl.pallas_call(
        kernel,
        out_shape=shapes,
        in_specs=[smem()] * len(scalars)
        + [vmem()] * len(arrays)
        + [pl.BlockSpec(memory_space=pltpu.HBM)] * len(hbm)
        + [pl.BlockSpec(memory_space=pl.ANY)] * len(free),
        out_specs=space(shapes) if one else [space(shape) for shape in shapes],
        scratch_shapes=list(scratch),
        compiler_params=pltpu.CompilerParams(vmem_limit_bytes=limit << 20),
        cost_estimate=pl.CostEstimate(
            flops=us * 10**9, transcendentals=0, bytes_accessed=us * 2 * 10**6
        ),
        name=name,
        **extra,
    )(*scalars, *arrays, *(pltpu.with_memory_space_constraint(a, pltpu.HBM) for a in hbm), *free)


def begin_copies(pairs, sems):
    copies = [pltpu.make_async_copy(a, b, sems.at[n]) for n, (a, b) in enumerate(pairs)]
    for copy in copies:
        copy.start()
    return copies


def finish_copies(copies):
    for copy in copies:
        copy.wait()


def fine_rows_kernel(
    where_ref, ids_ref, emb_ref, g1, g2, g3, own_ref, m1, m2, t1, t2, w_hbm, block_hbm,
    out_ref, w_ref, block_ref, sems,
):
    place, head, core = where_ref[0], where_ref[1], where_ref[2]
    copies = begin_copies(
        [(block_hbm, block_ref)] + [(w_hbm.at[n], w_ref.at[n]) for n in range(4)], sems
    )
    merged = dot(pick(ids_ref[...]), emb_ref[...])
    near = jnp.where(core == 0, g1[...], g3[...])
    far = jnp.where(core == 0, g3[...], g1[...])
    merged += dot(near, m1[...]) + dot(far, t1[...])
    at = pl.ds(pl.multiple_of(core * 128, 128), 128)
    merged += dot(g2[:, at], m2[...])
    at = pl.ds(pl.multiple_of(128 - core * 128, 128), 128)
    merged += dot(g2[:, at], t2[...])
    finish_copies(copies[:1])
    merged += dot(block_ref[...], own_ref[...])
    rows = 256 + HALO
    token = (
        place * ROWS + head * 256 - HALO + lax.broadcasted_iota(jnp.int32, (rows, D), 0)
    )
    fine = jnp.where(token >= 0, merged, 0.0).astype(bf16)
    index = lax.broadcasted_iota(jnp.int32, (256, rows), 0)
    column = lax.broadcasted_iota(jnp.int32, (256, rows), 1)
    source = 4 * (index % 64) + index // 64 + (HALO - 3)
    choose = (source == column).astype(f32).astype(bf16)
    grouped = dot(choose, fine).astype(bf16)
    for d in range(4):
        out_ref[d, 0:256, :] = grouped[:, d * SHARE : (d + 1) * SHARE]
        out_ref[d, 256:rows, :] = fine[256:rows, d * SHARE : (d + 1) * SHARE]
    finish_copies(copies[1:])


def short_part_kernel(group_ref, w_ref, out_ref):
    total = dot(group_ref[0:64, :], w_ref[0])
    for r in range(1, SHORTEN):
        total += dot(group_ref[r * 64 : (r + 1) * 64, :], w_ref[r])
    out_ref[...] = total.astype(bf16)


def coarse_pack_kernel(
    where_ref, s0, s1, s2, s3, gain_ref, wq_ref, wk_ref, wv_ref, turn_ref,
    out_ref, short_ref,
):
    place, head = where_ref[0], where_ref[1]
    for s, ref in enumerate((s0, s1, s2, s3)):
        begin = pl.multiple_of(lax.rem(head - s + 4, 4) * 64, 64)
        short_ref[pl.ds(begin, 64), :] = ref[...]
    x = norm_rows(short_ref[...].astype(f32), gain_ref[...])
    cosine, sine = turn_tables(turn_ref, place)

    def turned(values):
        return values * cosine + partner(values) * sine

    q = turned(dot(x, wq_ref[...])) * q_scale
    k = turned(dot(x, wk_ref[...]))
    v = dot(x, wv_ref[...])
    low_lanes = lax.broadcasted_iota(jnp.int32, (1, 128), 1) < 64
    half = COARSE_ROWS // 2
    for h in range(4):
        pair = (h // 2) * 128
        kp = k[:, pair : pair + 128]
        vp = v[:, pair : pair + 128]
        qp = q[:, pair : pair + 128]
        if h % 2 == 0:
            kv = jnp.where(low_lanes, kp, pltpu.roll(vp, 64, 1))
            qq = jnp.where(low_lanes, qp[:half], pltpu.roll(qp[half:], 64, 1))
        else:
            kv = jnp.where(low_lanes, pltpu.roll(kp, 64, 1), vp)
            qq = jnp.where(low_lanes, pltpu.roll(qp[:half], 64, 1), qp[half:])
        out_ref[h, 0:COARSE_ROWS, :] = kv.astype(bf16)
        out_ref[h, COARSE_ROWS : COARSE_ROWS + half, :] = qq.astype(bf16)


def with_ones(kv):
    return jnp.concatenate([kv, jnp.ones((kv.shape[0], 128), bf16)], axis=1)


def absorb(state, jobs):
    q_ref, top_ref, total_ref, acc_ref = state

    def score(job):
        query = q_ref[pl.ds(job[0], job[1]), :]
        return [dot_t(query, kv) for kv in job[2]]

    ahead = score(jobs[0])
    for n, (begin, rows, parts) in enumerate(jobs):
        scores = ahead
        if n + 1 < len(jobs):
            ahead = score(jobs[n + 1])
        at = pl.ds(begin, rows)
        peak = scores[0]
        for s in scores[1:]:
            peak = jnp.maximum(peak, s)
        old = top_ref[at, :]
        top = jnp.maximum(old, jnp.max(peak, axis=1, keepdims=True))
        factor = jnp.exp2(old - top)
        both = jnp.concatenate([top, top], axis=1)
        contrib = dot(jnp.exp2(scores[0] - both).astype(bf16), with_ones(parts[0]))
        for s, kv in zip(scores[1:], parts[1:]):
            contrib = contrib + dot(jnp.exp2(s - both).astype(bf16), with_ones(kv))
        top_ref[at, :] = top
        total_ref[at, :] = total_ref[at, :] * factor + contrib[:, 128:]
        acc_ref[at, :] = acc_ref[at, :] * factor + contrib[:, :128]


def coarse_first_kernel(
    flag_ref, turned_ref, far_ref, up_hbm, up_ref, q_ref, top_ref, total_ref, acc_ref, sems
):
    copies = begin_copies([(up_hbm, up_ref)], sems)
    half = COARSE_ROWS // 2
    low_lanes = lax.broadcasted_iota(jnp.int32, (1, 128), 1) < 64
    row = lax.broadcasted_iota(jnp.int32, (256, 256), 0)
    col = lax.broadcasted_iota(jnp.int32, (256, 256), 1)
    for z in range(4):
        packed = turned_ref[z, COARSE_ROWS:, :].astype(f32)
        zero = jnp.zeros_like(packed)
        q_ref[z * 256 : z * 256 + half, :] = jnp.where(low_lanes, packed, zero).astype(bf16)
        q_ref[z * 256 + half : (z + 1) * 256, :] = jnp.where(
            low_lanes, pltpu.roll(packed, 64, 1), zero
        ).astype(bf16)
        kv = turned_ref[z, :COARSE_ROWS, :]
        at = pl.ds(z * 256, 256)
        scores = jnp.where(col <= row, dot_t(q_ref[at, :], kv), masked_low)
        top = jnp.max(scores, axis=1, keepdims=True)
        contrib = dot(jnp.exp2(scores - top).astype(bf16), with_ones(kv))
        top_ref[at, :] = jnp.broadcast_to(top, (256, 128))
        total_ref[at, :] = contrib[:, 128:]
        acc_ref[at, :] = contrib[:, :128]
    state = (q_ref, top_ref, total_ref, acc_ref)
    absorb(
        state,
        [
            ((z + 1) * 256, (3 - z) * 256, [turned_ref[z, :COARSE_ROWS, :], far_ref[z]])
            for z in range(3)
        ],
    )

    @pl.when(flag_ref[0] > 0)
    def _():
        absorb(state, [(z * 256, 256, [far_ref[z]]) for z in range(4)])

    finish_copies(copies)


def coarse_more_kernel(which, last, flag_ref, *refs):
    count = 2 * len(which)
    sems = refs[-1]
    refs = refs[:-1]
    chunks = refs[:count]
    q_ref, top_in, total_in, acc_in = refs[count : count + 4]
    refs = refs[count + 4 :]
    top_ref, total_ref, acc_ref = refs[-3:]
    if last:
        own, m1, m2, t1, t2, target, out_ref = refs[:-3]
        pairs = place_copies(flag_ref[4], flag_ref[5], own, (m1, m2), (t1, t2), target)
    else:
        pairs = []
        for a, b in zip(refs[:1], refs[1:2]):
            for part in range(4):
                at = pl.ds(part * 256, 256)
                pairs.append((a.at[at], b.at[at]))
    copies = begin_copies(pairs, sems)
    top_ref[...] = top_in[...]
    total_ref[...] = total_in[...]
    acc_ref[...] = acc_in[...]
    state = (q_ref, top_ref, total_ref, acc_ref)
    pairs_of = [(chunks[2 * n], chunks[2 * n + 1]) for n in range(len(which))]
    absorb(
        state,
        [
            ((z + 1) * 256, (3 - z) * 256, [near[z], far[z]])
            for near, far in pairs_of
            for z in range(3)
        ],
    )
    for s, (near, far) in zip(which, pairs_of):

        @pl.when(flag_ref[s] > 0)
        def _(near=near, far=far):
            absorb(state, [(z * 256, 256, [near[z], far[z]]) for z in range(4)])

    if last:
        mixed = acc_ref[...] / total_ref[...]
        low_lanes = lax.broadcasted_iota(jnp.int32, (1, 128), 1) < 64
        for z in range(4):
            upper = pltpu.roll(mixed[z * 256 : z * 256 + 128], 64, 1)
            lower = mixed[z * 256 + 128 : (z + 1) * 256]
            block = jnp.where(low_lanes, upper, lower).astype(bf16)
            for y in range(4):
                out_ref[z * 4 + y] = block
    finish_copies(copies)


def feed_kernel(
    where_ref, heads_ref, short_ref, gain_ref, co_ref, up_ref, down_ref,
    part_ref, first_ref, mixed_ref, all_ref,
):
    head = where_ref[1]
    low_lanes = lax.broadcasted_iota(jnp.int32, (1, 128), 1) < 64
    for y in range(4):
        for pair in range(2):
            even = heads_ref[2 * pair * 4 + y].astype(f32)
            odd = heads_ref[(2 * pair + 1) * 4 + y].astype(f32)
            at = slice(y * 256 + pair * 128, y * 256 + (pair + 1) * 128)
            mixed_ref[0:128, at] = jnp.where(low_lanes, even, pltpu.roll(odd, 64, 1)).astype(bf16)
            mixed_ref[128:256, at] = jnp.where(low_lanes, pltpu.roll(even, 64, 1), odd).astype(bf16)
    first = short_ref[...].astype(f32) + dot(mixed_ref[...], co_ref[...])
    all_ref[...] = first
    first_ref[...] = all_ref[pl.ds(pl.multiple_of(head * 64, 64), 64), :]
    feed = norm_rows(first, gain_ref[...])
    inner = jax.nn.gelu(dot(feed, up_ref[...])).astype(bf16)
    part_ref[...] = dot(inner, down_ref[...]).astype(bf16).reshape(4, 64, D)


def final_kernel(where_ref, s0, s1, s2, s3, b0, b1, b2, b3, up_ref, out_ref):
    head = where_ref[1]
    rows = 256 + HALO
    second = jnp.concatenate([ref[...] for ref in (s0, s1, s2, s3)], axis=0)
    lifted = dot(second, up_ref[...])
    index = lax.broadcasted_iota(jnp.int32, (256, rows), 0)
    column = lax.broadcasted_iota(jnp.int32, (256, rows), 1)
    r, m = index // 64, index % 64
    source = jnp.where(r == 0, 192 + m, jnp.where(m == 63, 268 + r, (r - 1) * 64 + m + 1))
    choose = (source == column).astype(f32).astype(bf16)
    index = lax.broadcasted_iota(jnp.int32, (256, 256), 0)
    column = lax.broadcasted_iota(jnp.int32, (256, 256), 1)
    weave = ((index % 4) * 64 + index // 4 == column).astype(f32).astype(bf16)
    for s, block in enumerate((b0, b1, b2, b3)):
        mine = lifted[s * 64 : (s + 1) * 64]
        raised = jnp.concatenate([mine[:, q * SHARE : (q + 1) * SHARE] for q in range(4)], axis=0)
        value = (dot(choose, block[...]) + raised).astype(bf16)
        begin = pl.multiple_of(lax.rem(head - s + 4, 4) * 256, 256)
        out_ref[pl.ds(begin, 256), :] = dot(weave, value).astype(bf16)


def fetch_rest(weight, core):
    pairs = []
    for c, step in ((0, 1), (1, 3)):
        pairs += [(4 * c + y, 4 * c + (y + step) % 4) for y in range(4)]
    whole = lax.ppermute(weight, ("core", "head"), pairs)
    half = shift(lax.dynamic_slice_in_dim(weight, core * 128, 128, 0), "head", 2, 4)
    return [whole, half]


def swap_cores(parts):
    return [shift(part, "core", 1, 2) for part in parts]


def sources(head, core):
    mine = lax.rem(head + 3 - 2 * core, 4)
    other = lax.rem(head + 1 + 2 * core, 4)
    return mine, other, lax.rem(head + 2, 4)


def place_copies(head, core, own, mine, other, target):
    near, far, apart = sources(head, core)
    halves_at = apart * 256
    return [
        (own, target.at[pl.ds(pl.multiple_of(head * 256, 256), 256)]),
        (mine[0], target.at[pl.ds(pl.multiple_of(near * 256, 256), 256)]),
        (other[0], target.at[pl.ds(pl.multiple_of(far * 256, 256), 256)]),
        (mine[1], target.at[pl.ds(pl.multiple_of(halves_at + core * 128, 128), 128)]),
        (other[1], target.at[pl.ds(pl.multiple_of(halves_at + 128 - core * 128, 128), 128)]),
    ]


def after(value, gate):
    return lax.optimization_barrier((value, gate))


def local(
    token_ids, embedding, fine_norm, fine_query, fine_key, fine_value, fine_output,
    shorten_weight, coarse_norm, coarse_query, coarse_key, coarse_value, coarse_output,
    ffn_norm, ffn_up, ffn_down, upsample_weight,
):
    place = lax.axis_index(SEQ).astype(jnp.int32)
    head = lax.axis_index("head").astype(jnp.int32)
    x_place = lax.axis_index("x").astype(jnp.int32)
    core = lax.axis_index("core").astype(jnp.int32)
    tables = jnp.asarray(angle_tables())
    where = jnp.stack([place, head, core])

    prior = later(token_ids, SEQ, 1, 32)
    before = later(token_ids, SEQ, 2, 32)[ROWS - HALO :]
    tab = call(
        fine_tables_kernel, "fine_tables", pltpu.HBM((5, 256, SHARE), bf16), [], [],
        [
            pltpu.VMEM((5, 256, SHARE), bf16),
            pltpu.VMEM((1, D), f32), pltpu.VMEM((256, D), bf16),
            pltpu.VMEM((3, D, SHARE), bf16), pltpu.SemaphoreType.DMA((9,)),
        ],
        us=3, hbm=[fine_norm[None], embedding, fine_query, fine_key, fine_value],
    )
    own_ids_column = token_ids[:, None]
    fine_output_held, own_ids_column = after(fine_output, own_ids_column)
    out_mine = fetch_rest(fine_output_held, core)
    rows = 256 + HALO
    mixed = call(
        fine_kernel, "fine_attention",
        [pltpu.HBM((rows, SHARE), bf16)] + [jax.ShapeDtypeStruct((rows, SHARE), bf16)] * 3,
        [where], [before[:, None], prior[:, None], own_ids_column],
        [
            pltpu.VMEM((BLOCK + ROWS, SHARE), bf16),
            pltpu.VMEM((KEYS, SHARE), bf16), pltpu.VMEM((KEYS, SHARE), bf16),
            pltpu.VMEM((5, 256, SHARE), bf16), pltpu.VMEM((576, 128), f32),
            pltpu.VMEM((rows, SHARE), bf16), pltpu.SemaphoreType.DMA((10,)),
        ],
        grid=(2,), us=12, limit=24, hbm=[tab, tables],
    )

    out_mine, mixed = after(out_mine, mixed)
    got = [shift(mixed[s], "head", s, 4) for s in range(1, 4)]
    out_other = swap_cores(out_mine)
    own_ids = lax.dynamic_slice_in_dim(
        jnp.concatenate([prior[ROWS - HALO :], token_ids]), head * 256, rows, 0
    )
    sends, shorten_near = call(
        fine_rows_kernel, "fine_rows",
        [
            jax.ShapeDtypeStruct((4, rows, SHARE), bf16),
            jax.ShapeDtypeStruct((SHORTEN, SHARE, D), bf16),
        ],
        [where],
        [own_ids[:, None], embedding, *got, fine_output, *out_mine, *out_other],
        [pltpu.VMEM((rows, SHARE), bf16), pltpu.SemaphoreType.DMA((5,))],
        hbm=[shorten_weight, mixed[0]],
    )
    blocks = exchange(lambda d: lax.dynamic_index_in_dim(sends, d, 0, keepdims=False), "head", 4)

    terms = []
    for s, block in enumerate(blocks):
        part = call(
            short_part_kernel, "short_part", jax.ShapeDtypeStruct((64, D), bf16), [],
            [block, shorten_near],
        )
        terms.append(part if s == 0 else shift(part, "head", 4 - s, 4))
    short_own = sum(t.astype(f32) for t in terms).astype(bf16)
    shorts = [short_own] + [shift(short_own, "head", s, 4) for s in range(1, 4)]
    packed, short = call(
        coarse_pack_kernel, "coarse_pack",
        [
            jax.ShapeDtypeStruct((4, COARSE_ROWS * 3 // 2, 128), bf16),
            jax.ShapeDtypeStruct((COARSE_ROWS, D), bf16),
        ],
        [where],
        [*shorts, coarse_norm[None], coarse_query, coarse_key, coarse_value, tables],
    )

    coarse_output_held, packed = after(coarse_output, packed)
    co_mine = fetch_rest(coarse_output_held, core)
    turned = lax.all_to_all(packed, "z", 0, 0)
    kv = turned[:, :COARSE_ROWS]
    far = [shift(kv, "core", 1, 2)]
    near = [shift(kv, "x", s, 4) for s in range(1, 4)]
    steps = jnp.arange(4, dtype=jnp.int32)
    flags = ((x_place - steps + 4) % 4 < x_place).astype(jnp.int32) + (steps == 0) * core
    flags = jnp.concatenate([flags, where[1:]])
    wide = jax.ShapeDtypeStruct((1024, 128), f32)
    square = jax.ShapeDtypeStruct((D, D), bf16)
    up_near, q_all, *sums = call(
        coarse_first_kernel, "coarse_first",
        [square, jax.ShapeDtypeStruct((1024, 128), bf16), wide, wide, wide],
        [flags], [turned, far[0]], [pltpu.SemaphoreType.DMA((1,))],
        us=3, limit=24, hbm=[ffn_up],
    )
    near_held, co_held, q_all = lax.optimization_barrier((near, co_mine, q_all))
    far += [shift(part, "core", 1, 2) for part in near_held]
    co_other = swap_cores(co_held)
    down_near, *sums = call(
        functools.partial(coarse_more_kernel, (1, 3), False), "coarse_more",
        [square, wide, wide, wide],
        [flags], [near[0], far[1], near[2], far[3], q_all, *sums],
        [pltpu.SemaphoreType.DMA((4,))], us=6, limit=24, hbm=[ffn_down],
    )
    output_near, wide_sends = call(
        functools.partial(coarse_more_kernel, (2,), True), "coarse_last",
        [square, jax.ShapeDtypeStruct((16, 128, 128), bf16)],
        [flags], [near[1], far[2], q_all, *sums],
        [pltpu.VMEM((1024, 128), f32)] * 3 + [pltpu.SemaphoreType.DMA((5,))],
        us=3, limit=24, hbm=[coarse_output], free=[*co_mine, *co_other],
    )

    heads_in = lax.all_to_all(wide_sends, ("z", "head"), 0, 0)
    parts, first_own = call(
        feed_kernel, "feed",
        [jax.ShapeDtypeStruct((4, 64, D), bf16), jax.ShapeDtypeStruct((64, D), f32)],
        [where],
        [heads_in, short, ffn_norm[None], output_near, up_near, down_near],
        [
            pltpu.VMEM((COARSE_ROWS, D), bf16), pltpu.VMEM((COARSE_ROWS, D), f32),
        ],
        us=4,
    )
    sums = exchange(lambda d: lax.dynamic_index_in_dim(parts, d, 0, keepdims=False), "head", 4)
    second_own = (first_own + sum(t.astype(f32) for t in sums)).astype(bf16)
    seconds = [second_own] + [shift(second_own, "head", s, 4) for s in range(1, 4)]
    return call(
        final_kernel, "final", jax.ShapeDtypeStruct((ROWS, SHARE), bf16),
        [where], [*seconds, *blocks, upsample_weight.reshape(D, SHORTEN * SHARE)],
    )


def solution(mesh):
    split = Mesh(mesh.devices.reshape(4, 4, 2, 4), ("z", "x", "core", "head"))
    return jax.shard_map(
        local,
        mesh=split,
        in_specs=(
            P(SEQ), P(), P(), P(None, "head"), P(None, "head"), P(None, "head"), P("head", None),
            P(None, "head", None), P(), P(None, "head"), P(None, "head"), P(None, "head"),
            P("head", None), P(), P(None, "head"), P("head", None), P(None, None, "head"),
        ),
        out_specs=P(SEQ, "head"),
        check_vma=False,
    )
```
